32 devices in a mesh: media: 8 (over z, x), keys: 4 (over y, core).
Axes of the slice: x: 2, y: 2, z: 4, core: 2. Of those that a mesh axis runs over, the one named last changes fastest.
Arguments:
- latents: float32 [48, 64, 1024], P('media', 'keys'), may hold values from -6 to 6
- patches: bfloat16 [48, 2048, 1024], P('media', 'keys'), may hold values from -6 to 6
- frame_counts: int32 [48], P('media'), may hold values from 1 to 8
- time_embedding: float32 [8, 1024], replicated, may hold values from -6 to 6
- media_gain: float32 [1024], replicated, may hold values from 0.5 to 1.5
- media_bias: float32 [1024], replicated, may hold values from -3 to 3
- latent_gain: float32 [1024], replicated, may hold values from 0.5 to 1.5
- latent_bias: float32 [1024], replicated, may hold values from -3 to 3
- ff_gain: float32 [1024], replicated, may hold values from 0.5 to 1.5
- ff_bias: float32 [1024], replicated, may hold values from -3 to 3
- query_weight: bfloat16 [1024, 512], replicated, may hold values from -0.1875 to 0.1875
- key_weight: bfloat16 [1024, 512], replicated, may hold values from -0.1875 to 0.1875
- value_weight: bfloat16 [1024, 512], replicated, may hold values from -0.1875 to 0.1875
- out_weight: bfloat16 [512, 1024], replicated, may hold values from -4 to 4
- up_weight: bfloat16 [1024, 4096], replicated, may hold values from -0.1875 to 0.1875
- down_weight: bfloat16 [4096, 1024], replicated, may hold values from -0.09375 to 0.09375
- cotangent: float32 [48, 64, 1024], P('media', 'keys'), may hold values from -6 to 6
Outputs:
- resampled: float32 [48, 64, 1024], P('media', 'keys')
- patches_grad: bfloat16 [48, 2048, 1024], P('media', 'keys')
- latents_grad: float32 [48, 64, 1024], P('media', 'keys')
- time_grad: float32 [8, 1024], replicated
- media_gain_grad: float32 [1024], replicated
- media_bias_grad: float32 [1024], replicated
- latent_gain_grad: float32 [1024], replicated
- latent_bias_grad: float32 [1024], replicated
- ff_gain_grad: float32 [1024], replicated
- ff_bias_grad: float32 [1024], replicated
- query_weight_grad: float32 [1024, 512], P('media', 'keys')
- key_weight_grad: float32 [1024, 512], P('media', 'keys')
- value_weight_grad: float32 [1024, 512], P('media', 'keys')
- out_weight_grad: float32 [512, 1024], P('media', 'keys')
- up_weight_grad: float32 [1024, 4096], P('media', 'keys')
- down_weight_grad: float32 [4096, 1024], P('media', 'keys')
The draws below stay inside these ranges and needn't reach their ends.
Inputs may be any that keep to these rules, and one draw needn't show every extreme that they name: `frame_counts`: the number of frames of each medium; patch rows of its frame slots at or after this number still hold values, but their keys are invisible to the latents.
All inputs are finite; a program needn't handle non-finite values.
Results may differ from the reference program's by a relative error of at most 0.02.
Values may be sent and summed in bfloat16 or wider, within the bound.
No kernel may reach another device: no remote copies, remote signals or barrier semaphores. Data moves between devices by JAX's collectives and lax.ppermute only.
A program may use at most 192 MiB of HBM per device.

```python
import jax
import jax.numpy as jnp
from jax import lax

D = 1024
FF = 4096
HEADS = 8
HEAD = 64
INNER = 512
LAT = 64
PATCH = 256
FRAMES = 8
MEDIA = 48


def place_ends(array, stream_key, least, largest):
    extent = array.shape
    place = [jax.random.randint(jax.random.fold_in(stream_key, axis), (), 0, extent[axis]) for axis in range(len(extent))]
    array = array.at[tuple(place)].set(least)
    longest = extent.index(max(extent))
    place[longest] = (place[longest] + 1) % extent[longest]
    return array.at[tuple(place)].set(largest)


def with_spikes(drawn, key, source, target, shards_of, factor):
    def block_of(dim):
        return (jnp.arange(drawn.shape[dim]) // (drawn.shape[dim] // shards_of)).reshape((-1,) + (1,) * (drawn.ndim - 1 - dim))

    one_side = jax.random.permutation(key, shards_of)[block_of(target)]
    other_side = (block_of(target) + shards_of // 2) % shards_of
    return jnp.where((block_of(source) == one_side) | (block_of(source) == other_side), factor * drawn, drawn)


def level_of(key, dims, pieces, least, largest):
    loudness, own = 1.0, jax.random.fold_in(key, 6)
    for position, shards_of in pieces:
        heights = jnp.exp(jax.random.uniform(jax.random.fold_in(own, position), (shards_of,), jnp.float32, least / len(pieces), largest / len(pieces)))
        loudness = loudness * jnp.repeat(heights, dims[position] // shards_of).reshape([-1 if axis == position else 1 for axis in range(len(dims))])
    return loudness


def noise(stream_key, shape, scale, bound, cuts=(), kind=jnp.bfloat16):
    level = level_of(stream_key, shape, cuts, -0.22, 0.18) if cuts else 1.0
    array = jax.random.normal(stream_key, shape, jnp.float32) * scale * level
    return jnp.minimum(jnp.maximum(array, -bound), bound).astype(kind)


def noise_with(stream_key, extent, scale, reach, shards, heavy, kind=jnp.bfloat16):
    array = scale * jax.random.normal(stream_key, extent, jnp.float32)
    if shards:
        array = array * level_of(stream_key, extent, shards, -0.22, 0.18)
    return jnp.clip(with_spikes(array, jax.random.fold_in(stream_key, 3), *heavy), -reach, reach).astype(kind)


def setup_inputs(seed: int = 0) -> dict:
    keys = jax.random.split(jax.random.key(seed), 18)
    return {
        "latents": noise(keys[0], (MEDIA, LAT, D), 1.0, 6.0, ((0, 8), (1, 4)), jnp.float32),
        "patches": noise(keys[1], (MEDIA, FRAMES * PATCH, D), 1.0, 6.0, ((0, 8), (1, 4))),
        "frame_counts": place_ends(jax.random.randint(keys[2], (MEDIA,), 1, FRAMES + 1), jax.random.fold_in(keys[2], 1), 1, FRAMES).astype(jnp.int32),
        "time_embedding": noise(keys[3], (FRAMES, D), 1.0, 6.0, (), jnp.float32),
        "media_gain": jnp.clip(1.0 + 0.1 * jax.random.normal(keys[4], (D,), jnp.float32), 0.5, 1.5),
        "media_bias": noise(keys[5], (D,), 0.5, 3.0, (), jnp.float32),
        "latent_gain": jnp.clip(1.0 + 0.1 * jax.random.normal(keys[6], (D,), jnp.float32), 0.5, 1.5),
        "latent_bias": noise(keys[7], (D,), 0.5, 3.0, (), jnp.float32),
        "ff_gain": jnp.clip(1.0 + 0.1 * jax.random.normal(keys[8], (D,), jnp.float32), 0.5, 1.5),
        "ff_bias": noise(keys[9], (D,), 0.5, 3.0, (), jnp.float32),
        "query_weight": noise(keys[10], (D, INNER), D ** -0.5, 0.1875),
        "key_weight": noise(keys[11], (D, INNER), D ** -0.5, 0.1875),
        "value_weight": noise(keys[12], (D, INNER), D ** -0.5, 0.1875),
        "out_weight": noise(keys[13], (INNER, D), (max(INNER // 256, 1)) ** -0.5, 4.0),
        "up_weight": noise(keys[14], (D, FF), D ** -0.5, 0.1875),
        "down_weight": noise(keys[15], (FF, D), FF ** -0.5, 0.09375),
        "cotangent": noise_with(keys[16], (MEDIA, LAT, D), 1.0, 6.0, ((0, 8), (1, 4)), (0, 2, 8, 2.0), jnp.float32),
    }


@jax.custom_vjp
def low(v):
    return lax.optimization_barrier(v.astype(jnp.bfloat16)).astype(jnp.float32)

@jax.custom_vjp
def low_back(v):
    return v

def low_keep(v):
    return (low(v), None)

def low_pass(kept, grad):
    return (grad,)

def back_keep(v):
    return (v, None)

def back_low(kept, grad):
    return (low(grad),)
low.defvjp(low_keep, low_pass)
low_back.defvjp(back_keep, back_low)
EPS = 1e-05
NEG = -1e+30

def layer_norm(values, gain, bias):
    centre = lax.optimization_barrier(jnp.mean(values, -1, keepdims=True))
    shifted = values - centre
    spread = lax.optimization_barrier(jnp.mean(shifted * shifted, -1, keepdims=True))
    return shifted * lax.rsqrt(spread + EPS) * gain + bias

def product(left, right):
    return jnp.dot(left, right, precision=lax.Precision.HIGHEST)

def medium_forward(params, latent, patch_rows, count):
    time_embedding, media_gain, media_bias, latent_gain, latent_bias, ff_gain, ff_bias, query_weight, key_weight, value_weight, out_weight, up_weight, down_weight = params
    framed = patch_rows.reshape(FRAMES, PATCH, D) + time_embedding[:, None, :]
    media_norm = low(layer_norm(framed.reshape(FRAMES * PATCH, D), media_gain, media_bias))
    latent_norm = low(layer_norm(latent, latent_gain, latent_bias))
    joined = jnp.concatenate([media_norm, latent_norm], 0)
    queries = low(low_back(product(latent_norm, query_weight))).reshape(LAT, HEADS, HEAD)
    all_keys = low(low_back(product(joined, key_weight))).reshape(FRAMES * PATCH + LAT, HEADS, HEAD)
    all_values = low(low_back(product(joined, value_weight))).reshape(FRAMES * PATCH + LAT, HEADS, HEAD)
    scores = jnp.einsum('qhd,khd->hqk', queries, all_keys, precision=lax.Precision.HIGHEST) * HEAD ** (-0.5)
    scores = low_back(scores)
    frame_ids = jnp.arange(FRAMES * PATCH, dtype=jnp.int32) // PATCH
    visible = jnp.concatenate([frame_ids < count, jnp.ones((LAT,), dtype=jnp.bool_)])
    scores = jnp.where(visible[None, None, :], scores, NEG)
    probs_low = low(jax.nn.softmax(scores, -1))
    attended = jnp.einsum('hqk,khd->qhd', probs_low, all_values, precision=lax.Precision.HIGHEST).reshape(LAT, HEADS * HEAD)
    attended = low(low_back(attended))
    middle = latent + low_back(product(attended, out_weight))
    ff_input = low(layer_norm(middle, ff_gain, ff_bias))
    hidden = low_back(product(ff_input, up_weight))
    activated = low(jax.nn.gelu(hidden, approximate=False))
    return middle + low_back(product(activated, down_weight))

def reference(latents, patches, frame_counts, time_embedding, media_gain, media_bias, latent_gain, latent_bias, ff_gain, ff_bias, query_weight, key_weight, value_weight, out_weight, up_weight, down_weight, cotangent):
    params = (time_embedding, media_gain, media_bias, latent_gain, latent_bias, ff_gain, ff_bias, query_weight.astype(jnp.float32), key_weight.astype(jnp.float32), value_weight.astype(jnp.float32), out_weight.astype(jnp.float32), up_weight.astype(jnp.float32), down_weight.astype(jnp.float32))

    def forward(params, latent_all, patch_all):

        def per_medium(inputs):
            return jax.checkpoint(medium_forward)(params, inputs[0], inputs[1], inputs[2])
        return lax.map(per_medium, (latent_all, patch_all, frame_counts))
    resampled, pullback = jax.vjp(forward, params, latents, patches.astype(jnp.float32))
    grads, latents_grad, patches_grad = pullback(cotangent)
    return (resampled, patches_grad.astype(jnp.bfloat16), latents_grad, grads[0], grads[1], grads[2], grads[3], grads[4], grads[5], grads[6], grads[7], grads[8], grads[9], grads[10], grads[11], grads[12])
```

```python
import functools

import jax
import jax.numpy as jnp
from jax import lax
from jax.experimental import pallas as pl
from jax.experimental.pallas import tpu as pltpu
from jax.sharding import PartitionSpec as P

HEAD = 64
PATCH = 256
GROUP = 256
LANES = 128

EPS = 1e-05
NEG = -1e30
PAIR = 2

f32 = jnp.float32
bf16 = jnp.bfloat16


def mul(left, right, contract=((1,), (0,)), precision=None):
    return lax.dot_general(
        left, right, (contract, ((), ())), precision=precision, preferred_element_type=f32
    )


NN = ((1,), (0,))
NT = ((1,), (1,))
TN = ((0,), (0,))


def norm_parts(values):
    centre = jnp.mean(values, -1, keepdims=True)
    shifted = values - centre
    spread = jnp.mean(shifted * shifted, -1, keepdims=True)
    return centre, lax.rsqrt(spread + EPS), shifted


def norm(values, gain, bias):
    _, scale, shifted = norm_parts(values)
    return shifted * scale * gain + bias


def norm_back(values, gain, grad):
    _, scale, shifted = norm_parts(values)
    unit = shifted * scale
    scaled = grad * gain
    first = jnp.mean(scaled, -1, keepdims=True)
    second = jnp.mean(scaled * unit, -1, keepdims=True)
    back = scale * (scaled - first - unit * second)
    return (
        back,
        jnp.sum(grad * unit, 0, keepdims=True),
        jnp.sum(grad, 0, keepdims=True),
    )


def gelu_parts(hidden):
    cdf = 0.5 * (1.0 + lax.erf(hidden * (2.0**-0.5)))
    pdf = jnp.exp(-0.5 * hidden * hidden) * 0.3989422804014327
    return cdf, cdf + hidden * pdf


def head_mask(rows, width, heads):
    row = lax.broadcasted_iota(jnp.int32, (heads * rows, width), 0) // rows
    col = lax.broadcasted_iota(jnp.int32, (heads * rows, width), 1)
    return row, col


def spread_heads(values):
    heads = values.shape[1] // HEAD
    row, col = head_mask(values.shape[0], values.shape[1], heads)
    return jnp.where(row == col // HEAD, jnp.concatenate([values] * heads, 0), jnp.zeros((), values.dtype))


def fold_heads(values):
    heads = values.shape[1] // HEAD
    rows = values.shape[0] // heads
    row, col = head_mask(rows, values.shape[1], heads)
    kept = jnp.where(row == col // HEAD, values, 0.0)
    total = kept[:rows]
    for h in range(1, heads):
        total = total + kept[h * rows : (h + 1) * rows]
    return total


def three_parts(values, lane, start, slots):
    high = values.astype(bf16).astype(f32)
    rest = values - high
    middle = rest.astype(bf16).astype(f32)
    low = rest - middle
    place = lane // slots - start
    return jnp.where(place == 0, high, jnp.where(place == 1, middle, jnp.where(place == 2, low, 0.0)))


def cost(flops, moved, special=0):
    return pl.CostEstimate(flops=int(flops), bytes_accessed=int(moved), transcendentals=int(special))


def params(mib, grid=0):
    return pltpu.CompilerParams(vmem_limit_bytes=mib << 20)


def latent_kernel(lat, gain, bias, cot, wq, wk, wv, low_o, q_o, k_o, v_o, out_o):
    low = norm(lat[...], gain[...], bias[...]).astype(bf16)
    low_o[...] = low
    q_o[...] = mul(low, wq[...]).astype(bf16)
    k_o[...] = mul(low, wk[...]).astype(bf16)
    v_o[...] = mul(low, wv[...]).astype(bf16)
    out_o[...] = cot[...].astype(bf16)


def patch_kernel(frames, patches, time, gain, bias, wk, wv, low_o, k_o, v_o):
    for f in range(frames):
        rows = pl.ds(f * PATCH, PATCH)
        framed = patches[0, rows, :].astype(f32) + time[0, f : f + 1, :]
        low = norm(framed, gain[...], bias[...]).astype(bf16)
        low_o[0, rows, :] = low
        k_o[0, rows, :] = mul(low, wk[...]).astype(bf16)
        v_o[0, rows, :] = mul(low, wv[...]).astype(bf16)


def masked_scores(query, keys, frames, first, count):
    scores = mul(query, keys, NT)
    parts = []
    for f in range(frames):
        part = scores[:, f * PATCH : (f + 1) * PATCH]
        parts.append(jnp.where(first + f < count, part, NEG))
    return jnp.concatenate(parts, 1) if frames > 1 else parts[0]


def attend_kernel(n_keys, frames, scalars, counts, *refs):
    q = refs[:n_keys]
    kp, vp, kl, vl = refs[n_keys : n_keys + 4]
    outs = refs[n_keys + 4 :]
    own = q[0].shape[0]
    inner = q[0].shape[1]
    heads = inner // HEAD
    count = counts[pl.program_id(0)]
    first = scalars[0] * frames
    query = jnp.concatenate([r[...] for r in q], 0)
    rows = query.shape[0]
    stats = jnp.zeros((rows, LANES), f32)
    shares = []
    for g in range(inner // GROUP):
        cols = slice(g * GROUP, (g + 1) * GROUP)
        wide = spread_heads(query[:, cols] * bf16(HEAD**-0.5))
        scores = masked_scores(wide, kp[0, :, cols], frames, first, count)
        lat_scores = mul(wide, kl[:, cols], NT)
        top = jnp.maximum(
            jnp.max(scores, -1, keepdims=True), jnp.max(lat_scores, -1, keepdims=True)
        )
        raw = jnp.exp(scores - top)
        lat_raw = jnp.exp(lat_scores - top)
        total = jnp.sum(raw, -1, keepdims=True) + jnp.sum(lat_raw, -1, keepdims=True)
        share = mul(raw.astype(bf16), vp[0, :, cols]) + mul(lat_raw.astype(bf16), vl[:, cols])
        shares.append(fold_heads(share / total).astype(bf16))
        level = top + jnp.log(total)
        row, lane = head_mask(rows, LANES, GROUP // HEAD)
        kept = jnp.where(lane % heads == row + g * (GROUP // HEAD), level, 0.0)
        for h in range(GROUP // HEAD):
            stats = stats + kept[h * rows : (h + 1) * rows]
    lane = lax.broadcasted_iota(jnp.int32, stats.shape, 1)
    packed = jnp.concatenate(shares + [three_parts(stats, lane, 0, heads).astype(bf16)], 1)
    for s in range(n_keys):
        outs[s][...] = packed[s * own : (s + 1) * own]


def sum_runs(stats, heads, start):
    total = None
    for part in range(3):
        shift = (-(start + part) * heads) % LANES
        term = pltpu.roll(stats, shift, 1) if shift else stats
        total = term if total is None else total + term
    return total


def join_kernel(n_keys, latents, gain, bias, wo, *refs):
    slots = refs[:n_keys]
    att_o, low_o, mid_o, ff_o, lse_o = refs[n_keys:]
    inner = att_o.shape[1]
    heads = inner // HEAD
    levels = [sum_runs(r[:, inner:].astype(f32), heads, 0) for r in slots]
    top = functools.reduce(jnp.maximum, levels)
    weights = [jnp.exp(v - top) for v in levels]
    total = functools.reduce(jnp.add, weights)
    inverse = 1.0 / total
    lane = lax.broadcasted_iota(jnp.int32, (LANES, inner), 0)
    col = lax.broadcasted_iota(jnp.int32, (LANES, inner), 1)
    select = jnp.where(lane == col // HEAD, 1.0, 0.0)
    attended = None
    for s in range(n_keys):
        wide = mul(weights[s] * inverse, select, NN, lax.Precision.HIGHEST)
        term = wide * slots[s][:, :inner].astype(f32)
        attended = term if attended is None else attended + term
    low = attended.astype(bf16)
    middle = latents[...] + mul(low, wo[...])
    att_o[...] = attended
    low_o[...] = low
    mid_o[...] = middle
    ff_o[...] = norm(middle, gain[...], bias[...]).astype(bf16)
    lse_o[...] = top + jnp.log(total)


def forward_kernel(
    n_keys,
    scalars,
    attended,
    att_low,
    middle,
    ff_low,
    lse,
    cot,
    out_low,
    gain,
    wo,
    up,
    down,
    res_o,
    mid_grad_o,
    pack_o,
    gain_o,
    bias_o,
    wo_grad_o,
    res_acc,
    in_acc,
):
    step = pl.program_id(0)

    @pl.when(step == 0)
    def _():
        res_acc[...] = jnp.zeros_like(res_acc)
        in_acc[...] = jnp.zeros_like(in_acc)

    hidden = mul(ff_low[...], up[...])
    act_grad = mul(out_low[...], down[...], NT)
    cdf, slope = gelu_parts(hidden)
    res_acc[...] += mul((hidden * cdf).astype(bf16), down[...])
    in_acc[...] += mul((act_grad * slope).astype(bf16), up[...], NT)

    @pl.when(step == pl.num_programs(0) - 1)
    def _():
        inner = attended.shape[1]
        heads = inner // HEAD
        res_o[...] = middle[...] + res_acc[...]
        back, gain_grad, bias_grad = norm_back(middle[...], gain[...], in_acc[...])
        gain_o[...] = gain_grad
        bias_o[...] = bias_grad
        mid_grad = cot[...] + back
        mid_grad_o[...] = mid_grad
        branch = mid_grad.astype(bf16)
        att_grad = mul(branch, wo[...], NT).astype(bf16)
        col = lax.broadcasted_iota(jnp.int32, (inner, LANES), 0)
        lane = lax.broadcasted_iota(jnp.int32, (inner, LANES), 1)
        select = jnp.where(col // HEAD == lane % heads, 1.0, 0.0)
        delta = mul(attended[...] * att_grad.astype(f32), select, NN, lax.Precision.HIGHEST)
        lane = lax.broadcasted_iota(jnp.int32, delta.shape, 1)
        level = jnp.where(lane < heads, lse[...], 0.0)
        level = level + pltpu.roll(level, heads, 1) + pltpu.roll(level, 2 * heads, 1)
        stats = three_parts(level, lane, 0, heads) + three_parts(delta, lane, 3, heads)
        pack_o[...] = jnp.concatenate([att_grad, stats.astype(bf16)], 1)
        wo_grad_o[...] = mul(att_low[...], branch, TN).astype(bf16)


def ff_grad_kernel(n_slots, *refs):
    ins = refs[:n_slots]
    outs = refs[n_slots : 2 * n_slots]
    up, down, up_o, down_o = refs[2 * n_slots :]
    ff_all = jnp.concatenate([r[...] for r in ins], 0)
    out_all = jnp.concatenate([r[...] for r in outs], 0)
    hidden = mul(ff_all, up[...])
    act_grad = mul(out_all, down[...], NT)
    cdf, slope = gelu_parts(hidden)
    down_o[...] = mul((hidden * cdf).astype(bf16), out_all, TN).astype(bf16)
    up_o[...] = mul((act_grad * slope).astype(bf16), ff_all, TN).astype(bf16)


def attend_back_kernel(n_keys, frames, scalars, counts, *refs):
    q = refs[:n_keys]
    packs = refs[n_keys : 2 * n_keys]
    kp, vp, kl, vl = refs[2 * n_keys : 2 * n_keys + 4]
    kv_t_o, kl_o, vl_o = refs[2 * n_keys + 4 : 2 * n_keys + 7]
    q_o = refs[2 * n_keys + 7 :]
    own = q[0].shape[0]
    inner = q[0].shape[1]
    heads = inner // HEAD
    count = counts[pl.program_id(0)]
    first = scalars[0] * frames
    query = jnp.concatenate([r[...] for r in q], 0)
    grad = jnp.concatenate([r[:, :inner] for r in packs], 0)
    stats = jnp.concatenate([r[:, inner:] for r in packs], 0).astype(f32)
    rows = query.shape[0]
    for g in range(inner // GROUP):
        cols = slice(g * GROUP, (g + 1) * GROUP)
        row, lane = head_mask(rows, LANES, GROUP // HEAD)
        tiled = jnp.concatenate([stats] * (GROUP // HEAD), 0)
        mine = lane % heads == row + g * (GROUP // HEAD)
        level = jnp.sum(jnp.where(mine & (lane < 3 * heads), tiled, 0.0), -1, keepdims=True)
        delta = jnp.sum(
            jnp.where(mine & (lane >= 3 * heads) & (lane < 6 * heads), tiled, 0.0),
            -1,
            keepdims=True,
        )
        wide = spread_heads(query[:, cols] * bf16(HEAD**-0.5))
        wide_grad = spread_heads(grad[:, cols])
        probs = jnp.exp(masked_scores(wide, kp[0, :, cols], frames, first, count) - level)
        prob_grad = mul(wide_grad, vp[0, :, cols], NT)
        score_grad = (probs * (prob_grad - delta)).astype(bf16)
        kv_t_o[pl.ds(g * GROUP, GROUP), :] = mul(wide, score_grad, TN).astype(bf16)
        kv_t_o[pl.ds(inner + g * GROUP, GROUP), :] = mul(
            wide_grad, probs.astype(bf16), TN
        ).astype(bf16)
        lat_probs = jnp.exp(mul(wide, kl[:, cols], NT) - level)
        lat_prob_grad = mul(wide_grad, vl[:, cols], NT)
        lat_score_grad = (lat_probs * (lat_prob_grad - delta)).astype(bf16)
        kl_o[:, cols] = mul(lat_score_grad, wide, TN).astype(bf16)
        vl_o[:, cols] = mul(lat_probs.astype(bf16), wide_grad, TN).astype(bf16)
        query_grad = mul(score_grad, kp[0, :, cols]) + mul(lat_score_grad, kl[:, cols])
        query_grad = (fold_heads(query_grad) * HEAD**-0.5).astype(bf16)
        for s in range(n_keys):
            q_o[s][:, cols] = query_grad[s * own : (s + 1) * own]


def weight_kernel(n_keys, scalars, k_t, v_t, low, kl_t, lat_low, *refs):
    q_grads = refs[:n_keys]
    lats = refs[n_keys : 2 * n_keys]
    out = refs[-1]
    vl_t = refs[-2]
    width = k_t.shape[0]
    kv = jnp.concatenate([k_t[...], v_t[...]], 0)
    kv_lat = jnp.concatenate([kl_t[...], vl_t[...]], 1)
    total = mul(kv, low[...]) + mul(kv_lat, lat_low[...], TN)
    query = jnp.concatenate([r[...] for r in q_grads], 0)
    lat_all = jnp.concatenate([r[...] for r in lats], 0)
    out[0, :width, :] = mul(query, lat_all, TN).astype(bf16)
    out[0, width:, :] = total.astype(bf16)


def patch_back_kernel(frames, n_frames, scalars, kv_t, patches, time, gain, wk, wv, grad_o, small_o):
    inner = wk.shape[1]

    @pl.when(pl.program_id(0) == 0)
    def _():
        small_o[...] = jnp.zeros_like(small_o)

    for f in range(frames):
        rows = pl.ds(f * PATCH, PATCH)
        span = slice(f * PATCH, (f + 1) * PATCH)
        grad = mul(kv_t[:inner, span], wk[...], ((0,), (1,)))
        grad = grad + mul(kv_t[inner:, span], wv[...], ((0,), (1,)))
        framed = patches[0, rows, :].astype(f32) + time[0, f : f + 1, :]
        back, gain_grad, bias_grad = norm_back(framed, gain[...], grad)
        grad_o[0, rows, :] = back.astype(bf16)
        slot = pl.ds(scalars[0] * frames + f, 1)
        small_o[slot, :] += jnp.sum(back, 0, keepdims=True)
        small_o[n_frames : n_frames + 1, :] += gain_grad
        small_o[n_frames + 1 : n_frames + 2, :] += bias_grad


def latent_back_kernel(n_keys, latents, gain, mid_grad, kl_g, vl_g, wq, wk, wv, *refs):
    slots = refs[:n_keys]
    lat_o, gain_o, bias_o = refs[n_keys:]
    query = functools.reduce(jnp.add, [r[...].astype(f32) for r in slots]).astype(bf16)
    grad = mul(query, wq[...], NT) + mul(kl_g[...], wk[...], NT) + mul(vl_g[...], wv[...], NT)
    back, gain_grad, bias_grad = norm_back(latents[...], gain[...], grad)
    lat_o[...] = mid_grad[...] + back
    gain_o[...] = gain_grad
    bias_o[...] = bias_grad


def whole(shape):
    return pl.BlockSpec(shape, lambda *_: (0,) * len(shape))


def struct(shape, dtype):
    return jax.ShapeDtypeStruct(shape, dtype)


def tree_sum(parts):
    while len(parts) > 1:
        parts = [parts[i] + parts[i + 1] for i in range(0, len(parts), 2)]
    return parts[0]


def shards(
    n_media,
    n_keys,
    latents,
    patches,
    frame_counts,
    time_embedding,
    media_gain,
    media_bias,
    latent_gain,
    latent_bias,
    ff_gain,
    ff_bias,
    query_weight,
    key_weight,
    value_weight,
    out_weight,
    up_weight,
    down_weight,
    cotangent,
):
    media, own, dim = latents.shape
    key_rows = patches.shape[1]
    inner = query_weight.shape[1]
    hidden = up_weight.shape[1]
    frames = key_rows // PATCH
    n_frames = time_embedding.shape[0]
    rows = media * own
    n_far = n_media // PAIR
    width = inner // n_keys
    m_index = lax.axis_index("media")
    k_index = lax.axis_index("keys")
    near = m_index % PAIR
    far = m_index // PAIR
    scalars = k_index.astype(jnp.int32).reshape(1)

    def over_keys(value, shift):
        return lax.ppermute(value, "keys", [(i, i ^ shift) for i in range(n_keys)])

    def over_media(value, shift):
        return lax.ppermute(value, "media", [(i, i ^ shift) for i in range(n_media)])

    def gather_keys(value):
        slots = [None] * n_keys
        for s in range(0, n_keys, 2):
            slots[s] = value if s == 0 else over_keys(value, s)
        for s in range(0, n_keys, 2):
            slots[s + 1] = over_keys(slots[s], 1)
        return slots

    def gather_near(value):
        return gather_keys(value) + gather_keys(over_media(value, 1))

    def scatter_keys(slots):
        kept = [
            (slots[s].astype(f32) + over_keys(slots[s + 1], 1).astype(f32))
            for s in range(0, n_keys, 2)
        ]
        total = kept[0]
        for s in range(2, n_keys, 2):
            total = total + over_keys(kept[s // 2].astype(bf16), s).astype(f32)
        return total.astype(bf16)

    def scatter_far(parts):
        total = lax.dynamic_index_in_dim(parts, far, 0, False).astype(f32)
        for s in range(1, n_far):
            part = lax.dynamic_index_in_dim(parts, far ^ s, 0, False)
            total = total + over_media(part, PAIR * s).astype(f32)
        return total

    def scatter_media(value, axis):
        shape = value.shape
        each = shape[axis] // n_media
        parts = value.reshape(shape[:axis] + (n_far, PAIR, each) + shape[axis + 1 :])
        keep = lax.dynamic_index_in_dim(parts, near, axis + 1, False)
        send = lax.dynamic_index_in_dim(parts, 1 - near, axis + 1, False)
        half = (keep.astype(f32) + over_media(send, 1).astype(f32)).astype(bf16)
        return scatter_far(jnp.moveaxis(half, axis, 0))

    def everywhere(value):
        total = tree_sum([value] + [over_media(value, s) for s in range(1, n_media)])
        return tree_sum([total] + [over_keys(total, s) for s in range(1, n_keys)])

    lat = latents.reshape(rows, dim)
    cot = cotangent.reshape(rows, dim)
    row = lambda v: v.reshape(1, dim)
    time_blocks = time_embedding.reshape(n_keys, frames, dim)

    lat_low, q_own, kl, vl, out_low = pl.pallas_call(
        latent_kernel,
        name="latent_project",
        out_shape=(
            struct((rows, dim), bf16),
            struct((rows, inner), bf16),
            struct((rows, inner), bf16),
            struct((rows, inner), bf16),
            struct((rows, dim), bf16),
        ),
        compiler_params=params(24),
        cost_estimate=cost(6 * rows * dim * inner, 6 * dim * inner + 14 * rows * dim),
    )(lat, row(latent_gain), row(latent_bias), cot, query_weight, key_weight, value_weight)
    q_all = gather_keys(q_own)
    lat_all = gather_keys(lat_low)
    out_all = gather_near(out_low)

    patch_block = pl.BlockSpec((1, key_rows, dim), lambda i, *_: (i, 0, 0))
    inner_block = pl.BlockSpec((1, key_rows, inner), lambda i, *_: (i, 0, 0))
    time_block = pl.BlockSpec((1, frames, dim), lambda i, s, *_: (s[0], 0, 0))
    patch_flops = 4 * media * key_rows * dim * inner
    media_low, kp, vp = pl.pallas_call(
        lambda scalars, *refs: patch_kernel(frames, *refs),
        name="patch_project",
        grid_spec=pltpu.PrefetchScalarGridSpec(
            num_scalar_prefetch=1,
            grid=(media,),
            in_specs=[
                patch_block,
                time_block,
                whole((1, dim)),
                whole((1, dim)),
                whole((dim, inner)),
                whole((dim, inner)),
            ],
            out_specs=[patch_block, inner_block, inner_block],
        ),
        out_shape=(
            struct(patches.shape, bf16),
            struct((media, key_rows, inner), bf16),
            struct((media, key_rows, inner), bf16),
        ),
        compiler_params=params(40),
        cost_estimate=cost(patch_flops, 12 * media * key_rows * dim),
    )(scalars, patches, time_blocks, row(media_gain), row(media_bias), key_weight, value_weight)

    own_block = lambda w: pl.BlockSpec((own, w), lambda i, *_: (i, 0))
    packed = inner + LANES
    att_flops = 4 * media * n_keys * own * (key_rows + own) * inner * (GROUP // HEAD)
    shares = pl.pallas_call(
        functools.partial(attend_kernel, n_keys, frames),
        name="attend",
        grid_spec=pltpu.PrefetchScalarGridSpec(
            num_scalar_prefetch=2,
            grid=(media,),
            in_specs=[own_block(inner)] * n_keys
            + [inner_block, inner_block, own_block(inner), own_block(inner)],
            out_specs=[own_block(packed)] * n_keys,
        ),
        out_shape=[struct((rows, packed), bf16)] * n_keys,
        compiler_params=params(24),
        cost_estimate=cost(att_flops, 4 * media * key_rows * inner),
    )(scalars, frame_counts, *q_all, kp, vp, kl, vl)
    joined = [shares[0]] + [over_keys(shares[s], s) for s in range(1, n_keys)]

    attended, att_low, middle, ff_low, lse = pl.pallas_call(
        functools.partial(join_kernel, n_keys),
        name="join",
        out_shape=(
            struct((rows, inner), f32),
            struct((rows, inner), bf16),
            struct((rows, dim), f32),
            struct((rows, dim), bf16),
            struct((rows, LANES), f32),
        ),
        compiler_params=params(16),
        cost_estimate=cost(2 * rows * inner * dim, 2 * inner * dim + 16 * rows * dim),
    )(lat, row(ff_gain), row(ff_bias), out_weight, *joined)
    ff_all = gather_near(ff_low)

    chunk = min(512, hidden)
    steps = hidden // chunk
    resampled, mid_grad, pack, ff_gain_grad, ff_bias_grad, out_partial = pl.pallas_call(
        functools.partial(forward_kernel, n_keys),
        name="feed_forward",
        grid_spec=pltpu.PrefetchScalarGridSpec(
            num_scalar_prefetch=1,
            grid=(steps,),
            in_specs=[
                whole((rows, inner)),
                whole((rows, inner)),
                whole((rows, dim)),
                whole((rows, dim)),
                whole((rows, LANES)),
                whole((rows, dim)),
                whole((rows, dim)),
                whole((1, dim)),
                whole((inner, dim)),
                pl.BlockSpec((dim, chunk), lambda i, *_: (0, i)),
                pl.BlockSpec((chunk, dim), lambda i, *_: (i, 0)),
            ],
            out_specs=[
                whole((rows, dim)),
                whole((rows, dim)),
                whole((rows, packed)),
                whole((1, dim)),
                whole((1, dim)),
                whole((inner, dim)),
            ],
            scratch_shapes=[pltpu.VMEM((rows, dim), f32), pltpu.VMEM((rows, dim), f32)],
        ),
        out_shape=(
            struct((rows, dim), f32),
            struct((rows, dim), f32),
            struct((rows, packed), bf16),
            struct((1, dim), f32),
            struct((1, dim), f32),
            struct((inner, dim), bf16),
        ),
        compiler_params=params(32),
        cost_estimate=cost(8 * rows * dim * hidden, 4 * dim * hidden + 24 * rows * dim),
    )(
        scalars,
        attended,
        att_low,
        middle,
        ff_low,
        lse,
        cot,
        out_low,
        row(ff_gain),
        out_weight,
        up_weight,
        down_weight,
    )
    packs = gather_keys(pack)

    units = hidden // (n_keys * PAIR)
    slice_index = (k_index * PAIR + near).astype(jnp.int32).reshape(1)
    n_slots = PAIR * n_keys
    up_partial, down_partial = pl.pallas_call(
        lambda s, *refs: ff_grad_kernel(n_slots, *refs),
        name="feed_forward_weights",
        grid_spec=pltpu.PrefetchScalarGridSpec(
            num_scalar_prefetch=1,
            grid=(1,),
            in_specs=[whole((rows, dim))] * (2 * n_slots)
            + [
                pl.BlockSpec((dim, units), lambda i, s: (0, s[0])),
                pl.BlockSpec((units, dim), lambda i, s: (s[0], 0)),
            ],
            out_specs=[whole((units, dim)), whole((units, dim))],
        ),
        out_shape=(struct((units, dim), bf16), struct((units, dim), bf16)),
        compiler_params=params(40),
        cost_estimate=cost(
            8 * n_slots * rows * dim * units, 8 * dim * units + 4 * n_slots * rows * dim
        ),
    )(slice_index, *ff_all, *out_all, up_weight, down_weight)
    each = dim // n_media
    up_parts = jnp.moveaxis(up_partial.reshape(units, n_far, PAIR * each), 1, 0)
    up_sum = scatter_far(up_parts).astype(bf16).reshape(units, PAIR, each)
    up_keep = lax.dynamic_index_in_dim(up_sum, near, 1, False)
    up_send = lax.dynamic_index_in_dim(up_sum, 1 - near, 1, False)
    up_got = over_media(up_send, 1)
    up_grad = jnp.where(
        near == 0,
        jnp.concatenate([up_keep, up_got], 0),
        jnp.concatenate([up_got, up_keep], 0),
    ).T.astype(f32)
    blocks = n_far // n_keys
    down_parts = down_partial.reshape(blocks, units // blocks, n_keys, dim // n_keys)
    down_parts = down_parts.transpose(0, 2, 1, 3).reshape(
        n_far, units // blocks, dim // n_keys
    )
    down_sum = scatter_far(down_parts).astype(bf16)
    route = []
    for m in range(n_media):
        for k in range(n_keys):
            block, owner = divmod(m // PAIR, n_keys)
            target = (k * PAIR + m % PAIR) * blocks + block
            route.append((m * n_keys + k, target * n_keys + owner))
    down_grad = lax.ppermute(down_sum, ("media", "keys"), route).astype(f32)

    back = pl.pallas_call(
        functools.partial(attend_back_kernel, n_keys, frames),
        name="attend_back",
        grid_spec=pltpu.PrefetchScalarGridSpec(
            num_scalar_prefetch=2,
            grid=(media,),
            in_specs=[own_block(inner)] * n_keys
            + [own_block(packed)] * n_keys
            + [inner_block, inner_block, own_block(inner), own_block(inner)],
            out_specs=[
                pl.BlockSpec((2 * inner, key_rows), lambda i, *_: (0, i)),
                own_block(inner),
                own_block(inner),
            ]
            + [own_block(inner)] * n_keys,
        ),
        out_shape=[
            struct((2 * inner, media * key_rows), bf16),
            struct((rows, inner), bf16),
            struct((rows, inner), bf16),
        ]
        + [struct((rows, inner), bf16)] * n_keys,
        compiler_params=params(40),
        cost_estimate=cost(5 * att_flops // 2, 8 * media * key_rows * inner),
    )(scalars, frame_counts, *q_all, *packs, kp, vp, kl, vl)
    kv_t, kl_grad, vl_grad = back[:3]
    q_partial = back[3:]
    q_slots = [q_partial[0]] + [over_keys(q_partial[s], s) for s in range(1, n_keys)]

    all_rows = media * key_rows
    slot_rows = lambda base: pl.BlockSpec(
        (width, all_rows), lambda i, s, base=base: (base + (s[0] ^ i), 0)
    )
    slot_cols = pl.BlockSpec((rows, width), lambda i, s: (0, s[0] ^ i))
    if width % LANES == 0:
        kl_cols, vl_cols, q_cols, cols_spec = kl_grad, vl_grad, q_partial, slot_cols
    else:
        cut = lambda v: v.reshape(rows, n_keys, width).transpose(1, 0, 2)
        kl_cols, vl_cols, q_cols = cut(kl_grad), cut(vl_grad), [cut(v) for v in q_partial]
        cols_spec = pl.BlockSpec((None, rows, width), lambda i, s: (s[0] ^ i, 0, 0))
    w_slots = pl.pallas_call(
        functools.partial(weight_kernel, n_keys),
        name="projection_weights",
        grid_spec=pltpu.PrefetchScalarGridSpec(
            num_scalar_prefetch=1,
            grid=(n_keys,),
            in_specs=[
                slot_rows(0),
                slot_rows(n_keys),
                whole((all_rows, dim)),
                cols_spec,
                whole((rows, dim)),
            ]
            + [cols_spec] * n_keys
            + [whole((rows, dim))] * n_keys
            + [cols_spec],
            out_specs=pl.BlockSpec((1, 3 * width, dim), lambda i, s: (i, 0, 0)),
        ),
        out_shape=struct((n_keys, 3 * width, dim), bf16),
        compiler_params=params(48),
        cost_estimate=cost(patch_flops, 4 * media * key_rows * dim),
    )(
        scalars,
        kv_t,
        kv_t,
        media_low.reshape(all_rows, dim),
        kl_cols,
        lat_low,
        *q_cols,
        *lat_all,
        vl_cols,
    )
    w_sum = scatter_keys([w_slots[s] for s in range(n_keys)])
    w_grads = scatter_media(w_sum, 1).reshape(3, width, each).transpose(0, 2, 1)

    out_slots = out_partial.reshape(inner, n_keys, dim // n_keys)
    out_slots = [
        lax.dynamic_index_in_dim(out_slots, k_index ^ s, 1, False) for s in range(n_keys)
    ]
    out_grad = scatter_media(scatter_keys(out_slots), 0)

    small_rows = -(-(n_frames + 2) // 8) * 8
    patches_grad, small = pl.pallas_call(
        functools.partial(patch_back_kernel, frames, n_frames),
        name="patch_back",
        grid_spec=pltpu.PrefetchScalarGridSpec(
            num_scalar_prefetch=1,
            grid=(media,),
            in_specs=[
                pl.BlockSpec((2 * inner, key_rows), lambda i, *_: (0, i)),
                patch_block,
                time_block,
                whole((1, dim)),
                whole((dim, inner)),
                whole((dim, inner)),
            ],
            out_specs=[patch_block, whole((small_rows, dim))],
        ),
        out_shape=(struct(patches.shape, bf16), struct((small_rows, dim), f32)),
        compiler_params=params(40),
        cost_estimate=cost(patch_flops, 8 * media * key_rows * dim),
    )(scalars, kv_t, patches, time_blocks, row(media_gain), key_weight, value_weight)

    latents_grad, lat_gain_grad, lat_bias_grad = pl.pallas_call(
        functools.partial(latent_back_kernel, n_keys),
        name="latent_back",
        out_shape=(struct((rows, dim), f32), struct((1, dim), f32), struct((1, dim), f32)),
        compiler_params=params(24),
        cost_estimate=cost(6 * rows * dim * inner, 6 * dim * inner + 20 * rows * dim),
    )(
        lat,
        row(latent_gain),
        mid_grad,
        kl_grad,
        vl_grad,
        query_weight,
        key_weight,
        value_weight,
        *q_slots,
    )

    early = everywhere(
        jnp.concatenate([ff_gain_grad, ff_bias_grad, lat_gain_grad, lat_bias_grad], 0)
    )
    late = everywhere(small[: n_frames + 2])
    return (
        resampled.reshape(latents.shape),
        patches_grad,
        latents_grad.reshape(latents.shape),
        late[:n_frames],
        late[n_frames],
        late[n_frames + 1],
        early[2],
        early[3],
        early[0],
        early[1],
        w_grads[0],
        w_grads[1],
        w_grads[2],
        out_grad,
        up_grad,
        down_grad,
    )


def solution(mesh):
    split = P("media", "keys", None)
    return jax.shard_map(
        functools.partial(shards, mesh.shape["media"], mesh.shape["keys"]),
        mesh=mesh,
        in_specs=(split, split, P("media")) + (P(),) * 13 + (split,),
        out_specs=(split,) * 3 + (P(),) * 7 + (P("media", "keys"),) * 6,
        check_vma=False,
    )
```

```python
import functools

import jax
import jax.numpy as jnp
from jax import lax
from jax.experimental import pallas as pl
from jax.experimental.pallas import tpu as pltpu
from jax.sharding import Mesh, PartitionSpec as P

HEAD = 64
PATCH = 256
GROUP = 256
LANES = 128

VMEM_LIMIT = 60 << 20

EPS = 1e-05
NEG = -1e30
PAIR = 2

f32 = jnp.float32
bf16 = jnp.bfloat16


def mul(left, right, contract=((1,), (0,)), precision=None):
    return lax.dot_general(
        left, right, (contract, ((), ())), precision=precision, preferred_element_type=f32
    )


NN = ((1,), (0,))
NT = ((1,), (1,))
TN = ((0,), (0,))


def norm_parts(values):
    centre = jnp.mean(values, -1, keepdims=True)
    shifted = values - centre
    spread = jnp.mean(shifted * shifted, -1, keepdims=True)
    return centre, lax.rsqrt(spread + EPS), shifted


def norm(values, gain, bias):
    _, scale, shifted = norm_parts(values)
    return shifted * scale * gain + bias


def norm_back(values, gain, grad):
    _, scale, shifted = norm_parts(values)
    unit = shifted * scale
    scaled = grad * gain
    first = jnp.mean(scaled, -1, keepdims=True)
    second = jnp.mean(scaled * unit, -1, keepdims=True)
    back = scale * (scaled - first - unit * second)
    return (
        back,
        jnp.sum(grad * unit, 0, keepdims=True),
        jnp.sum(grad, 0, keepdims=True),
    )


def gelu_parts(hidden):
    cdf = 0.5 * (1.0 + lax.erf(hidden * (2.0**-0.5)))
    pdf = jnp.exp(-0.5 * hidden * hidden) * 0.3989422804014327
    return cdf, cdf + hidden * pdf


def head_mask(rows, width, heads):
    row = lax.broadcasted_iota(jnp.int32, (heads * rows, width), 0) // rows
    col = lax.broadcasted_iota(jnp.int32, (heads * rows, width), 1)
    return row, col


def spread_heads(values):
    heads = values.shape[1] // HEAD
    row, col = head_mask(values.shape[0], values.shape[1], heads)
    return jnp.where(row == col // HEAD, jnp.concatenate([values] * heads, 0), jnp.zeros((), values.dtype))


def fold_heads(values):
    heads = values.shape[1] // HEAD
    rows = values.shape[0] // heads
    row, col = head_mask(rows, values.shape[1], heads)
    kept = jnp.where(row == col // HEAD, values, 0.0)
    total = kept[:rows]
    for h in range(1, heads):
        total = total + kept[h * rows : (h + 1) * rows]
    return total


def three_parts(values, lane, start, slots):
    high = values.astype(bf16).astype(f32)
    rest = values - high
    middle = rest.astype(bf16).astype(f32)
    low = rest - middle
    place = lane // slots - start
    return jnp.where(place == 0, high, jnp.where(place == 1, middle, jnp.where(place == 2, low, 0.0)))


def cost(flops, moved, special=0):
    return pl.CostEstimate(flops=int(flops), bytes_accessed=int(moved), transcendentals=int(special))


def params():
    return pltpu.CompilerParams(vmem_limit_bytes=VMEM_LIMIT)


def tie(*values):
    return lax.optimization_barrier(values)


def latent_kernel(_, lat, gain, bias, cot, wq, rows_o, q_o):
    dim = lat.shape[1]
    low = norm(lat[...], gain[...], bias[...]).astype(bf16)
    rows_o[:, :dim] = low
    rows_o[:, dim:] = cot[...].astype(bf16)
    q_o[...] = mul(low, wq[...]).astype(bf16)


def two_parts(values):
    high = values.astype(bf16)
    return high, (values - high.astype(f32)).astype(bf16)


def patch_kernel(
    frames, scalars, patches, time, gain, bias, wk, wv, lat_low, low_o, k_o, v_o, kl_o, vl_o, stat_o, once_o, vec_o
):
    for f in range(frames):
        rows = pl.ds(f * PATCH, PATCH)
        framed = patches[0, rows, :].astype(f32) + time[0, f : f + 1, :]
        centre, scale, shifted = norm_parts(framed)
        low = (shifted * scale * gain[...] + bias[...]).astype(bf16)
        low_o[0, rows, :] = low
        k_o[0, rows, :] = mul(low, wk[...]).astype(bf16)
        v_o[0, rows, :] = mul(low, wv[...]).astype(bf16)
        lane = lax.broadcasted_iota(jnp.int32, (PATCH, LANES), 1)
        stat = jnp.where(lane == 0, centre, jnp.where(lane == 1, scale, 0.0))
        stat_o[:, f * PATCH : (f + 1) * PATCH] = stat.T[:8]
        high = scale.astype(bf16).astype(f32)
        once = jnp.where(lane == 0, 1.0, jnp.where(lane == 1 + f, high, 0.0))
        once_o[0, rows, :] = jnp.where(lane == 1 + frames + f, scale - high, once).astype(bf16)

    @pl.when(pl.program_id(0) == pl.num_programs(0) - 1)
    def _():
        kl_o[...] = mul(lat_low[...], wk[...]).astype(bf16)
        vl_o[...] = mul(lat_low[...], wv[...]).astype(bf16)
        row = lax.broadcasted_iota(jnp.int32, (16, gain.shape[1]), 0)
        both = jnp.where(row % 2 == 0, gain[...], bias[...])
        high, low = two_parts(both)
        both = jnp.where(row < 2, high.astype(f32), jnp.where(row < 4, low.astype(f32), 0.0)).astype(bf16)
        for i, w in enumerate((wk, wv)):
            term = mul(both, w[...])
            vec_o[:, i * w.shape[1] : (i + 1) * w.shape[1]] = term[:8] + pltpu.roll(term, 14, 0)[:8]


def masked_scores(query, keys, frames, first, count):
    scores = mul(query, keys, NT)
    parts = []
    for f in range(frames):
        part = scores[:, f * PATCH : (f + 1) * PATCH]
        parts.append(jnp.where(first + f < count, part, NEG))
    return jnp.concatenate(parts, 1) if frames > 1 else parts[0]


def attend_kernel(n_keys, frames, scalars, counts, *refs):
    q = refs[:n_keys]
    kp, vp, kl, vl = refs[n_keys : n_keys + 4]
    outs = refs[n_keys + 4 :]
    own = q[0].shape[0]
    inner = q[0].shape[1]
    heads = inner // HEAD
    count = counts[pl.program_id(0)]
    first = scalars[0] * frames
    query = jnp.concatenate([r[...] for r in q], 0)
    rows = query.shape[0]
    stats = jnp.zeros((rows, LANES), f32)
    shares = []
    for g in range(inner // GROUP):
        cols = slice(g * GROUP, (g + 1) * GROUP)
        wide = spread_heads(query[:, cols] * bf16(HEAD**-0.5))
        scores = masked_scores(wide, kp[0, :, cols], frames, first, count)
        lat_scores = mul(wide, kl[:, cols], NT)
        top = jnp.maximum(
            jnp.max(scores, -1, keepdims=True), jnp.max(lat_scores, -1, keepdims=True)
        )
        raw = jnp.exp(scores - top)
        lat_raw = jnp.exp(lat_scores - top)
        total = jnp.sum(raw, -1, keepdims=True) + jnp.sum(lat_raw, -1, keepdims=True)
        share = mul(raw.astype(bf16), vp[0, :, cols]) + mul(lat_raw.astype(bf16), vl[:, cols])
        shares.append(fold_heads(share / total).astype(bf16))
        level = top + jnp.log(total)
        row, lane = head_mask(rows, LANES, GROUP // HEAD)
        kept = jnp.where(lane % heads == row + g * (GROUP // HEAD), level, 0.0)
        for h in range(GROUP // HEAD):
            stats = stats + kept[h * rows : (h + 1) * rows]
    lane = lax.broadcasted_iota(jnp.int32, stats.shape, 1)
    packed = jnp.concatenate(shares + [three_parts(stats, lane, 0, heads).astype(bf16)], 1)
    for s in range(n_keys):
        outs[s][...] = packed[s * own : (s + 1) * own]


def sum_runs(stats, heads, start):
    total = None
    for part in range(3):
        shift = (-(start + part) * heads) % LANES
        term = pltpu.roll(stats, shift, 1) if shift else stats
        total = term if total is None else total + term
    return total


def join_kernel(n_keys, _, latents, gain, bias, wo, *refs):
    slots = refs[:n_keys]
    att_o, low_o, mid_o, ff_o, lse_o = refs[n_keys:]
    inner = att_o.shape[1]
    heads = inner // HEAD
    levels = [sum_runs(r[:, inner:].astype(f32), heads, 0) for r in slots]
    top = functools.reduce(jnp.maximum, levels)
    weights = [jnp.exp(v - top) for v in levels]
    total = functools.reduce(jnp.add, weights)
    inverse = 1.0 / total
    lane = lax.broadcasted_iota(jnp.int32, (LANES, inner), 0)
    col = lax.broadcasted_iota(jnp.int32, (LANES, inner), 1)
    select = jnp.where(lane == col // HEAD, 1.0, 0.0)
    attended = None
    for s in range(n_keys):
        wide = mul(weights[s] * inverse, select, NN, lax.Precision.HIGHEST)
        term = wide * slots[s][:, :inner].astype(f32)
        attended = term if attended is None else attended + term
    low = attended.astype(bf16)
    middle = latents[...] + mul(low, wo[...])
    att_o[...] = attended
    low_o[...] = low
    mid_o[...] = middle
    ff_o[...] = norm(middle, gain[...], bias[...]).astype(bf16)
    lse_o[...] = top + jnp.log(total)


def forward_kernel(
    n_keys,
    aligned,
    scalars,
    attended,
    att_low,
    middle,
    ff_low,
    lse,
    cot,
    out_low,
    gain,
    wo,
    up,
    down,
    res_o,
    mid_grad_o,
    pack_o,
    small_o,
    wo_grad_o,
    res_acc,
    in_acc,
    wo_acc,
):
    step = pl.program_id(0)

    @pl.when(step == 0)
    def _():
        res_acc[...] = jnp.zeros_like(res_acc)
        in_acc[...] = jnp.zeros_like(in_acc)

    hidden = mul(ff_low[...], up[...])
    act_grad = mul(out_low[...], down[...], NT)
    cdf, slope = gelu_parts(hidden)
    res_acc[...] += mul((hidden * cdf).astype(bf16), down[...])
    in_acc[...] += mul((act_grad * slope).astype(bf16), up[...], NT)

    @pl.when(step == pl.num_programs(0) - 1)
    def _():
        inner = attended.shape[1]
        heads = inner // HEAD
        res_o[...] = middle[...] + res_acc[...]
        back, gain_grad, bias_grad = norm_back(middle[...], gain[...], in_acc[...])
        small_o[0:1, :] = gain_grad
        small_o[1:2, :] = bias_grad
        mid_grad = cot[...] + back
        mid_grad_o[...] = mid_grad
        branch = mid_grad.astype(bf16)
        att_grad = mul(branch, wo[...], NT).astype(bf16)
        col = lax.broadcasted_iota(jnp.int32, (inner, LANES), 0)
        lane = lax.broadcasted_iota(jnp.int32, (inner, LANES), 1)
        select = jnp.where(col // HEAD == lane % heads, 1.0, 0.0)
        delta = mul(attended[...] * att_grad.astype(f32), select, NN, lax.Precision.HIGHEST)
        lane = lax.broadcasted_iota(jnp.int32, delta.shape, 1)
        level = jnp.where(lane < heads, lse[...], 0.0)
        level = level + pltpu.roll(level, heads, 1) + pltpu.roll(level, 2 * heads, 1)
        stats = three_parts(level, lane, 0, heads) + three_parts(delta, lane, 3, heads)
        pack_o[...] = jnp.concatenate([att_grad, stats.astype(bf16)], 1)
        wo_grad = mul(att_low[...], branch, TN)
        if aligned:
            wo_acc[...] = wo_grad
            slot_rows(scalars, wo_acc, wo_grad_o, n_keys)
        else:
            wo_grad_o[...] = wo_grad.astype(bf16)


def slot_rows(scalars, full, out, n_keys):
    lanes = LANES
    n_media = out.shape[2] // lanes
    r = full.shape[0] // n_media
    c = full.shape[1] // n_keys
    for s in range(n_keys):
        owner = (scalars[0] ^ s) * c
        for m in range(n_media):
            place = (scalars[2] ^ (m // PAIR)) * PAIR + m % PAIR
            place = pl.ds(pl.multiple_of(place * lanes, lanes), lanes)
            for h in range(c // lanes):
                start = pl.multiple_of(owner + h * lanes, lanes)
                out[s, h * r : (h + 1) * r, place] = full[
                    m * r : (m + 1) * r, pl.ds(start, lanes)
                ].astype(bf16)


def ff_grad_kernel(aligned, scalars, ff_all, out_all, up, down, grad_o):
    units, dim = down.shape
    hidden = mul(ff_all[...], up[...])
    act_grad = mul(out_all[...], down[...], NT)
    cdf, slope = gelu_parts(hidden)
    grad_o[units:, :] = mul((hidden * cdf).astype(bf16), out_all[...], TN).astype(bf16)
    up_grad = mul((act_grad * slope).astype(bf16), ff_all[...], TN).astype(bf16)
    if aligned:
        for j in range(dim // LANES):
            place = ((j // PAIR) * PAIR + (scalars[1] ^ (j % PAIR))) * LANES
            grad_o[:units, pl.ds(pl.multiple_of(place, LANES), LANES)] = up_grad[
                :, j * LANES : (j + 1) * LANES
            ]
    else:
        grad_o[:units, :] = up_grad


def attend_back_kernel(n_keys, frames, turn, heads, scalars, counts, *refs):
    q = refs[:n_keys]
    grads = refs[n_keys : 2 * n_keys]
    stat = refs[2 * n_keys : 3 * n_keys]
    kp, vp, kl, vl, k_vec, v_vec = refs[3 * n_keys : 3 * n_keys + 6]
    n_out = 4 + n_keys
    kv_t_o, stat_o, kl_o, vl_o = refs[-n_out : -n_keys]
    q_o = refs[-n_keys:]
    q_before = refs[3 * n_keys + 6 : -n_out]
    own = q[0].shape[0]
    per = GROUP // HEAD
    count = counts[pl.program_id(0)]
    first = scalars[0] * frames
    group = scalars[5] ^ (1 - turn)
    query = jnp.concatenate([r[...] for r in q], 0)
    grad = jnp.concatenate([r[...] for r in grads], 0)
    stats = jnp.concatenate([r[...] for r in stat], 0).astype(f32)
    rows = query.shape[0]
    row, lane = head_mask(rows, LANES, per)
    tiled = jnp.concatenate([stats] * per, 0)
    mine = lane % heads == row + group * per
    level = jnp.sum(jnp.where(mine & (lane < 3 * heads), tiled, 0.0), -1, keepdims=True)
    delta = jnp.sum(
        jnp.where(mine & (lane >= 3 * heads) & (lane < 6 * heads), tiled, 0.0), -1, keepdims=True
    )
    wide = spread_heads(query * bf16(HEAD**-0.5))
    wide_grad = spread_heads(grad)
    scores = masked_scores(wide, kp[0], frames, first, count)
    probs = jnp.exp(scores - level)
    prob_grad = mul(wide_grad, vp[0], NT)
    score_grad = probs * (prob_grad - delta)
    along = jnp.sum(score_grad * scores + probs * prob_grad, 0, keepdims=True)
    score_grad = score_grad.astype(bf16)
    key_side = jnp.concatenate([wide, mul(wide, k_vec[...].astype(bf16), NT).astype(bf16)], 1)
    value_side = jnp.concatenate(
        [wide_grad, mul(wide_grad, v_vec[...].astype(bf16), NT).astype(bf16)], 1
    )
    key_t = mul(key_side, score_grad, TN)
    value_t = mul(value_side, probs.astype(bf16), TN)
    kv_t_o[0] = key_t[:GROUP].astype(bf16)
    kv_t_o[1] = value_t[:GROUP].astype(bf16)
    ends = key_t[GROUP:] + value_t[GROUP:]
    line = lax.broadcasted_iota(jnp.int32, ends.shape, 0)
    stat_o[...] = jnp.where(line == 1, along - ends, ends)
    lat_probs = jnp.exp(mul(wide, kl[...], NT) - level)
    lat_prob_grad = mul(wide_grad, vl[...], NT)
    lat_score_grad = (lat_probs * (lat_prob_grad - delta)).astype(bf16)
    kl_o[...] = mul(lat_score_grad, wide, TN).astype(bf16)
    vl_o[...] = mul(lat_probs.astype(bf16), wide_grad, TN).astype(bf16)
    query_grad = mul(score_grad, kp[0]) + mul(lat_score_grad, kl[...])
    query_grad = (fold_heads(query_grad) * HEAD**-0.5).astype(bf16)
    if turn == 0:
        for s in range(n_keys):
            q_o[s][...] = query_grad[s * own : (s + 1) * own]
    else:
        here = pl.ds(pl.multiple_of(group * GROUP, GROUP), GROUP)
        there = pl.ds(pl.multiple_of((1 - group) * GROUP, GROUP), GROUP)
        for s in range(n_keys):
            q_o[s][:, here] = query_grad[s * own : (s + 1) * own]
            q_o[s][:, there] = q_before[s][...]


def weight_kernel(
    n_keys,
    turn,
    width,
    frames,
    aligned,
    scalars,
    kv_t,
    low,
    kl_g,
    vl_g,
    lat_own,
    rows_all,
    wo_g,
    once,
    norm_stat,
    grad_stat,
    wk,
    wv,
    gain,
    bias,
    *refs,
):
    q_grads = refs[:n_keys]
    before = refs[n_keys:-5]
    given, kept, small, total, sums = refs[-5:]
    rows = q_grads[0].shape[0]
    per = GROUP // width
    kv = jnp.concatenate([kv_t[0], kv_t[1]], 0)
    keys = kv.shape[1]

    @pl.when(pl.program_id(0) == 0)
    def _():
        sums[...] = mul(kv, once[...])

    inverse = 1.0 / (scalars[6].astype(f32))
    scale = norm_stat[1:2, :] * inverse
    first = grad_stat[0:1, :] * scale
    second = grad_stat[1:2, :] * scale
    frame = (lax.broadcasted_iota(jnp.int32, (16, keys), 1) // PATCH) % frames
    row = lax.broadcasted_iota(jnp.int32, (16, keys), 0)
    high = second.astype(bf16).astype(f32)
    mine = frame == row % frames
    ends = jnp.where(mine & (row < frames), high, 0.0)
    ends = jnp.where(mine & (row >= frames) & (row < 2 * frames), second - high, ends)
    out = mul(jnp.concatenate([kv, ends.astype(bf16)], 0), low[...])
    main = out[: 2 * GROUP]
    ends = out[2 * GROUP :]
    behind = None
    for part in two_parts(sums[...]):
        for i, w in enumerate((wk, wv)):
            term = mul(part[i * GROUP : (i + 1) * GROUP], w[...], ((0,), (1,)))
            behind = term if behind is None else behind + term
    bias_grad = behind[0:1]
    turned = jnp.concatenate([wk[...].astype(f32).T, wv[...].astype(f32).T], 0)
    over = 1.0 / gain[...]
    gain_grad = (jnp.sum(main * turned, 0, keepdims=True) - bias[...] * bias_grad) * over
    lines = []
    for f in range(frames):
        here = frame[0:1] == f
        first_sum = jnp.sum(jnp.where(here, first, 0.0), -1, keepdims=True)
        second_sum = jnp.sum(jnp.where(here, second, 0.0), -1, keepdims=True)
        along = ends[f : f + 1] + ends[frames + f : frames + f + 1]
        scaled = behind[1 + f : 2 + f] + behind[1 + frames + f : 2 + frames + f]
        lines.append(gain[...] * scaled - first_sum - (along - bias[...] * second_sum) * over)
    for i, line in enumerate(lines + [gain_grad, bias_grad]):
        small[i : i + 1, :] = line + before[0][i : i + 1, :] if turn else line

    kv_lat = jnp.concatenate([kl_g[...], vl_g[...]], 1)
    total[GROUP:, :] = main + mul(kv_lat, lat_own[...], TN)
    base = scalars[1] * n_keys
    query = None
    for s in range(n_keys):
        slot = pl.ds(pl.multiple_of((base + (scalars[0] ^ s)) * rows, 8), rows)
        term = mul(q_grads[s][...], rows_all[slot, :], TN)
        query = term if query is None else query + term
    total[:GROUP, :] = query
    near = scalars[1] if aligned else 0
    lanes = total.shape[1] // PAIR
    for j in range(per):
        out = (given, kept)[j % 2]
        slot = per * (1 - turn) + 2 * (j // 2) + 1 - j % 2
        start = ((scalars[0] ^ slot) % per) * width
        for part in range(3):
            piece = total[pl.ds(pl.multiple_of(part * GROUP + start, width), width), :].astype(bf16)
            for n in range(PAIR):
                out[j // 2, near ^ n, part * width : (part + 1) * width, :] = piece[
                    :, n * lanes : (n + 1) * lanes
                ]
        piece = wo_g[slot]
        for n in range(PAIR):
            out[j // 2, near ^ n, 3 * width :, :] = piece[:, n * lanes : (n + 1) * lanes]


def patch_back_kernel(
    frames, scalars, kv_a, kv_b, stat_a, stat_b, norm_stat, patches, time, gain, wk_a, wv_a, wk_b, wv_b, _, grad_o
):
    turned = ((0,), (1,))
    inverse = 1.0 / gain.shape[1]
    for f in range(frames):
        rows = pl.ds(f * PATCH, PATCH)
        span = slice(f * PATCH, (f + 1) * PATCH)
        scale = norm_stat[1:2, span]
        first = (stat_a[0:1, span] + stat_b[0:1, span]) * inverse
        second = (stat_a[1:2, span] + stat_b[1:2, span]) * inverse
        slope = scale * scale * second
        level = scale * first - norm_stat[0:1, span] * slope
        line = lax.broadcasted_iota(jnp.int32, (8, PATCH), 0)
        columns = jnp.where(line == 0, scale, jnp.where(line == 1, level, slope)).T
        grad = mul(kv_a[0, :, span], wk_a[...], turned)
        grad = grad + mul(kv_a[1, :, span], wv_a[...], turned)
        grad = grad + mul(kv_b[0, :, span], wk_b[...], turned)
        grad = grad + mul(kv_b[1, :, span], wv_b[...], turned)
        framed = patches[0, rows, :].astype(f32) + time[0, f : f + 1, :]
        back = grad * gain[...] * columns[:, 0:1] - columns[:, 1:2] - framed * columns[:, 2:3]
        grad_o[0, rows, :] = back.astype(bf16)


def latent_back_kernel(n_keys, frames, n_frames, scalars, latents, gain, mid_grad, media_small, ff_small, *refs):
    keys = refs[:8]
    wq = refs[8]
    slots = refs[9 : 9 + n_keys]
    lat_o, small_o = refs[9 + n_keys :]
    query = functools.reduce(jnp.add, [r[...].astype(f32) for r in slots]).astype(bf16)
    grad = mul(query, wq[...], NT)
    for i in range(4):
        grad = grad + mul(keys[2 * i][...], keys[2 * i + 1][...], NT)
    back, gain_grad, bias_grad = norm_back(latents[...], gain[...], grad)
    lat_o[...] = mid_grad[...] + back
    small_o[...] = jnp.zeros_like(small_o)
    for f in range(frames):
        small_o[pl.ds(scalars[0] * frames + f, 1), :] = media_small[f : f + 1, :]
    for i, line in enumerate(
        (media_small[frames : frames + 1, :], media_small[frames + 1 : frames + 2, :], gain_grad, bias_grad)
    ):
        small_o[n_frames + i : n_frames + i + 1, :] = line
    small_o[n_frames + 4 : n_frames + 6, :] = ff_small[...]


def finish_kernel(width, scalars, *refs):
    parts = refs[:-4]
    q_o, k_o, v_o, out_o = refs[-4:]
    total = functools.reduce(jnp.add, [r[...].astype(f32) for r in parts])
    for i, ref in enumerate((q_o, k_o, v_o)):
        ref[...] = total[i * width : (i + 1) * width].T
    r = out_o.shape[0]
    for h in range(out_o.shape[1] // LANES):
        out_o[:, h * LANES : (h + 1) * LANES] = total[3 * width + h * r : 3 * width + (h + 1) * r]


def finish_up_kernel(scalars, keep, got, out):
    units = keep.shape[0]
    near = scalars[1]
    own = pl.ds(pl.multiple_of(near * units, LANES), units)
    other = pl.ds(pl.multiple_of((1 - near) * units, LANES), units)
    out[:, own] = keep[...].astype(f32).T
    out[:, other] = got[...].astype(f32).T


def whole(shape):
    return pl.BlockSpec(shape, lambda *_: (0,) * len(shape))


def struct(shape, dtype):
    return jax.ShapeDtypeStruct(shape, dtype)


def shards(
    n_far,
    n_keys,
    latents,
    patches,
    frame_counts,
    time_embedding,
    media_gain,
    media_bias,
    latent_gain,
    latent_bias,
    ff_gain,
    ff_bias,
    query_weight,
    key_weight,
    value_weight,
    out_weight,
    up_weight,
    down_weight,
    cotangent,
):
    media, own, dim = latents.shape
    key_rows = patches.shape[1]
    inner = query_weight.shape[1]
    hidden = up_weight.shape[1]
    frames = key_rows // PATCH
    n_frames = time_embedding.shape[0]
    n_media = n_far * PAIR
    rows = media * own
    all_rows = media * key_rows
    width = inner // n_keys
    each = dim // n_media
    aligned = each == LANES and width % LANES == 0 and n_far == n_keys
    far = lax.axis_index("far")
    near = lax.axis_index("near")
    key = lax.axis_index("keys")
    own_group = key // (n_keys // 2)
    scalars = jnp.stack([key, near, far, far, key * PAIR + near, own_group, jnp.full_like(far, dim)])
    scalars = scalars.astype(jnp.int32)

    def over_keys(value, shift):
        return lax.ppermute(value, "keys", [(i, i ^ shift) for i in range(n_keys)])

    def over_near(value):
        return lax.ppermute(value, "near", [(0, 1), (1, 0)])

    def over_far(value, shift):
        return lax.ppermute(value, "far", [(i, i ^ shift) for i in range(n_far)])

    def exchange_keys(slots):
        return [slots[0]] + [over_keys(slots[s], s) for s in range(1, n_keys)]

    def gather_keys(value):
        slots = [None] * n_keys
        for s in range(0, n_keys, 2):
            slots[s] = value if s == 0 else over_keys(value, s)
        for s in range(0, n_keys, 2):
            slots[s + 1] = over_keys(slots[s], 1)
        return slots

    def add(left, right):
        return (left.astype(f32) + right.astype(f32)).astype(bf16)

    lat = latents.reshape(rows, dim)
    cot = cotangent.reshape(rows, dim)
    row = lambda v: v.reshape(1, dim)
    time_blocks = time_embedding.reshape(n_keys, frames, dim)
    packed = inner + LANES
    own_block = lambda w: pl.BlockSpec((own, w), lambda i, *_: (i, 0))
    patch_block = pl.BlockSpec((1, key_rows, dim), lambda i, *_: (i, 0, 0))
    inner_block = pl.BlockSpec((1, key_rows, inner), lambda i, *_: (i, 0, 0))
    time_block = pl.BlockSpec((1, frames, dim), lambda i, s, *_: (s[0], 0, 0))
    stat_block = pl.BlockSpec((8, key_rows), lambda i, *_: (0, i))
    patch_flops = 4 * all_rows * dim * inner
    att_flops = 4 * media * n_keys * own * (key_rows + own) * inner * (GROUP // HEAD)

    def call(kernel, name, grid, in_specs, out_specs, out_shape, price, prefetch=1, **more):
        run = pl.pallas_call(
            kernel,
            name=name,
            grid_spec=pltpu.PrefetchScalarGridSpec(
                num_scalar_prefetch=prefetch,
                grid=grid,
                in_specs=in_specs,
                out_specs=out_specs,
                scratch_shapes=more.pop("scratch_shapes", ()),
            ),
            out_shape=out_shape,
            compiler_params=params(),
            cost_estimate=price,
            **more,
        )

        def pinned(*args):
            args = list(args)
            for i in range(prefetch, len(args)):
                if in_specs[i - prefetch].memory_space is None:
                    args[i] = pltpu.with_memory_space_constraint(args[i], pltpu.HBM)
            return run(*args)

        return pinned

    own_rows, q_own = call(
        latent_kernel,
        "latent_project",
        (1,),
        [whole((rows, dim)), whole((1, dim)), whole((1, dim)), whole((rows, dim)), whole((dim, inner))],
        [whole((rows, 2 * dim)), whole((rows, inner))],
        (struct((rows, 2 * dim), bf16), struct((rows, inner), bf16)),
        cost(2 * rows * dim * inner, 2 * dim * inner + 14 * rows * dim),
    )(scalars, lat, row(latent_gain), row(latent_bias), cot, query_weight)
    q_all = exchange_keys([q_own] * n_keys)
    rows_all = lax.all_gather(own_rows, ("near", "keys"), axis=0, tiled=True)

    media_low, kp, vp, kl, vl, norm_stat, once, norm_vec = call(
        functools.partial(patch_kernel, frames),
        "patch_project",
        (media,),
        [
            patch_block,
            time_block,
            whole((1, dim)),
            whole((1, dim)),
            whole((dim, inner)),
            whole((dim, inner)),
            whole((rows, dim)),
        ],
        [
            patch_block,
            inner_block,
            inner_block,
            whole((rows, inner)),
            whole((rows, inner)),
            stat_block,
            pl.BlockSpec((1, key_rows, LANES), lambda i, *_: (i, 0, 0)),
            whole((8, 2 * inner)),
        ],
        (
            struct(patches.shape, bf16),
            struct((media, key_rows, inner), bf16),
            struct((media, key_rows, inner), bf16),
            struct((rows, inner), bf16),
            struct((rows, inner), bf16),
            struct((8, all_rows), f32),
            struct((media, key_rows, LANES), bf16),
            struct((8, 2 * inner), f32),
        ),
        cost(patch_flops, 12 * all_rows * dim),
    )(
        scalars,
        patches,
        time_blocks,
        row(media_gain),
        row(media_bias),
        key_weight,
        value_weight,
        own_rows,
    )

    shares = call(
        functools.partial(attend_kernel, n_keys, frames),
        "attend",
        (media,),
        [own_block(inner)] * n_keys
        + [inner_block, inner_block, own_block(inner), own_block(inner)],
        [own_block(packed)] * n_keys,
        [struct((rows, packed), bf16)] * n_keys,
        cost(att_flops, 4 * all_rows * inner),
        prefetch=2,
    )(scalars, frame_counts, *q_all, kp, vp, kl, vl)
    joined = exchange_keys(shares)

    attended, att_low, middle, ff_low, lse = call(
        functools.partial(join_kernel, n_keys),
        "join",
        (1,),
        [whole((rows, dim)), whole((1, dim)), whole((1, dim)), whole((inner, dim))]
        + [whole((rows, packed))] * n_keys,
        [
            whole((rows, inner)),
            whole((rows, inner)),
            whole((rows, dim)),
            whole((rows, dim)),
            whole((rows, LANES)),
        ],
        (
            struct((rows, inner), f32),
            struct((rows, inner), bf16),
            struct((rows, dim), f32),
            struct((rows, dim), bf16),
            struct((rows, LANES), f32),
        ),
        cost(2 * rows * inner * dim, 2 * inner * dim + 16 * rows * dim),
    )(scalars, lat, row(ff_gain), row(ff_bias), out_weight, *joined)
    ff_all = lax.all_gather(ff_low, ("near", "keys"), axis=0, tiled=True)

    chunk = min(512, hidden)
    wo_rows = inner * dim // n_keys // dim
    wo_shape = (n_keys, wo_rows, dim) if aligned else (inner, dim)
    resampled, mid_grad, pack, ff_small, out_slots = call(
        functools.partial(forward_kernel, n_keys, aligned),
        "feed_forward",
        (hidden // chunk,),
        [
            whole((rows, inner)),
            whole((rows, inner)),
            whole((rows, dim)),
            whole((rows, dim)),
            whole((rows, LANES)),
            whole((rows, dim)),
            pl.BlockSpec((rows, dim), lambda i, *_: (0, 1)),
            whole((1, dim)),
            whole((inner, dim)),
            pl.BlockSpec((dim, chunk), lambda i, *_: (0, i)),
            pl.BlockSpec((chunk, dim), lambda i, *_: (i, 0)),
        ],
        [
            whole((rows, dim)),
            whole((rows, dim)),
            whole((rows, packed)),
            whole((2, dim)),
            whole(wo_shape),
        ],
        (
            struct((rows, dim), f32),
            struct((rows, dim), f32),
            struct((rows, packed), bf16),
            struct((2, dim), f32),
            struct(wo_shape, bf16),
        ),
        cost(8 * rows * dim * hidden, 4 * dim * hidden + 24 * rows * dim),
        scratch_shapes=[
            pltpu.VMEM((rows, dim), f32),
            pltpu.VMEM((rows, dim), f32),
            pltpu.VMEM((inner, dim) if aligned else (8, LANES), f32),
        ],
    )(
        scalars,
        attended,
        att_low,
        middle,
        ff_low,
        lse,
        cot,
        own_rows,
        row(ff_gain),
        out_weight,
        up_weight,
        down_weight,
    )
    if not aligned:
        c = dim // n_keys
        out_slots = out_slots.reshape(n_media, inner // n_media, n_keys, c // each, each)
        out_slots = out_slots.transpose(2, 3, 1, 0, 4).reshape(n_keys, wo_rows, dim)
        out_slots = jnp.stack(
            [lax.dynamic_index_in_dim(out_slots, key ^ s, 0, False) for s in range(n_keys)]
        )
    packs = gather_keys(pack)

    half_keys = n_keys // 2
    pick = lambda turn: (lambda s: s[5] ^ (1 - turn))
    high = 3 * width + wo_rows

    def attend_back(turn, packs, before):
        g = pick(turn)
        own_cols = pl.BlockSpec((own, GROUP), lambda i, s, *_: (i, g(s)))
        stat_cols = pl.BlockSpec((own, LANES), lambda i, *_: (i, inner // LANES))
        key_cols = pl.BlockSpec((1, key_rows, GROUP), lambda i, s, *_: (i, 0, g(s)))
        q_width = GROUP if turn == 0 else inner
        out = call(
            functools.partial(attend_back_kernel, n_keys, frames, turn, inner // HEAD),
            "attend_back",
            (media,),
            [own_cols] * (2 * n_keys)
            + [stat_cols] * n_keys
            + [key_cols, key_cols, own_cols, own_cols]
            + [
                pl.BlockSpec((8, GROUP), lambda i, s, *_: (0, g(s))),
                pl.BlockSpec((8, GROUP), lambda i, s, *_: (0, inner // GROUP + g(s))),
            ]
            + [own_block(GROUP)] * len(before),
            [
                pl.BlockSpec((2, GROUP, key_rows), lambda i, *_: (0, 0, i)),
                stat_block,
                own_block(GROUP),
                own_block(GROUP),
            ]
            + [own_block(q_width)] * n_keys,
            [
                struct((2, GROUP, all_rows), bf16),
                struct((8, all_rows), f32),
                struct((rows, GROUP), bf16),
                struct((rows, GROUP), bf16),
            ]
            + [struct((rows, q_width), bf16)] * n_keys,
            cost(5 * att_flops // 4, 4 * all_rows * inner),
            prefetch=2,
        )(
            scalars,
            frame_counts,
            *q_all,
            *packs,
            *packs,
            kp,
            vp,
            kl,
            vl,
            norm_vec,
            norm_vec,
            *before,
        )
        return out[:4], out[4:]

    def regroup(value):
        value = jnp.moveaxis(value, 1, 2).reshape(-1, high, n_far, PAIR, each)
        value = value.transpose(0, 3, 1, 2, 4).reshape(-1, PAIR, high, n_far * each)
        return jnp.where(near == 0, value, value[:, ::-1])

    def weights(turn, kv_t, stat, kl_g, vl_g, q_grads, before):
        g = pick(turn)
        lanes = dim // n_far
        cols = pl.BlockSpec((rows, GROUP), lambda i, s: (0, g(s) if turn else 0))
        place = (lambda i, s: (0, 0, 0, i ^ s[2])) if aligned else (lambda i, s: (0, 0, 0, i))
        if aligned:
            grid, run = (n_far,), lanes
            out = [pl.BlockSpec((n_keys // 4, PAIR, high, run // PAIR), place)] * 2
        else:
            grid, run = (1,), dim
            out = [whole((n_keys // 4, PAIR, high, dim // PAIR))] * 2
        small_run = pl.BlockSpec((8, run), lambda i, s: (0, i))
        wo_run = pl.BlockSpec((n_keys, wo_rows, run), (lambda i, s: (0, 0, i ^ s[2])) if aligned else (lambda i, s: (0, 0, 0)))
        grads = call(
            functools.partial(weight_kernel, n_keys, turn, width, frames, aligned),
            "projection_weights",
            grid,
            [
                whole((2, GROUP, all_rows)),
                pl.BlockSpec((all_rows, run), lambda i, s: (0, i)),
                whole((rows, GROUP)),
                whole((rows, GROUP)),
                pl.BlockSpec((rows, run), lambda i, s: (0, i)),
                pl.BlockSpec((group_rows, run), lambda i, s: (0, i)),
                wo_run,
                whole((all_rows, LANES)),
                whole((8, all_rows)),
                whole((8, all_rows)),
                pl.BlockSpec((run, GROUP), lambda i, s: (i, g(s))),
                pl.BlockSpec((run, GROUP), lambda i, s: (i, g(s))),
                pl.BlockSpec((1, run), lambda i, s: (0, i)),
                pl.BlockSpec((1, run), lambda i, s: (0, i)),
            ]
            + [cols] * n_keys
            + [small_run] * len(before),
            out + [small_run],
            [struct((n_keys // 4, PAIR, high, dim // PAIR), bf16)] * 2 + [struct((8, dim), f32)],
            cost(patch_flops // 2, 4 * all_rows * dim),
            scratch_shapes=[pltpu.VMEM((3 * GROUP, run), f32), pltpu.VMEM((2 * GROUP, LANES), f32)],
        )(
            scalars,
            kv_t,
            media_low.reshape(all_rows, dim),
            kl_g,
            vl_g,
            own_rows,
            rows_all,
            out_slots,
            once.reshape(all_rows, LANES),
            norm_stat,
            stat,
            key_weight,
            value_weight,
            row(media_gain),
            row(media_bias),
            *q_grads,
            *before,
        )
        return grads if aligned else [regroup(v) for v in grads[:2]] + [grads[2]]

    group_rows = PAIR * n_keys * rows
    (kv_a, stat_a, kl_a, vl_a), q_a = attend_back(0, packs, [])
    given_a, kept_a, media_small = weights(0, kv_a, stat_a, kl_a, vl_a, q_a, [])
    far_core = over_keys(given_a, 1)
    ff_all, kept_a = tie(ff_all, kept_a)

    units = hidden // (n_keys * PAIR)
    ff_partial = call(
        functools.partial(ff_grad_kernel, aligned),
        "feed_forward_weights",
        (1,),
        [
            whole((group_rows, dim)),
            pl.BlockSpec((group_rows, dim), lambda i, s: (0, 1)),
            pl.BlockSpec((dim, units), lambda i, s: (0, s[4])),
            pl.BlockSpec((units, dim), lambda i, s: (s[4], 0)),
        ],
        whole((2 * units, dim)),
        struct((2 * units, dim), bf16),
        cost(8 * group_rows * dim * units, 8 * dim * units + 4 * group_rows * dim),
    )(scalars, ff_all, rows_all, up_weight, down_weight)
    blocks = n_far // n_keys
    if not aligned:
        pieces = ff_partial[units:].reshape(blocks, units // blocks, n_keys, dim // n_keys)
        pieces = pieces.transpose(0, 2, 1, 3).reshape(n_far, units, dim // n_far)
        pieces = pieces.transpose(1, 0, 2).reshape(units, dim)
        ups = ff_partial[:units].reshape(units, n_far, PAIR, each)
        ups = jnp.where(near == 0, ups, ups[:, :, ::-1]).reshape(units, dim)
        ff_partial = jnp.concatenate([ups, pieces], 0)
    far_core, ff_partial = tie(far_core, ff_partial)
    ff_sum = lax.psum_scatter(ff_partial, "far", scatter_dimension=1, tiled=True)
    far_sum = add(kept_a, far_core)
    far_sum, packs[0] = tie(far_sum, packs[0])
    far_near = over_near(far_sum[:, 1])
    (kv_b, stat_b, kl_b, vl_b), q_b = attend_back(1, packs, q_a)
    q_slots = exchange_keys(q_b)
    far_near, kv_b = tie(far_near, kv_b)
    far_half = add(far_sum[:, 0], far_near)
    far_half, kv_b = tie(far_half, kv_b)
    far_got = [over_keys(far_half[j], half_keys + 2 * j) for j in range(n_keys // 4)]
    given_b, kept_b, media_small = weights(1, kv_b, stat_b, kl_b, vl_b, q_b, [media_small])
    near_core = over_keys(given_b, 1)
    kept_b, lat = tie(kept_b, lat)

    col = lambda turn: pl.BlockSpec((dim, GROUP), lambda i, s: (0, s[5] ^ (1 - turn)))
    both = lambda value: [value, value]
    small_rows = -(-(n_frames + 6) // 8) * 8
    latents_grad, small = call(
        functools.partial(latent_back_kernel, n_keys, frames, n_frames),
        "latent_back",
        (1,),
        [whole((rows, dim)), whole((1, dim)), whole((rows, dim)), whole((8, dim)), whole((2, dim))]
        + [whole((rows, GROUP)), col(0), whole((rows, GROUP)), col(0)]
        + [whole((rows, GROUP)), col(1), whole((rows, GROUP)), col(1)]
        + [whole((dim, inner))]
        + [whole((rows, inner))] * n_keys,
        [whole((rows, dim)), whole((small_rows, dim))],
        (struct((rows, dim), f32), struct((small_rows, dim), f32)),
        cost(6 * rows * dim * inner, 6 * dim * inner + 20 * rows * dim),
    )(
        scalars,
        lat,
        row(latent_gain),
        mid_grad,
        media_small,
        ff_small,
        kl_a,
        key_weight,
        vl_a,
        value_weight,
        kl_b,
        key_weight,
        vl_b,
        value_weight,
        query_weight,
        *q_slots,
    )

    pieces = 3
    each_piece = media // pieces

    def patch_back(piece, gain, patches_grad):
        at = piece * each_piece
        block = pl.BlockSpec((1, key_rows, dim), lambda i, *_: (i + at, 0, 0))
        keys = pl.BlockSpec((2, GROUP, key_rows), lambda i, *_: (0, 0, i + at))
        stat = pl.BlockSpec((8, key_rows), lambda i, *_: (0, i + at))
        return call(
            functools.partial(patch_back_kernel, frames),
            "patch_back",
            (each_piece,),
            [
                keys,
                keys,
                stat,
                stat,
                stat,
                block,
                time_block,
                whole((1, dim)),
                col(0),
                col(0),
                col(1),
                col(1),
                pl.BlockSpec(memory_space=pl.ANY),
            ],
            block,
            struct(patches.shape, bf16),
            cost(patch_flops // pieces, 8 * all_rows * dim // pieces),
            **({} if piece == 0 else {"input_output_aliases": {13: 0}}),
        )(
            scalars,
            kv_a,
            kv_b,
            stat_a,
            stat_b,
            norm_stat,
            patches,
            time_blocks,
            gain,
            key_weight,
            value_weight,
            key_weight,
            value_weight,
            gain if piece == 0 else patches_grad,
        )

    def butterfly(value, step):
        axis, shift = step
        size = {"keys": n_keys, "near": PAIR, "far": n_far}[axis]
        return lax.ppermute(value, axis, [(i, i ^ shift) for i in range(size)])

    steps = [
        (axis, 1 << i)
        for axis, size in (("keys", n_keys), ("near", PAIR), ("far", n_far))
        for i in range(size.bit_length() - 1)
    ]
    gain = row(media_gain)
    small = small + butterfly(small, steps[0])
    near_core, latents_grad = tie(near_core, latents_grad)
    near_sum = add(kept_b, near_core)
    total = near_sum[0]
    for j in range(1, n_keys // 4):
        total = add(total, over_keys(near_sum[j], 2 * j))
    total, small, gain = tie(total, small, gain)
    near_got = over_near(total[1])
    small_got = butterfly(small, steps[1])
    patches_grad = patch_back(0, gain, None)
    patches_grad, small_got, *far_got = tie(patches_grad, small_got, *far_got)
    total = total[0]
    for value in far_got:
        total = add(total, value)
    small = small + small_got
    total, small, gain, ff_sum = tie(total, small, gain, ff_sum)
    small_got = butterfly(small, steps[2])
    up_keep = ff_sum[:units, :each]
    up_got = over_near(ff_sum[:units, each:])
    patches_grad = patch_back(1, gain, patches_grad)
    patches_grad, small_got, near_got, up_got = tie(patches_grad, small_got, near_got, up_got)
    total = add(total, near_got)
    small = small + small_got
    if not aligned:
        total = total.reshape(-1, n_far, each)
        total = jnp.concatenate(
            [lax.dynamic_index_in_dim(total, far ^ s, 1, False) for s in range(n_far)], 1
        )
    total, small, gain = tie(total, small, gain)
    parts = [over_far(total[:, s * each : (s + 1) * each], s) for s in range(1, n_far)]
    small_got = butterfly(small, steps[3])
    route = []
    for m in range(n_media):
        for k in range(n_keys):
            block, owner = divmod(m // PAIR, n_keys)
            target = (k * PAIR + m % PAIR) * blocks + block
            route.append((m * n_keys + k, target * n_keys + owner))
    down_grad = lax.ppermute(ff_sum[units:], ("far", "near", "keys"), route)
    patches_grad = patch_back(2, gain, patches_grad)
    patches_grad, small_got, down_grad, *parts = tie(patches_grad, small_got, down_grad, *parts)
    parts = [total[:, :each]] + parts
    small = small + small_got
    for step in steps[4:]:
        small = small + butterfly(small, step)
    if aligned:
        up_grad = call(
            finish_up_kernel,
            "finish_up",
            (1,),
            [whole((units, each))] * 2,
            whole((each, PAIR * units)),
            struct((each, PAIR * units), f32),
            cost(0, 8 * units * each),
        )(scalars, up_keep, up_got)
    else:
        up_grad = jnp.where(
            near == 0,
            jnp.concatenate([up_keep, up_got], 0),
            jnp.concatenate([up_got, up_keep], 0),
        ).T.astype(f32)
    down_grad = down_grad.reshape(units // blocks, dim // n_keys).astype(f32)

    if aligned:
        q_grad, k_grad, v_grad, out_grad = call(
            functools.partial(finish_kernel, width),
            "finish_projections",
            (1,),
            [whole(p.shape) for p in parts],
            [whole((each, width))] * 3 + [whole((inner // n_media, dim // n_keys))],
            [struct((each, width), f32)] * 3
            + [struct((inner // n_media, dim // n_keys), f32)],
            cost(0, 16 * width * each),
        )(scalars, *parts)
    else:
        total = functools.reduce(jnp.add, [p.astype(f32) for p in parts])
        q_grad, k_grad, v_grad = (total[i * width : (i + 1) * width].T for i in range(3))
        out_grad = total[3 * width :].reshape(-1, inner // n_media, each)
        out_grad = out_grad.transpose(1, 0, 2).reshape(inner // n_media, dim // n_keys)

    return (
        resampled.reshape(latents.shape),
        patches_grad,
        latents_grad.reshape(latents.shape),
        small[:n_frames],
        small[n_frames],
        small[n_frames + 1],
        small[n_frames + 2],
        small[n_frames + 3],
        small[n_frames + 4],
        small[n_frames + 5],
        q_grad,
        k_grad,
        v_grad,
        out_grad,
        up_grad,
        down_grad,
    )


def solution(mesh):
    n_media, n_keys = mesh.shape["media"], mesh.shape["keys"]
    n_far = n_media // PAIR
    fine = Mesh(mesh.devices.reshape(n_far, PAIR, n_keys), ("far", "near", "keys"))
    split = P(("far", "near"), "keys", None)
    return jax.shard_map(
        functools.partial(shards, n_far, n_keys),
        mesh=fine,
        in_specs=(split, split, P(("far", "near"))) + (P(),) * 13 + (split,),
        out_specs=(split,) * 3 + (P(),) * 7 + (P(("far", "near"), "keys"),) * 6,
        check_vma=False,
    )
```

```python
import functools

import jax
import jax.numpy as jnp
from jax import lax
from jax.experimental import pallas as pl
from jax.experimental.pallas import tpu as pltpu
from jax.sharding import Mesh, PartitionSpec as P

HEAD = 64
PATCH = 256
GROUP = 256
LANES = 128

VMEM_LIMIT = 60 << 20

EPS = 1e-05
NEG = -1e30
PAIR = 2

f32 = jnp.float32
bf16 = jnp.bfloat16


def mul(left, right, contract=((1,), (0,)), precision=None):
    return lax.dot_general(
        left, right, (contract, ((), ())), precision=precision, preferred_element_type=f32
    )


NN = ((1,), (0,))
NT = ((1,), (1,))
TN = ((0,), (0,))


def norm_parts(values):
    centre = jnp.mean(values, -1, keepdims=True)
    shifted = values - centre
    spread = jnp.mean(shifted * shifted, -1, keepdims=True)
    return centre, lax.rsqrt(spread + EPS), shifted


def norm(values, gain, bias):
    _, scale, shifted = norm_parts(values)
    return shifted * scale * gain + bias


def norm_back(values, gain, grad):
    _, scale, shifted = norm_parts(values)
    unit = shifted * scale
    scaled = grad * gain
    first = jnp.mean(scaled, -1, keepdims=True)
    second = jnp.mean(scaled * unit, -1, keepdims=True)
    back = scale * (scaled - first - unit * second)
    return (
        back,
        jnp.sum(grad * unit, 0, keepdims=True),
        jnp.sum(grad, 0, keepdims=True),
    )


def gelu_parts(hidden):
    cdf = 0.5 * (1.0 + lax.erf(hidden * (2.0**-0.5)))
    pdf = jnp.exp(-0.5 * hidden * hidden) * 0.3989422804014327
    return cdf, cdf + hidden * pdf


def head_mask(rows, width, heads):
    row = lax.broadcasted_iota(jnp.int32, (heads * rows, width), 0) // rows
    col = lax.broadcasted_iota(jnp.int32, (heads * rows, width), 1)
    return row, col


def spread_heads(values):
    heads = values.shape[1] // HEAD
    row, col = head_mask(values.shape[0], values.shape[1], heads)
    return jnp.where(row == col // HEAD, jnp.concatenate([values] * heads, 0), jnp.zeros((), values.dtype))


def fold_heads(values):
    heads = values.shape[1] // HEAD
    rows = values.shape[0] // heads
    row, col = head_mask(rows, values.shape[1], heads)
    kept = jnp.where(row == col // HEAD, values, 0.0)
    total = kept[:rows]
    for h in range(1, heads):
        total = total + kept[h * rows : (h + 1) * rows]
    return total


def three_parts(values, lane, start, slots):
    high = values.astype(bf16).astype(f32)
    rest = values - high
    middle = rest.astype(bf16).astype(f32)
    low = rest - middle
    place = lane // slots - start
    return jnp.where(place == 0, high, jnp.where(place == 1, middle, jnp.where(place == 2, low, 0.0)))


def cost(flops, moved, special=0):
    return pl.CostEstimate(flops=int(flops), bytes_accessed=int(moved), transcendentals=int(special))


def params():
    return pltpu.CompilerParams(vmem_limit_bytes=VMEM_LIMIT)


def tie(*values):
    return lax.optimization_barrier(values)


def latent_kernel(_, lat, gain, bias, cot, wq, rows_o, q_o):
    dim = lat.shape[1]
    low = norm(lat[...], gain[...], bias[...]).astype(bf16)
    rows_o[:, :dim] = low
    rows_o[:, dim:] = cot[...].astype(bf16)
    q_o[...] = mul(low, wq[...]).astype(bf16)


def two_parts(values):
    high = values.astype(bf16)
    return high, (values - high.astype(f32)).astype(bf16)


def masked_scores(query, keys, frames, first, count):
    scores = mul(query, keys, NT)
    parts = []
    for f in range(frames):
        part = scores[:, f * PATCH : (f + 1) * PATCH]
        parts.append(jnp.where(first + f < count, part, NEG))
    return jnp.concatenate(parts + [scores[:, frames * PATCH :]], 1)


def patch_kernel(n_keys, frames, scalars, counts, patches, time, gain, bias, wk, wv, lat_low, *refs):
    q = refs[:n_keys]
    low_o, k_o, v_o, kl_o, vl_o, stat_o, once_o, vec_o = refs[n_keys : n_keys + 8]
    outs = refs[n_keys + 8 :]
    step = pl.program_id(0)

    @pl.when(step == 0)
    def _():
        kl_o[...] = mul(lat_low[...], wk[...]).astype(bf16)
        vl_o[...] = mul(lat_low[...], wv[...]).astype(bf16)
        row = lax.broadcasted_iota(jnp.int32, (16, gain.shape[1]), 0)
        both = jnp.where(row % 2 == 0, gain[...], bias[...])
        high, low = two_parts(both)
        both = jnp.where(row < 2, high.astype(f32), jnp.where(row < 4, low.astype(f32), 0.0)).astype(bf16)
        for i, w in enumerate((wk, wv)):
            term = mul(both, w[...])
            vec_o[:, i * w.shape[1] : (i + 1) * w.shape[1]] = term[:8] + pltpu.roll(term, 14, 0)[:8]

    for f in range(frames):
        rows = pl.ds(f * PATCH, PATCH)
        framed = patches[0, rows, :].astype(f32) + time[pl.ds(scalars[0] * frames + f, 1), :]
        centre, scale, shifted = norm_parts(framed)
        low = (shifted * scale * gain[...] + bias[...]).astype(bf16)
        low_o[0, rows, :] = low
        k_o[0, rows, :] = mul(low, wk[...]).astype(bf16)
        v_o[0, rows, :] = mul(low, wv[...]).astype(bf16)
        lane = lax.broadcasted_iota(jnp.int32, (PATCH, LANES), 1)
        stat = jnp.where(lane == 0, centre, jnp.where(lane == 1, scale, 0.0))
        stat_o[:, f * PATCH : (f + 1) * PATCH] = stat.T[:8]
        high = scale.astype(bf16).astype(f32)
        once = jnp.where(lane == 0, 1.0, jnp.where(lane == 1 + f, high, 0.0))
        once_o[0, rows, :] = jnp.where(lane == 1 + frames + f, scale - high, once).astype(bf16)

    own = q[0].shape[0] // pl.num_programs(0)
    inner = q[0].shape[1]
    heads = inner // HEAD
    count = counts[step]
    first = scalars[0] * frames
    here = pl.ds(pl.multiple_of(step * own, own), own)
    query = jnp.concatenate([r[here, :] for r in q], 0)
    rows = query.shape[0]
    stats = jnp.zeros((rows, LANES), f32)
    shares = []
    for g in range(inner // GROUP):
        cols = slice(g * GROUP, (g + 1) * GROUP)
        wide = spread_heads(query[:, cols] * bf16(HEAD**-0.5))
        keys = jnp.concatenate([k_o[0, :, cols], kl_o[here, cols]], 0)
        values = jnp.concatenate([v_o[0, :, cols], vl_o[here, cols]], 0)
        scores = masked_scores(wide, keys, frames, first, count)
        top = jnp.max(scores, -1, keepdims=True)
        raw = jnp.exp(scores - top)
        total = jnp.sum(raw, -1, keepdims=True)
        share = mul(raw.astype(bf16), values) * (1.0 / total)
        shares.append(fold_heads(share).astype(bf16))
        level = top + jnp.log(total)
        row, lane = head_mask(rows, LANES, GROUP // HEAD)
        kept = jnp.where(lane % heads == row + g * (GROUP // HEAD), level, 0.0)
        for h in range(GROUP // HEAD):
            stats = stats + kept[h * rows : (h + 1) * rows]
    lane = lax.broadcasted_iota(jnp.int32, stats.shape, 1)
    packed = jnp.concatenate(shares + [three_parts(stats, lane, 0, heads).astype(bf16)], 1)
    for s in range(n_keys):
        outs[s][here, :] = packed[s * own : (s + 1) * own]


def sum_runs(stats, heads, start):
    total = None
    for part in range(3):
        shift = (-(start + part) * heads) % LANES
        term = pltpu.roll(stats, shift, 1) if shift else stats
        total = term if total is None else total + term
    return total


def join_kernel(n_keys, _, latents, gain, bias, wo, *refs):
    slots = refs[:n_keys]
    att_o, low_o, mid_o, ff_o, lse_o = refs[n_keys:]
    inner = att_o.shape[1]
    heads = inner // HEAD
    levels = [sum_runs(r[:, inner:].astype(f32), heads, 0) for r in slots]
    top = functools.reduce(jnp.maximum, levels)
    weights = [jnp.exp(v - top) for v in levels]
    total = functools.reduce(jnp.add, weights)
    inverse = 1.0 / total
    lane = lax.broadcasted_iota(jnp.int32, (LANES, inner), 0)
    col = lax.broadcasted_iota(jnp.int32, (LANES, inner), 1)
    select = jnp.where(lane == col // HEAD, 1.0, 0.0)
    attended = None
    for s in range(n_keys):
        wide = mul(weights[s] * inverse, select, NN, lax.Precision.HIGHEST)
        term = wide * slots[s][:, :inner].astype(f32)
        attended = term if attended is None else attended + term
    low = attended.astype(bf16)
    middle = latents[...] + mul(low, wo[...])
    att_o[...] = attended
    low_o[...] = low
    mid_o[...] = middle
    ff_o[...] = norm(middle, gain[...], bias[...]).astype(bf16)
    lse_o[...] = top + jnp.log(total)


def forward_kernel(
    n_keys,
    aligned,
    scalars,
    attended,
    att_low,
    middle,
    ff_low,
    lse,
    cot,
    out_low,
    gain,
    wo,
    up,
    down,
    res_o,
    mid_grad_o,
    pack_o,
    small_o,
    wo_grad_o,
    res_acc,
    in_acc,
    wo_acc,
):
    step = pl.program_id(0)

    @pl.when(step == 0)
    def _():
        res_acc[...] = jnp.zeros_like(res_acc)
        in_acc[...] = jnp.zeros_like(in_acc)

    hidden = mul(ff_low[...], up[...])
    act_grad = mul(out_low[...], down[...], NT)
    cdf, slope = gelu_parts(hidden)
    res_acc[...] += mul((hidden * cdf).astype(bf16), down[...])
    in_acc[...] += mul((act_grad * slope).astype(bf16), up[...], NT)

    @pl.when(step == pl.num_programs(0) - 1)
    def _():
        inner = attended.shape[1]
        heads = inner // HEAD
        res_o[...] = middle[...] + res_acc[...]
        back, gain_grad, bias_grad = norm_back(middle[...], gain[...], in_acc[...])
        small_o[0:1, :] = gain_grad
        small_o[1:2, :] = bias_grad
        mid_grad = cot[...] + back
        mid_grad_o[...] = mid_grad
        branch = mid_grad.astype(bf16)
        att_grad = mul(branch, wo[...], NT).astype(bf16)
        col = lax.broadcasted_iota(jnp.int32, (inner, LANES), 0)
        lane = lax.broadcasted_iota(jnp.int32, (inner, LANES), 1)
        select = jnp.where(col // HEAD == lane % heads, 1.0, 0.0)
        delta = mul(attended[...] * att_grad.astype(f32), select, NN, lax.Precision.HIGHEST)
        lane = lax.broadcasted_iota(jnp.int32, delta.shape, 1)
        level = jnp.where(lane < heads, lse[...], 0.0)
        level = level + pltpu.roll(level, heads, 1) + pltpu.roll(level, 2 * heads, 1)
        stats = three_parts(level, lane, 0, heads) + three_parts(delta, lane, 3, heads)
        pack_o[...] = jnp.concatenate([att_grad, stats.astype(bf16)], 1)
        wo_grad = mul(att_low[...], branch, TN)
        if aligned:
            wo_acc[...] = wo_grad
            slot_rows(scalars, wo_acc, wo_grad_o, n_keys)
        else:
            wo_grad_o[...] = wo_grad.astype(bf16)


def slot_rows(scalars, full, out, n_keys):
    lanes = LANES
    n_media = out.shape[2] // lanes
    r = full.shape[0] // n_media
    c = full.shape[1] // n_keys
    for s in range(n_keys):
        owner = (scalars[0] ^ s) * c
        for m in range(n_media):
            place = slice(m * lanes, (m + 1) * lanes)
            for h in range(c // lanes):
                start = pl.multiple_of(owner + h * lanes, lanes)
                out[s, h * r : (h + 1) * r, place] = full[
                    m * r : (m + 1) * r, pl.ds(start, lanes)
                ].astype(bf16)


def ff_grad_kernel(aligned, scalars, ff_all, out_all, up, down, grad_o):
    units, dim = down.shape
    hidden = mul(ff_all[...], up[...])
    act_grad = mul(out_all[...], down[...], NT)
    cdf, slope = gelu_parts(hidden)
    grad_o[units:, :] = mul((hidden * cdf).astype(bf16), out_all[...], TN).astype(bf16)
    up_grad = mul((act_grad * slope).astype(bf16), ff_all[...], TN).astype(bf16)
    if aligned:
        for j in range(dim // LANES):
            place = ((j // PAIR) * PAIR + (scalars[1] ^ (j % PAIR))) * LANES
            grad_o[:units, pl.ds(pl.multiple_of(place, LANES), LANES)] = up_grad[
                :, j * LANES : (j + 1) * LANES
            ]
    else:
        grad_o[:units, :] = up_grad


def attend_back_kernel(n_keys, frames, turn, heads, width, aligned, scalars, counts, *refs):
    refs = list(refs)
    take = lambda n: [refs.pop(0) for _ in range(n)]
    q, grads, stat = take(n_keys), take(n_keys), take(n_keys)
    kp, vp, kl, vl, k_vec, v_vec, low, once, norm_stat, lat_own, gain, bias = take(12)
    rows_far, wo_far, wk_far, wv_far = take(4)
    q_before = take(n_keys if turn else 0)
    small_before = take(turn)
    kv_t_o, stat_o, kl_o, vl_o, given, kept, small = take(7)
    q_o = take(n_keys)
    grad_acc, sums, scalar_sums, q_acc, rows_all, wo_g, wk, wv, sems = refs
    rows = kl_o.shape[0]
    own = rows // pl.num_programs(0)
    dim = low.shape[2]
    per = GROUP // HEAD
    step = pl.program_id(0)
    count = counts[step]
    first_frame = scalars[0] * frames
    group = scalars[5] ^ (1 - turn)
    owners = GROUP // width
    group_cols = pl.ds(pl.multiple_of(group * GROUP, GROUP), GROUP)
    near_rows = pl.ds(pl.multiple_of(scalars[1] * n_keys * rows, 8), n_keys * rows)
    fetches = [
        pltpu.make_async_copy(rows_far.at[near_rows, pl.ds(0, dim)], rows_all, sems.at[0]),
        pltpu.make_async_copy(wo_far.at[pl.ds(owners * (1 - turn), owners)], wo_g, sems.at[1]),
        pltpu.make_async_copy(wk_far.at[:, group_cols], wk, sems.at[2]),
        pltpu.make_async_copy(wv_far.at[:, group_cols], wv, sems.at[3]),
    ]

    @pl.when(step == 0)
    def _():
        for fetch in fetches:
            fetch.start()
        grad_acc[...] = jnp.zeros_like(grad_acc)
        sums[...] = jnp.zeros_like(sums)
        scalar_sums[...] = jnp.zeros_like(scalar_sums)

    here = pl.ds(pl.multiple_of(step * own, own), own)
    query = jnp.concatenate([r[here, :] for r in q], 0)
    grad = jnp.concatenate([r[here, :] for r in grads], 0)
    stats = jnp.concatenate([r[here, :] for r in stat], 0).astype(f32)
    n_query = query.shape[0]
    row, lane = head_mask(n_query, LANES, per)
    tiled = jnp.concatenate([stats] * per, 0)
    mine = lane % heads == row + group * per
    level = jnp.sum(jnp.where(mine & (lane < 3 * heads), tiled, 0.0), -1, keepdims=True)
    delta = jnp.sum(
        jnp.where(mine & (lane >= 3 * heads) & (lane < 6 * heads), tiled, 0.0), -1, keepdims=True
    )
    wide = spread_heads(query * bf16(HEAD**-0.5))
    wide_grad = spread_heads(grad)
    keys = jnp.concatenate([kp[0], kl[here, :]], 0)
    values = jnp.concatenate([vp[0], vl[here, :]], 0)
    n_patch = kp.shape[1]
    scores = masked_scores(wide, keys, frames, first_frame, count)
    probs = jnp.exp(scores - level)
    prob_grad = mul(wide_grad, values, NT)
    score_grad = probs * (prob_grad - delta)
    along = jnp.sum(score_grad * scores + probs * prob_grad, 0, keepdims=True)
    score_grad = score_grad.astype(bf16)
    key_side = jnp.concatenate([wide, mul(wide, k_vec[...].astype(bf16), NT).astype(bf16)], 1)
    value_side = jnp.concatenate(
        [wide_grad, mul(wide_grad, v_vec[...].astype(bf16), NT).astype(bf16)], 1
    )
    key_t = mul(key_side, score_grad, TN)
    value_t = mul(value_side, probs.astype(bf16), TN)
    kl_o[here, :] = key_t[:GROUP, n_patch:].T.astype(bf16)
    vl_o[here, :] = value_t[:GROUP, n_patch:].T.astype(bf16)
    kv = jnp.concatenate([key_t[:GROUP, :n_patch], value_t[:GROUP, :n_patch]], 0).astype(bf16)
    kv_t_o[0] = kv[:GROUP]
    kv_t_o[1] = kv[GROUP:]
    ends = key_t[GROUP:, :n_patch] + value_t[GROUP:, :n_patch]
    line = lax.broadcasted_iota(jnp.int32, ends.shape, 0)
    stat_rows = jnp.where(line == 1, along[:, :n_patch] - ends, ends)
    span = pl.ds(pl.multiple_of(step * n_patch, n_patch), n_patch)
    stat_o[:, span] = stat_rows

    scale = norm_stat[1:2, span] * (1.0 / dim)
    first = stat_rows[0:1, :] * scale
    second = stat_rows[1:2, :] * scale
    frame = lax.broadcasted_iota(jnp.int32, (16, n_patch), 1) // PATCH
    row16 = lax.broadcasted_iota(jnp.int32, (16, n_patch), 0)
    high = second.astype(bf16).astype(f32)
    same = frame == row16 % frames
    ends = jnp.where(same & (row16 < frames), high, 0.0)
    ends = jnp.where(same & (row16 >= frames) & (row16 < 2 * frames), second - high, ends)
    grad_acc[...] += mul(jnp.concatenate([kv, ends.astype(bf16)], 0), low[0])
    sums[...] += mul(kv, once[0])
    line = lax.broadcasted_iota(jnp.int32, scalar_sums.shape, 0)
    adds = jnp.zeros(scalar_sums.shape, f32)
    for f in range(frames):
        span = slice(f * PATCH, (f + 1) * PATCH)
        adds = jnp.where(line == f, jnp.sum(first[:, span], -1, keepdims=True), adds)
        adds = jnp.where(line == frames + f, jnp.sum(second[:, span], -1, keepdims=True), adds)
    scalar_sums[...] += adds

    query_grad = mul(score_grad, keys)
    query_grad = (fold_heads(query_grad) * HEAD**-0.5).astype(bf16)
    for s in range(n_keys):
        part = query_grad[s * own : (s + 1) * own]
        place = pl.multiple_of((scalars[0] ^ s) * rows + step * own, own)
        q_acc[pl.ds(place, own), :] = part
        if turn == 0:
            q_o[s][here, :] = part
        else:
            other = pl.ds(pl.multiple_of((1 - group) * GROUP, GROUP), GROUP)
            q_o[s][here, group_cols] = part
            q_o[s][here, other] = q_before[s][here, :]

    @pl.when(step == pl.num_programs(0) - 1)
    def _():
        for fetch in fetches:
            fetch.wait()
        behind = None
        for part in two_parts(sums[...]):
            for i, w in enumerate((wk, wv)):
                term = mul(part[i * GROUP : (i + 1) * GROUP], w[...], ((0,), (1,)))
                behind = term if behind is None else behind + term
        bias_grad = behind[0:1]
        main = grad_acc[: 2 * GROUP, :]
        ends = grad_acc[2 * GROUP :, :]
        total = jnp.sum(main[:GROUP] * wk[...].astype(f32).T, 0, keepdims=True)
        total = total + jnp.sum(main[GROUP:] * wv[...].astype(f32).T, 0, keepdims=True)
        over = 1.0 / gain[...]
        lines = []
        for f in range(frames):
            along = ends[f : f + 1] + ends[frames + f : frames + f + 1]
            scaled = behind[1 + f : 2 + f] + behind[1 + frames + f : 2 + frames + f]
            second_sum = scalar_sums[frames + f : frames + f + 1, 0:1]
            lines.append(
                gain[...] * scaled
                - scalar_sums[f : f + 1, 0:1]
                - (along - bias[...] * second_sum) * over
            )
        lines += [(total - bias[...] * bias_grad) * over, bias_grad]
        for i, value in enumerate(lines):
            small[i : i + 1, :] = value + small_before[0][i : i + 1, :] if turn else value
        kv_lat = jnp.concatenate([kl_o[...], vl_o[...]], 1)
        grad_acc[: 2 * GROUP, :] = main + mul(kv_lat, lat_own[...], TN)
        q_grad = mul(q_acc[...], rows_all[...], TN)
        sums_q = q_grad.astype(bf16)
        near = scalars[1] if aligned else 0
        runs = dim // PAIR // LANES
        for j in range(owners):
            out = (given, kept)[j % 2]
            slot = 2 * (j // 2) + 1 - j % 2
            start = ((scalars[0] ^ slot) % owners) * width
            for part in range(3):
                at = pl.multiple_of((part - 1) * GROUP + start, width)
                if part == 0:
                    piece = jnp.zeros((width, dim), bf16)
                    for o in range(owners):
                        same = start == o * width
                        piece = jnp.where(same, sums_q[o * width : (o + 1) * width], piece)
                else:
                    piece = grad_acc[pl.ds(at, width), :].astype(bf16)
                place_rows(out, scalars, j // 2, part * width, piece, aligned)
            place_rows(out, scalars, j // 2, 3 * width, wo_g[slot], aligned)


def place_rows(out, scalars, slot, start, piece, aligned):
    rows = slice(start, start + piece.shape[0])
    half = piece.shape[1] // PAIR
    if aligned:
        for m in range(piece.shape[1] // LANES):
            place = pl.ds(pl.multiple_of((scalars[2] ^ (m // PAIR)) * LANES, LANES), LANES)
            out[slot, scalars[1] ^ (m % PAIR), rows, place] = piece[:, m * LANES : (m + 1) * LANES]
    else:
        for n in range(PAIR):
            out[slot, n, rows, :] = piece[:, n * half : (n + 1) * half]


def patch_back_kernel(
    frames, scalars, kv_a, kv_b, stat_a, stat_b, norm_stat, patches, time, gain, wk_a, wv_a, wk_b, wv_b, _, grad_o
):
    turned = ((0,), (1,))
    inverse = 1.0 / gain.shape[1]
    for f in range(frames):
        rows = pl.ds(f * PATCH, PATCH)
        span = slice(f * PATCH, (f + 1) * PATCH)
        scale = norm_stat[1:2, span]
        first = (stat_a[0:1, span] + stat_b[0:1, span]) * inverse
        second = (stat_a[1:2, span] + stat_b[1:2, span]) * inverse
        slope = scale * scale * second
        level = scale * first - norm_stat[0:1, span] * slope
        line = lax.broadcasted_iota(jnp.int32, (8, PATCH), 0)
        columns = jnp.where(line == 0, scale, jnp.where(line == 1, level, slope)).T
        grad = mul(kv_a[0, :, span], wk_a[...], turned)
        grad = grad + mul(kv_a[1, :, span], wv_a[...], turned)
        grad = grad + mul(kv_b[0, :, span], wk_b[...], turned)
        grad = grad + mul(kv_b[1, :, span], wv_b[...], turned)
        framed = patches[0, rows, :].astype(f32) + time[pl.ds(scalars[0] * frames + f, 1), :]
        back = grad * gain[...] * columns[:, 0:1] - columns[:, 1:2] - framed * columns[:, 2:3]
        grad_o[0, rows, :] = back.astype(bf16)


def latent_back_kernel(n_keys, frames, n_frames, scalars, latents, gain, mid_grad, media_small, ff_small, *refs):
    keys = refs[:8]
    wq = refs[8]
    slots = refs[9 : 9 + n_keys]
    lat_o, small_o = refs[9 + n_keys :]
    query = functools.reduce(jnp.add, [r[...].astype(f32) for r in slots]).astype(bf16)
    grad = mul(query, wq[...], NT)
    for i in range(4):
        grad = grad + mul(keys[2 * i][...], keys[2 * i + 1][...], NT)
    back, gain_grad, bias_grad = norm_back(latents[...], gain[...], grad)
    lat_o[...] = mid_grad[...] + back
    small_o[...] = jnp.zeros_like(small_o)
    for f in range(frames):
        small_o[pl.ds(scalars[0] * frames + f, 1), :] = media_small[f : f + 1, :]
    for i, line in enumerate(
        (media_small[frames : frames + 1, :], media_small[frames + 1 : frames + 2, :], gain_grad, bias_grad)
    ):
        small_o[n_frames + i : n_frames + i + 1, :] = line
    small_o[n_frames + 4 : n_frames + 6, :] = ff_small[...]


def finish_kernel(width, scalars, up_keep, up_got, down, *refs):
    parts = refs[:-6]
    q_o, k_o, v_o, out_o, up_o, down_o = refs[-6:]
    total = functools.reduce(jnp.add, [r[...].astype(f32) for r in parts])
    for i, ref in enumerate((q_o, k_o, v_o)):
        ref[...] = total[i * width : (i + 1) * width].T
    r = out_o.shape[0]
    for h in range(out_o.shape[1] // LANES):
        out_o[:, h * LANES : (h + 1) * LANES] = total[3 * width + h * r : 3 * width + (h + 1) * r]
    units = up_keep.shape[0]
    near = scalars[1]
    own = pl.ds(pl.multiple_of(near * units, LANES), units)
    other = pl.ds(pl.multiple_of((1 - near) * units, LANES), units)
    up_o[:, own] = up_keep[...].astype(f32).T
    up_o[:, other] = up_got[...].astype(f32).T
    down_o[...] = down[...].astype(f32)


def whole(shape):
    return pl.BlockSpec(shape, lambda *_: (0,) * len(shape))


def struct(shape, dtype):
    return jax.ShapeDtypeStruct(shape, dtype)


def tree_sum(parts):
    while len(parts) > 1:
        parts = [parts[i] + parts[i + 1] for i in range(0, len(parts), 2)]
    return parts[0]


def shards(
    n_far,
    n_keys,
    latents,
    patches,
    frame_counts,
    time_embedding,
    media_gain,
    media_bias,
    latent_gain,
    latent_bias,
    ff_gain,
    ff_bias,
    query_weight,
    key_weight,
    value_weight,
    out_weight,
    up_weight,
    down_weight,
    cotangent,
):
    media, own, dim = latents.shape
    key_rows = patches.shape[1]
    inner = query_weight.shape[1]
    hidden = up_weight.shape[1]
    frames = key_rows // PATCH
    n_frames = time_embedding.shape[0]
    n_media = n_far * PAIR
    rows = media * own
    all_rows = media * key_rows
    width = inner // n_keys
    each = dim // n_media
    aligned = each == LANES and width % LANES == 0 and n_far == n_keys
    far = lax.axis_index("far")
    near = lax.axis_index("near")
    key = lax.axis_index("keys")
    own_group = key // (n_keys // 2)
    scalars = jnp.stack([key, near, far, far, key * PAIR + near, own_group, jnp.full_like(far, dim)])
    scalars = scalars.astype(jnp.int32)

    def over_keys(value, shift):
        return lax.ppermute(value, "keys", [(i, i ^ shift) for i in range(n_keys)])

    def over_near(value):
        return lax.ppermute(value, "near", [(0, 1), (1, 0)])

    def over_far(value, shift):
        return lax.ppermute(value, "far", [(i, i ^ shift) for i in range(n_far)])

    def exchange_keys(slots):
        return [slots[0]] + [over_keys(slots[s], s) for s in range(1, n_keys)]

    def gather_keys(value):
        slots = [None] * n_keys
        for s in range(0, n_keys, 2):
            slots[s] = value if s == 0 else over_keys(value, s)
        for s in range(0, n_keys, 2):
            slots[s + 1] = over_keys(slots[s], 1)
        return slots

    def add(left, right):
        return (left.astype(f32) + right.astype(f32)).astype(bf16)

    lat = latents.reshape(rows, dim)
    cot = cotangent.reshape(rows, dim)
    row = lambda v: v.reshape(1, dim)
    packed = inner + LANES
    patch_block = pl.BlockSpec((1, key_rows, dim), lambda i, *_: (i, 0, 0))
    inner_block = pl.BlockSpec((1, key_rows, inner), lambda i, *_: (i, 0, 0))
    time_block = whole((n_frames, dim))
    stat_block = pl.BlockSpec((8, key_rows), lambda i, *_: (0, i))
    patch_flops = 4 * all_rows * dim * inner
    att_flops = 4 * media * n_keys * own * (key_rows + own) * inner * (GROUP // HEAD)

    def call(kernel, name, grid, in_specs, out_specs, out_shape, price, prefetch=1, **more):
        run = pl.pallas_call(
            kernel,
            name=name,
            grid_spec=pltpu.PrefetchScalarGridSpec(
                num_scalar_prefetch=prefetch,
                grid=grid,
                in_specs=in_specs,
                out_specs=out_specs,
                scratch_shapes=more.pop("scratch_shapes", ()),
            ),
            out_shape=out_shape,
            compiler_params=params(),
            cost_estimate=price,
            **more,
        )

        def pinned(*args):
            args = list(args)
            for i in range(prefetch, len(args)):
                if in_specs[i - prefetch].memory_space is None:
                    args[i] = pltpu.with_memory_space_constraint(args[i], pltpu.HBM)
            return run(*args)

        return pinned

    own_rows, q_own = call(
        latent_kernel,
        "latent_project",
        (1,),
        [whole((rows, dim)), whole((1, dim)), whole((1, dim)), whole((rows, dim)), whole((dim, inner))],
        [whole((rows, 2 * dim)), whole((rows, inner))],
        (struct((rows, 2 * dim), bf16), struct((rows, inner), bf16)),
        cost(2 * rows * dim * inner, 2 * dim * inner + 14 * rows * dim),
    )(scalars, lat, row(latent_gain), row(latent_bias), cot, query_weight)
    q_all = exchange_keys([q_own] * n_keys)
    rows_all = lax.all_gather(own_rows, ("near", "keys"), axis=0, tiled=True)

    out = call(
        functools.partial(patch_kernel, n_keys, frames),
        "project_attend",
        (media,),
        [
            patch_block,
            time_block,
            whole((1, dim)),
            whole((1, dim)),
            whole((dim, inner)),
            whole((dim, inner)),
            whole((rows, dim)),
        ]
        + [whole((rows, inner))] * n_keys,
        [
            patch_block,
            inner_block,
            inner_block,
            whole((rows, inner)),
            whole((rows, inner)),
            stat_block,
            pl.BlockSpec((1, key_rows, LANES), lambda i, *_: (i, 0, 0)),
            whole((8, 2 * inner)),
        ]
        + [whole((rows, packed))] * n_keys,
        [
            struct(patches.shape, bf16),
            struct((media, key_rows, inner), bf16),
            struct((media, key_rows, inner), bf16),
            struct((rows, inner), bf16),
            struct((rows, inner), bf16),
            struct((8, all_rows), f32),
            struct((media, key_rows, LANES), bf16),
            struct((8, 2 * inner), f32),
        ]
        + [struct((rows, packed), bf16)] * n_keys,
        cost(patch_flops + att_flops, 12 * all_rows * dim),
        prefetch=2,
    )(
        scalars,
        frame_counts,
        patches,
        time_embedding,
        row(media_gain),
        row(media_bias),
        key_weight,
        value_weight,
        own_rows,
        *q_all,
    )
    media_low, kp, vp, kl, vl, norm_stat, once, norm_vec = out[:8]
    shares = out[8:]
    joined = exchange_keys(shares)

    attended, att_low, middle, ff_low, lse = call(
        functools.partial(join_kernel, n_keys),
        "join",
        (1,),
        [whole((rows, dim)), whole((1, dim)), whole((1, dim)), whole((inner, dim))]
        + [whole((rows, packed))] * n_keys,
        [
            whole((rows, inner)),
            whole((rows, inner)),
            whole((rows, dim)),
            whole((rows, dim)),
            whole((rows, LANES)),
        ],
        (
            struct((rows, inner), f32),
            struct((rows, inner), bf16),
            struct((rows, dim), f32),
            struct((rows, dim), bf16),
            struct((rows, LANES), f32),
        ),
        cost(2 * rows * inner * dim, 2 * inner * dim + 16 * rows * dim),
    )(scalars, lat, row(ff_gain), row(ff_bias), out_weight, *joined)
    ff_low, rows_all = tie(ff_low, rows_all)
    ff_all = lax.all_gather(ff_low, ("near", "keys"), axis=0, tiled=True)

    chunk = min(1024, hidden)
    wo_rows = inner * dim // n_keys // dim
    wo_shape = (n_keys, wo_rows, dim) if aligned else (inner, dim)
    resampled, mid_grad, pack, ff_small, out_slots = call(
        functools.partial(forward_kernel, n_keys, aligned),
        "feed_forward",
        (hidden // chunk,),
        [
            whole((rows, inner)),
            whole((rows, inner)),
            whole((rows, dim)),
            whole((rows, dim)),
            whole((rows, LANES)),
            whole((rows, dim)),
            pl.BlockSpec((rows, dim), lambda i, *_: (0, 1)),
            whole((1, dim)),
            whole((inner, dim)),
            pl.BlockSpec((dim, chunk), lambda i, *_: (0, i)),
            pl.BlockSpec((chunk, dim), lambda i, *_: (i, 0)),
        ],
        [
            whole((rows, dim)),
            whole((rows, dim)),
            whole((rows, packed)),
            whole((2, dim)),
            whole(wo_shape),
        ],
        (
            struct((rows, dim), f32),
            struct((rows, dim), f32),
            struct((rows, packed), bf16),
            struct((2, dim), f32),
            struct(wo_shape, bf16),
        ),
        cost(8 * rows * dim * hidden, 4 * dim * hidden + 24 * rows * dim),
        scratch_shapes=[
            pltpu.VMEM((rows, dim), f32),
            pltpu.VMEM((rows, dim), f32),
            pltpu.VMEM((inner, dim) if aligned else (8, LANES), f32),
        ],
    )(
        scalars,
        attended,
        att_low,
        middle,
        ff_low,
        lse,
        cot,
        own_rows,
        row(ff_gain),
        out_weight,
        up_weight,
        down_weight,
    )
    if not aligned:
        c = dim // n_keys
        out_slots = out_slots.reshape(n_media, inner // n_media, n_keys, c // each, each)
        out_slots = out_slots.transpose(2, 3, 1, 0, 4).reshape(n_keys, wo_rows, dim)
        out_slots = jnp.stack(
            [lax.dynamic_index_in_dim(out_slots, key ^ s, 0, False) for s in range(n_keys)]
        )
    packs = gather_keys(pack)

    half_keys = n_keys // 2
    pick = lambda turn: (lambda s: s[5] ^ (1 - turn))
    high = 3 * width + wo_rows

    def regroup(value):
        value = jnp.moveaxis(value, 1, 2).reshape(-1, high, n_far, PAIR, each)
        value = value.transpose(0, 3, 1, 2, 4).reshape(-1, PAIR, high, n_far * each)
        return jnp.where(near == 0, value, value[:, ::-1])

    def attend_back(turn, packs, q_before, small_before):
        g = pick(turn)
        own_cols = pl.BlockSpec((rows, GROUP), lambda i, s, *_: (0, g(s)))
        stat_cols = pl.BlockSpec((rows, LANES), lambda i, *_: (0, inner // LANES))
        key_cols = pl.BlockSpec((1, key_rows, GROUP), lambda i, s, *_: (i, 0, g(s)))
        far_spec = pl.BlockSpec(memory_space=pl.ANY)
        q_width = GROUP if turn == 0 else inner
        chain = (n_keys // 4, PAIR, high, dim // PAIR)
        out = call(
            functools.partial(
                attend_back_kernel, n_keys, frames, turn, inner // HEAD, width, aligned
            ),
            "attend_back",
            (media,),
            [own_cols] * (2 * n_keys)
            + [stat_cols] * n_keys
            + [key_cols, key_cols, own_cols, own_cols]
            + [
                pl.BlockSpec((8, GROUP), lambda i, s, *_: (0, g(s))),
                pl.BlockSpec((8, GROUP), lambda i, s, *_: (0, inner // GROUP + g(s))),
                patch_block,
                pl.BlockSpec((1, key_rows, LANES), lambda i, *_: (i, 0, 0)),
                whole((8, all_rows)),
                pl.BlockSpec((rows, dim), lambda i, *_: (0, 0)),
                whole((1, dim)),
                whole((1, dim)),
            ]
            + [far_spec] * 4
            + [whole((rows, GROUP))] * len(q_before)
            + [whole((8, dim))] * len(small_before),
            [
                pl.BlockSpec((2, GROUP, key_rows), lambda i, *_: (0, 0, i)),
                whole((8, all_rows)),
                whole((rows, GROUP)),
                whole((rows, GROUP)),
                whole(chain),
                whole(chain),
                whole((8, dim)),
            ]
            + [whole((rows, q_width))] * n_keys,
            [
                struct((2, GROUP, all_rows), bf16),
                struct((8, all_rows), f32),
                struct((rows, GROUP), bf16),
                struct((rows, GROUP), bf16),
                struct(chain, bf16),
                struct(chain, bf16),
                struct((8, dim), f32),
            ]
            + [struct((rows, q_width), bf16)] * n_keys,
            cost(5 * att_flops // 4 + patch_flops // 2, 4 * all_rows * (inner + dim)),
            prefetch=2,
            scratch_shapes=[
                pltpu.VMEM((2 * GROUP + 16, dim), f32),
                pltpu.VMEM((2 * GROUP, LANES), f32),
                pltpu.VMEM((8, LANES), f32),
                pltpu.VMEM((n_keys * rows, GROUP), bf16),
                pltpu.VMEM((n_keys * rows, dim), bf16),
                pltpu.VMEM((GROUP // width, wo_rows, dim), bf16),
                pltpu.VMEM((dim, GROUP), bf16),
                pltpu.VMEM((dim, GROUP), bf16),
                pltpu.SemaphoreType.DMA((4,)),
            ],
        )(
            scalars,
            frame_counts,
            *q_all,
            *packs,
            *packs,
            kp,
            vp,
            kl,
            vl,
            norm_vec,
            norm_vec,
            media_low,
            once,
            norm_stat,
            own_rows,
            row(media_gain),
            row(media_bias),
            rows_all,
            out_slots,
            key_weight,
            value_weight,
            *q_before,
            *small_before,
        )
        chains = out[4:6] if aligned else [regroup(v) for v in out[4:6]]
        return out[:4], chains, out[6], out[7:]

    group_rows = PAIR * n_keys * rows
    ff_all, *packs = tie(ff_all, *packs)

    units = hidden // (n_keys * PAIR)
    ff_partial = call(
        functools.partial(ff_grad_kernel, aligned),
        "feed_forward_weights",
        (1,),
        [
            whole((group_rows, dim)),
            pl.BlockSpec((group_rows, dim), lambda i, s: (0, 1)),
            pl.BlockSpec((dim, units), lambda i, s: (0, s[4])),
            pl.BlockSpec((units, dim), lambda i, s: (s[4], 0)),
        ],
        whole((2 * units, dim)),
        struct((2 * units, dim), bf16),
        cost(8 * group_rows * dim * units, 8 * dim * units + 4 * group_rows * dim),
    )(scalars, ff_all, rows_all, up_weight, down_weight)
    blocks = n_far // n_keys
    if not aligned:
        pieces = ff_partial[units:].reshape(blocks, units // blocks, n_keys, dim // n_keys)
        pieces = pieces.transpose(0, 2, 1, 3).reshape(n_far, units, dim // n_far)
        pieces = pieces.transpose(1, 0, 2).reshape(units, dim)
        ups = ff_partial[:units].reshape(units, n_far, PAIR, each)
        ups = jnp.where(near == 0, ups, ups[:, :, ::-1]).reshape(units, dim)
        ff_partial = jnp.concatenate([ups, pieces], 0)
    ff_partial, packs[0] = tie(ff_partial, packs[0])
    ff_sum = lax.psum_scatter(ff_partial, "far", scatter_dimension=1, tiled=True)

    (kv_a, stat_a, kl_a, vl_a), (given_a, kept_a), media_small, q_a = attend_back(0, packs, [], [])
    far_core = over_keys(given_a, 1)
    (kv_b, stat_b, kl_b, vl_b), (given_b, kept_b), media_small, q_b = attend_back(
        1, packs, q_a, [media_small]
    )
    far_core, given_b, *q_b = tie(far_core, given_b, *q_b)
    far_sum = add(kept_a, far_core)

    col = lambda turn: pl.BlockSpec((dim, GROUP), lambda i, s: (0, s[5] ^ (1 - turn)))
    both = lambda value: [value, value]

    pieces = 3
    each_piece = media // pieces

    def patch_back(piece, gain, patches_grad):
        at = piece * each_piece
        block = pl.BlockSpec((1, key_rows, dim), lambda i, *_: (i + at, 0, 0))
        keys = pl.BlockSpec((2, GROUP, key_rows), lambda i, *_: (0, 0, i + at))
        stat = pl.BlockSpec((8, key_rows), lambda i, *_: (0, i + at))
        return call(
            functools.partial(patch_back_kernel, frames),
            "patch_back",
            (each_piece,),
            [
                keys,
                keys,
                stat,
                stat,
                stat,
                block,
                time_block,
                whole((1, dim)),
                col(0),
                col(0),
                col(1),
                col(1),
                pl.BlockSpec(memory_space=pl.ANY),
            ],
            block,
            struct(patches.shape, bf16),
            cost(patch_flops // pieces, 8 * all_rows * dim // pieces),
            **({} if piece == 0 else {"input_output_aliases": {13: 0}}),
        )(
            scalars,
            kv_a,
            kv_b,
            stat_a,
            stat_b,
            norm_stat,
            patches,
            time_embedding,
            gain,
            key_weight,
            value_weight,
            key_weight,
            value_weight,
            gain if piece == 0 else patches_grad,
        )

    def sum_far(value):
        return tree_sum([value] + [over_far(value, s) for s in range(1, n_far)])

    gain = row(media_gain)
    far_sum, gain, given_b, *q_b = tie(far_sum, gain, given_b, *q_b)
    far_near = over_near(far_sum[:, 1])
    near_core = over_keys(given_b, 1)
    q_slots = exchange_keys(q_b)
    patches_grad = patch_back(0, gain, None)
    patches_grad, far_near, near_core, *q_slots = tie(patches_grad, far_near, near_core, *q_slots)
    far_half = add(far_sum[:, 0], far_near)
    near_sum = add(kept_b, near_core)
    near_sum, far_half, lat, ff_sum = tie(near_sum, far_half, lat, ff_sum)
    far_got = [over_keys(far_half[j], half_keys + 2 * j) for j in range(n_keys // 4)]
    total = near_sum[0]
    for j in range(1, n_keys // 4):
        total = add(total, over_keys(near_sum[j], 2 * j))
    near_got = over_near(total[1])
    route = []
    for m in range(n_media):
        for k in range(n_keys):
            block, owner = divmod(m // PAIR, n_keys)
            target = (k * PAIR + m % PAIR) * blocks + block
            route.append((m * n_keys + k, target * n_keys + owner))
    down_grad = lax.ppermute(ff_sum[units:], ("far", "near", "keys"), route)
    small_rows = -(-(n_frames + 6) // 8) * 8
    latents_grad, small = call(
        functools.partial(latent_back_kernel, n_keys, frames, n_frames),
        "latent_back",
        (1,),
        [whole((rows, dim)), whole((1, dim)), whole((rows, dim)), whole((8, dim)), whole((2, dim))]
        + [whole((rows, GROUP)), col(0), whole((rows, GROUP)), col(0)]
        + [whole((rows, GROUP)), col(1), whole((rows, GROUP)), col(1)]
        + [whole((dim, inner))]
        + [whole((rows, inner))] * n_keys,
        [whole((rows, dim)), whole((small_rows, dim))],
        (struct((rows, dim), f32), struct((small_rows, dim), f32)),
        cost(6 * rows * dim * inner, 6 * dim * inner + 20 * rows * dim),
    )(
        scalars,
        lat,
        row(latent_gain),
        mid_grad,
        media_small,
        ff_small,
        kl_a,
        key_weight,
        vl_a,
        value_weight,
        kl_b,
        key_weight,
        vl_b,
        value_weight,
        query_weight,
        *q_slots,
    )

    gain, small, ff_sum = tie(gain, small, ff_sum)
    small_got = over_keys(small, 1)
    up_keep = ff_sum[:units, :each]
    up_got = over_near(ff_sum[:units, each:])
    patches_grad = patch_back(1, gain, patches_grad)
    patches_grad, small_got, near_got, *far_got = tie(patches_grad, small_got, near_got, *far_got)
    small = small + small_got
    total = total[0]
    for value in far_got:
        total = add(total, value)
    total = add(total, near_got)
    if not aligned:
        total = total.reshape(-1, n_far, each)
        total = jnp.concatenate(
            [lax.dynamic_index_in_dim(total, far ^ s, 1, False) for s in range(n_far)], 1
        )
    total, small, gain = tie(total, small, gain)
    parts = [over_far(total[:, s * each : (s + 1) * each], s) for s in range(1, n_far)]
    small = tree_sum([small] + [over_keys(small, s) for s in range(2, n_keys, 2)])
    patches_grad = patch_back(2, gain, patches_grad)
    patches_grad, small, up_got, down_grad, *parts = tie(
        patches_grad, small, up_got, down_grad, *parts
    )
    small = small + over_near(small)
    small, up_got = tie(small, up_got)
    small = sum_far(small)
    parts = [total[:, :each]] + parts
    if aligned:
        q_grad, k_grad, v_grad, out_grad, up_grad, down_grad = call(
            functools.partial(finish_kernel, width),
            "finish_weights",
            (1,),
            [whole((units, each))] * 2
            + [whole((units, dim // n_keys))]
            + [whole(p.shape) for p in parts],
            [whole((each, width))] * 3
            + [
                whole((inner // n_media, dim // n_keys)),
                whole((each, PAIR * units)),
                whole((units, dim // n_keys)),
            ],
            [struct((each, width), f32)] * 3
            + [
                struct((inner // n_media, dim // n_keys), f32),
                struct((each, PAIR * units), f32),
                struct((units, dim // n_keys), f32),
            ],
            cost(0, 16 * width * each + 12 * units * each),
        )(scalars, up_keep, up_got, down_grad, *parts)
    else:
        total = functools.reduce(jnp.add, [p.astype(f32) for p in parts])
        q_grad, k_grad, v_grad = (total[i * width : (i + 1) * width].T for i in range(3))
        out_grad = total[3 * width :].reshape(-1, inner // n_media, each)
        out_grad = out_grad.transpose(1, 0, 2).reshape(inner // n_media, dim // n_keys)
        up_grad = jnp.where(
            near == 0,
            jnp.concatenate([up_keep, up_got], 0),
            jnp.concatenate([up_got, up_keep], 0),
        ).T.astype(f32)
        down_grad = down_grad.reshape(units // blocks, dim // n_keys).astype(f32)

    return (
        resampled.reshape(latents.shape),
        patches_grad,
        latents_grad.reshape(latents.shape),
        small[:n_frames],
        small[n_frames],
        small[n_frames + 1],
        small[n_frames + 2],
        small[n_frames + 3],
        small[n_frames + 4],
        small[n_frames + 5],
        q_grad,
        k_grad,
        v_grad,
        out_grad,
        up_grad,
        down_grad,
    )


def solution(mesh):
    n_media, n_keys = mesh.shape["media"], mesh.shape["keys"]
    n_far = n_media // PAIR
    fine = Mesh(mesh.devices.reshape(n_far, PAIR, n_keys), ("far", "near", "keys"))
    split = P(("far", "near"), "keys", None)
    return jax.shard_map(
        functools.partial(shards, n_far, n_keys),
        mesh=fine,
        in_specs=(split, split, P(("far", "near"))) + (P(),) * 13 + (split,),
        out_specs=(split,) * 3 + (P(),) * 7 + (P(("far", "near"), "keys"),) * 6,
        check_vma=False,
    )
```

```python
import functools

import jax
import jax.numpy as jnp
from jax import lax
from jax.experimental import pallas as pl
from jax.experimental.pallas import tpu as pltpu
from jax.sharding import Mesh, PartitionSpec as P

HEAD = 64
PATCH = 256
GROUP = 256
LANES = 128

VMEM_LIMIT = 60 << 20

EPS = 1e-05
NEG = -1e30
PAIR = 2

f32 = jnp.float32
bf16 = jnp.bfloat16


def mul(left, right, contract=((1,), (0,)), precision=None):
    return lax.dot_general(
        left, right, (contract, ((), ())), precision=precision, preferred_element_type=f32
    )


NN = ((1,), (0,))
NT = ((1,), (1,))
TN = ((0,), (0,))


def norm_parts(values):
    centre = jnp.mean(values, -1, keepdims=True)
    shifted = values - centre
    spread = jnp.mean(shifted * shifted, -1, keepdims=True)
    return centre, lax.rsqrt(spread + EPS), shifted


def norm(values, gain, bias):
    _, scale, shifted = norm_parts(values)
    return shifted * scale * gain + bias


def norm_back(values, gain, grad):
    _, scale, shifted = norm_parts(values)
    unit = shifted * scale
    scaled = grad * gain
    first = jnp.mean(scaled, -1, keepdims=True)
    second = jnp.mean(scaled * unit, -1, keepdims=True)
    back = scale * (scaled - first - unit * second)
    return (
        back,
        jnp.sum(grad * unit, 0, keepdims=True),
        jnp.sum(grad, 0, keepdims=True),
    )


def gelu_parts(hidden):
    cdf = 0.5 * (1.0 + lax.erf(hidden * (2.0**-0.5)))
    pdf = jnp.exp(-0.5 * hidden * hidden) * 0.3989422804014327
    return cdf, cdf + hidden * pdf


def head_mask(rows, width, heads):
    row = lax.broadcasted_iota(jnp.int32, (heads * rows, width), 0) // rows
    col = lax.broadcasted_iota(jnp.int32, (heads * rows, width), 1)
    return row, col


def spread_heads(values):
    heads = values.shape[1] // HEAD
    row, col = head_mask(values.shape[0], values.shape[1], heads)
    return jnp.where(row == col // HEAD, jnp.concatenate([values] * heads, 0), jnp.zeros((), values.dtype))


def fold_heads(values):
    heads = values.shape[1] // HEAD
    rows = values.shape[0] // heads
    row, col = head_mask(rows, values.shape[1], heads)
    kept = jnp.where(row == col // HEAD, values, 0.0)
    total = kept[:rows]
    for h in range(1, heads):
        total = total + kept[h * rows : (h + 1) * rows]
    return total


def three_parts(values, lane, start, slots):
    high = values.astype(bf16).astype(f32)
    rest = values - high
    middle = rest.astype(bf16).astype(f32)
    low = rest - middle
    place = lane // slots - start
    return jnp.where(place == 0, high, jnp.where(place == 1, middle, jnp.where(place == 2, low, 0.0)))


def cost(flops, moved, special=0):
    return pl.CostEstimate(flops=int(flops), bytes_accessed=int(moved), transcendentals=int(special))


def params():
    return pltpu.CompilerParams(vmem_limit_bytes=VMEM_LIMIT)


def tie(*values):
    return lax.optimization_barrier(values)


def latent_kernel(lat, gain, bias, cot, wq, rows_o, q_o):
    dim = lat.shape[1]
    low = norm(lat[...], gain[...], bias[...]).astype(bf16)
    rows_o[:, :dim] = low
    rows_o[:, dim:] = cot[...].astype(bf16)
    q_o[...] = mul(low, wq[...]).astype(bf16)


def two_parts(values):
    high = values.astype(bf16)
    return high, (values - high.astype(f32)).astype(bf16)


def masked_scores(query, keys, frames, first, count):
    scores = mul(query, keys, NT)
    parts = []
    for f in range(frames):
        part = scores[:, f * PATCH : (f + 1) * PATCH]
        parts.append(jnp.where(first + f < count, part, NEG))
    return jnp.concatenate(parts + [scores[:, frames * PATCH :]], 1)


def patch_kernel(n_keys, frames, scalars, counts, patches, time, gain, bias, wk, wv, lat_low, *refs):
    q = refs[:n_keys]
    low_o, k_o, v_o, kl_o, vl_o, stat_o, once_o, vec_o = refs[n_keys : n_keys + 8]
    outs = refs[n_keys + 8 :]
    step = pl.program_id(0)

    @pl.when(step == 0)
    def _():
        kl_o[...] = mul(lat_low[...], wk[...]).astype(bf16)
        vl_o[...] = mul(lat_low[...], wv[...]).astype(bf16)
        row = lax.broadcasted_iota(jnp.int32, (16, gain.shape[1]), 0)
        both = jnp.where(row % 2 == 0, gain[...], bias[...])
        high, low = two_parts(both)
        both = jnp.where(row < 2, high.astype(f32), jnp.where(row < 4, low.astype(f32), 0.0)).astype(bf16)
        for i, w in enumerate((wk, wv)):
            term = mul(both, w[...])
            vec_o[:, i * w.shape[1] : (i + 1) * w.shape[1]] = term[:8] + pltpu.roll(term, 14, 0)[:8]

    for f in range(frames):
        rows = pl.ds(f * PATCH, PATCH)
        framed = patches[0, rows, :].astype(f32) + time[pl.ds(scalars[0] * frames + f, 1), :]
        centre, scale, shifted = norm_parts(framed)
        low = (shifted * scale * gain[...] + bias[...]).astype(bf16)
        low_o[0, rows, :] = low
        k_o[0, rows, :] = mul(low, wk[...]).astype(bf16)
        v_o[0, rows, :] = mul(low, wv[...]).astype(bf16)
        lane = lax.broadcasted_iota(jnp.int32, (PATCH, LANES), 1)
        stat = jnp.where(lane == 0, centre, jnp.where(lane == 1, scale, 0.0))
        stat_o[:, f * PATCH : (f + 1) * PATCH] = stat.T[:8]
        high = scale.astype(bf16).astype(f32)
        once = jnp.where(lane == 0, 1.0, jnp.where(lane == 1 + f, high, 0.0))
        once_o[0, rows, :] = jnp.where(lane == 1 + frames + f, scale - high, once).astype(bf16)

    own = q[0].shape[0] // pl.num_programs(0)
    inner = q[0].shape[1]
    heads = inner // HEAD
    count = counts[step]
    first = scalars[0] * frames
    here = pl.ds(pl.multiple_of(step * own, own), own)
    query = jnp.concatenate([r[here, :] for r in q], 0)
    rows = query.shape[0]
    stats = jnp.zeros((rows, LANES), f32)
    shares = []
    for g in range(inner // GROUP):
        cols = slice(g * GROUP, (g + 1) * GROUP)
        wide = spread_heads(query[:, cols] * bf16(HEAD**-0.5))
        keys = jnp.concatenate([k_o[0, :, cols], kl_o[here, cols]], 0)
        values = jnp.concatenate([v_o[0, :, cols], vl_o[here, cols]], 0)
        scores = masked_scores(wide, keys, frames, first, count)
        top = jnp.max(scores, -1, keepdims=True)
        raw = jnp.exp(scores - top)
        total = jnp.sum(raw, -1, keepdims=True)
        share = mul(raw.astype(bf16), values) * (1.0 / total)
        shares.append(fold_heads(share).astype(bf16))
        level = top + jnp.log(total)
        row, lane = head_mask(rows, LANES, GROUP // HEAD)
        kept = jnp.where(lane % heads == row + g * (GROUP // HEAD), level, 0.0)
        for h in range(GROUP // HEAD):
            stats = stats + kept[h * rows : (h + 1) * rows]
    lane = lax.broadcasted_iota(jnp.int32, stats.shape, 1)
    packed = jnp.concatenate(shares + [three_parts(stats, lane, 0, heads).astype(bf16)], 1)
    for s in range(n_keys):
        outs[s][here, :] = packed[s * own : (s + 1) * own]


def sum_runs(stats, heads, start):
    total = None
    for part in range(3):
        shift = (-(start + part) * heads) % LANES
        term = pltpu.roll(stats, shift, 1) if shift else stats
        total = term if total is None else total + term
    return total


def join(latents, gain, bias, wo, slots, att_o, low_o, mid_o, ff_o, lse_o):
    inner = att_o.shape[1]
    heads = inner // HEAD
    levels = [sum_runs(r[:, inner:].astype(f32), heads, 0) for r in slots]
    top = functools.reduce(jnp.maximum, levels)
    weights = [jnp.exp(v - top) for v in levels]
    total = functools.reduce(jnp.add, weights)
    inverse = 1.0 / total
    lane = lax.broadcasted_iota(jnp.int32, (LANES, inner), 0)
    col = lax.broadcasted_iota(jnp.int32, (LANES, inner), 1)
    select = jnp.where(lane == col // HEAD, 1.0, 0.0)
    attended = None
    for s in range(len(slots)):
        wide = mul(weights[s] * inverse, select, NN, lax.Precision.HIGHEST)
        term = wide * slots[s][:, :inner].astype(f32)
        attended = term if attended is None else attended + term
    low = attended.astype(bf16)
    middle = latents[...] + mul(low, wo[...])
    att_o[...] = attended
    low_o[...] = low
    mid_o[...] = middle
    ff_o[...] = norm(middle, gain[...], bias[...]).astype(bf16)
    lse_o[...] = top + jnp.log(total)


def forward_kernel(
    n_keys,
    aligned,
    scalars,
    latents,
    cot,
    out_low,
    gain,
    bias,
    wo,
    up,
    down,
    *refs,
):
    slots = refs[:n_keys]
    res_o, mid_grad_o, pack_o, small_o, wo_grad_o, ff_low = refs[n_keys : n_keys + 6]
    res_acc, in_acc, wo_acc, attended, att_low, middle, lse = refs[n_keys + 6 :]
    step = pl.program_id(0)

    @pl.when(step == 0)
    def _():
        res_acc[...] = jnp.zeros_like(res_acc)
        in_acc[...] = jnp.zeros_like(in_acc)
        join(latents, gain, bias, wo, slots, attended, att_low, middle, ff_low, lse)

    hidden = mul(ff_low[...], up[...])
    act_grad = mul(out_low[...], down[...], NT)
    cdf, slope = gelu_parts(hidden)
    res_acc[...] += mul((hidden * cdf).astype(bf16), down[...])
    in_acc[...] += mul((act_grad * slope).astype(bf16), up[...], NT)

    @pl.when(step == pl.num_programs(0) - 1)
    def _():
        inner = attended.shape[1]
        heads = inner // HEAD
        res_o[...] = middle[...] + res_acc[...]
        back, gain_grad, bias_grad = norm_back(middle[...], gain[...], in_acc[...])
        small_o[0:1, :] = gain_grad
        small_o[1:2, :] = bias_grad
        mid_grad = cot[...] + back
        mid_grad_o[...] = mid_grad
        branch = mid_grad.astype(bf16)
        att_grad = mul(branch, wo[...], NT).astype(bf16)
        col = lax.broadcasted_iota(jnp.int32, (inner, LANES), 0)
        lane = lax.broadcasted_iota(jnp.int32, (inner, LANES), 1)
        select = jnp.where(col // HEAD == lane % heads, 1.0, 0.0)
        delta = mul(attended[...] * att_grad.astype(f32), select, NN, lax.Precision.HIGHEST)
        lane = lax.broadcasted_iota(jnp.int32, delta.shape, 1)
        level = jnp.where(lane < heads, lse[...], 0.0)
        level = level + pltpu.roll(level, heads, 1) + pltpu.roll(level, 2 * heads, 1)
        stats = three_parts(level, lane, 0, heads) + three_parts(delta, lane, 3, heads)
        pack_o[...] = jnp.concatenate([att_grad, stats.astype(bf16)], 1)
        wo_grad = mul(att_low[...], branch, TN)
        if aligned:
            wo_acc[...] = wo_grad
            slot_rows(scalars, wo_acc, wo_grad_o, n_keys)
        else:
            wo_grad_o[...] = wo_grad.astype(bf16)


def slot_rows(scalars, full, out, n_keys):
    lanes = LANES
    n_media = out.shape[2] // lanes
    r = full.shape[0] // n_media
    c = full.shape[1] // n_keys
    for s in range(n_keys):
        owner = (scalars[0] ^ s) * c
        for m in range(n_media):
            place = slice(m * lanes, (m + 1) * lanes)
            for h in range(c // lanes):
                start = pl.multiple_of(owner + h * lanes, lanes)
                out[s, h * r : (h + 1) * r, place] = full[
                    m * r : (m + 1) * r, pl.ds(start, lanes)
                ].astype(bf16)


def ff_grad_kernel(n_keys, aligned, scalars, ff_all, out_all, up, down, *refs):
    own_ups, grad_o = refs[:-1], refs[-1]
    units, dim = down.shape
    step = pl.program_id(0)
    hidden = mul(ff_all[...], up[...])
    act_grad = mul(out_all[...], down[...], NT)
    _, slope = gelu_parts(hidden)
    up_grad = mul((act_grad * slope).astype(bf16), ff_all[...], TN).astype(bf16)
    rows = pl.ds(pl.multiple_of(step * units, 8), units)
    if not aligned:
        grad_o[0] = up_grad
        hidden = mul(ff_all[...], own_ups[0][...])
        cdf, _ = gelu_parts(hidden)
        grad_o[1] = mul((hidden * cdf).astype(bf16), out_all[...], TN).astype(bf16)
        return
    for j in range(dim // LANES):
        place = ((j // PAIR) * PAIR + (scalars[1] ^ (j % PAIR))) * LANES
        grad_o[0, rows, pl.ds(pl.multiple_of(place, LANES), LANES)] = up_grad[
            :, j * LANES : (j + 1) * LANES
        ]
    each = own_ups[0].shape[1]
    cols = dim // n_keys
    hidden = mul(ff_all[...], jnp.concatenate([r[...] for r in own_ups], 1))
    cdf, _ = gelu_parts(hidden)
    down_grad = mul((hidden * cdf).astype(bf16), out_all[...], TN).astype(bf16)
    for n in range(len(own_ups)):
        lanes = pl.ds(pl.multiple_of((step * len(own_ups) + n) * cols, LANES), cols)
        for k in range(n_keys):
            place = pl.ds(pl.multiple_of((scalars[0] ^ k) * each, each), each)
            grad_o[1, place, lanes] = down_grad[
                n * each : (n + 1) * each, k * cols : (k + 1) * cols
            ]


def attend_back_kernel(n_keys, frames, turn, heads, width, aligned, scalars, counts, *refs):
    refs = list(refs)
    take = lambda n: [refs.pop(0) for _ in range(n)]
    q, grads, stat = take(n_keys), take(n_keys), take(n_keys)
    kp, vp, kl, vl, k_vec, v_vec, low, once, norm_stat, lat_own, gain, bias = take(12)
    rows_far, wo_far, wk_far, wv_far = take(4)
    q_before = take(n_keys if turn else 0)
    small_before = take(turn)
    kv_t_o, stat_o, kl_o, vl_o, given, kept, small = take(7)
    q_o = take(n_keys)
    grad_acc, sums, scalar_sums, q_acc, rows_all, wo_g, wk, wv, sems = refs
    rows = kl_o.shape[0]
    own = rows // pl.num_programs(0)
    dim = low.shape[2]
    per = GROUP // HEAD
    step = pl.program_id(0)
    count = counts[step]
    first_frame = scalars[0] * frames
    group = scalars[5] ^ (1 - turn)
    owners = GROUP // width
    group_cols = pl.ds(pl.multiple_of(group * GROUP, GROUP), GROUP)
    near_rows = pl.ds(pl.multiple_of(scalars[1] * n_keys * rows, 8), n_keys * rows)
    fetches = [
        pltpu.make_async_copy(rows_far.at[near_rows, pl.ds(0, dim)], rows_all, sems.at[0]),
        pltpu.make_async_copy(wo_far.at[pl.ds(owners * (1 - turn), owners)], wo_g, sems.at[1]),
        pltpu.make_async_copy(wk_far.at[:, group_cols], wk, sems.at[2]),
        pltpu.make_async_copy(wv_far.at[:, group_cols], wv, sems.at[3]),
    ]

    @pl.when(step == 0)
    def _():
        for fetch in fetches:
            fetch.start()
        grad_acc[...] = jnp.zeros_like(grad_acc)
        sums[...] = jnp.zeros_like(sums)
        scalar_sums[...] = jnp.zeros_like(scalar_sums)

    here = pl.ds(pl.multiple_of(step * own, own), own)
    query = jnp.concatenate([r[here, :] for r in q], 0)
    grad = jnp.concatenate([r[here, :] for r in grads], 0)
    stats = jnp.concatenate([r[here, :] for r in stat], 0).astype(f32)
    n_query = query.shape[0]
    row, lane = head_mask(n_query, LANES, per)
    tiled = jnp.concatenate([stats] * per, 0)
    mine = lane % heads == row + group * per
    level = jnp.sum(jnp.where(mine & (lane < 3 * heads), tiled, 0.0), -1, keepdims=True)
    delta = jnp.sum(
        jnp.where(mine & (lane >= 3 * heads) & (lane < 6 * heads), tiled, 0.0), -1, keepdims=True
    )
    wide = spread_heads(query * bf16(HEAD**-0.5))
    wide_grad = spread_heads(grad)
    keys = jnp.concatenate([kp[0], kl[here, :]], 0)
    values = jnp.concatenate([vp[0], vl[here, :]], 0)
    n_patch = kp.shape[1]
    scores = masked_scores(wide, keys, frames, first_frame, count)
    probs = jnp.exp(scores - level)
    prob_grad = mul(wide_grad, values, NT)
    score_grad = probs * (prob_grad - delta)
    along = jnp.sum(score_grad * scores + probs * prob_grad, 0, keepdims=True)
    score_grad = score_grad.astype(bf16)
    key_side = jnp.concatenate([wide, mul(wide, k_vec[...].astype(bf16), NT).astype(bf16)], 1)
    value_side = jnp.concatenate(
        [wide_grad, mul(wide_grad, v_vec[...].astype(bf16), NT).astype(bf16)], 1
    )
    key_t = mul(key_side, score_grad, TN)
    value_t = mul(value_side, probs.astype(bf16), TN)
    kl_o[here, :] = key_t[:GROUP, n_patch:].T.astype(bf16)
    vl_o[here, :] = value_t[:GROUP, n_patch:].T.astype(bf16)
    kv = jnp.concatenate([key_t[:GROUP, :n_patch], value_t[:GROUP, :n_patch]], 0).astype(bf16)
    kv_t_o[0] = kv[:GROUP]
    kv_t_o[1] = kv[GROUP:]
    ends = key_t[GROUP:, :n_patch] + value_t[GROUP:, :n_patch]
    line = lax.broadcasted_iota(jnp.int32, ends.shape, 0)
    stat_rows = jnp.where(line == 1, along[:, :n_patch] - ends, ends)
    span = pl.ds(pl.multiple_of(step * n_patch, n_patch), n_patch)
    stat_o[:, span] = stat_rows

    scale = norm_stat[1:2, span] * (1.0 / dim)
    first = stat_rows[0:1, :] * scale
    second = stat_rows[1:2, :] * scale
    frame = lax.broadcasted_iota(jnp.int32, (16, n_patch), 1) // PATCH
    row16 = lax.broadcasted_iota(jnp.int32, (16, n_patch), 0)
    high = second.astype(bf16).astype(f32)
    same = frame == row16 % frames
    ends = jnp.where(same & (row16 < frames), high, 0.0)
    ends = jnp.where(same & (row16 >= frames) & (row16 < 2 * frames), second - high, ends)
    grad_acc[...] += mul(jnp.concatenate([kv, ends.astype(bf16)], 0), low[0])
    sums[...] += mul(kv, once[0])
    line = lax.broadcasted_iota(jnp.int32, scalar_sums.shape, 0)
    adds = jnp.zeros(scalar_sums.shape, f32)
    for f in range(frames):
        span = slice(f * PATCH, (f + 1) * PATCH)
        adds = jnp.where(line == f, jnp.sum(first[:, span], -1, keepdims=True), adds)
        adds = jnp.where(line == frames + f, jnp.sum(second[:, span], -1, keepdims=True), adds)
    scalar_sums[...] += adds

    query_grad = mul(score_grad, keys)
    query_grad = (fold_heads(query_grad) * HEAD**-0.5).astype(bf16)
    for s in range(n_keys):
        part = query_grad[s * own : (s + 1) * own]
        place = pl.multiple_of((scalars[0] ^ s) * rows + step * own, own)
        q_acc[pl.ds(place, own), :] = part
        if turn == 0:
            q_o[s][here, :] = part
        else:
            other = pl.ds(pl.multiple_of((1 - group) * GROUP, GROUP), GROUP)
            q_o[s][here, group_cols] = part
            q_o[s][here, other] = q_before[s][here, :]

    @pl.when(step == pl.num_programs(0) - 1)
    def _():
        for fetch in fetches:
            fetch.wait()
        behind = None
        for part in two_parts(sums[...]):
            for i, w in enumerate((wk, wv)):
                term = mul(part[i * GROUP : (i + 1) * GROUP], w[...], ((0,), (1,)))
                behind = term if behind is None else behind + term
        bias_grad = behind[0:1]
        main = grad_acc[: 2 * GROUP, :]
        ends = grad_acc[2 * GROUP :, :]
        total = jnp.sum(main[:GROUP] * wk[...].astype(f32).T, 0, keepdims=True)
        total = total + jnp.sum(main[GROUP:] * wv[...].astype(f32).T, 0, keepdims=True)
        over = 1.0 / gain[...]
        lines = []
        for f in range(frames):
            along = ends[f : f + 1] + ends[frames + f : frames + f + 1]
            scaled = behind[1 + f : 2 + f] + behind[1 + frames + f : 2 + frames + f]
            second_sum = scalar_sums[frames + f : frames + f + 1, 0:1]
            lines.append(
                gain[...] * scaled
                - scalar_sums[f : f + 1, 0:1]
                - (along - bias[...] * second_sum) * over
            )
        lines += [(total - bias[...] * bias_grad) * over, bias_grad]
        for i, value in enumerate(lines):
            small[i : i + 1, :] = value + small_before[0][i : i + 1, :] if turn else value
        kv_lat = jnp.concatenate([kl_o[...], vl_o[...]], 1)
        grad_acc[: 2 * GROUP, :] = main + mul(kv_lat, lat_own[...], TN)
        q_grad = mul(q_acc[...], rows_all[...], TN)
        sums_q = q_grad.astype(bf16)
        near = scalars[1] if aligned else 0
        runs = dim // PAIR // LANES
        for j in range(owners):
            out = (given, kept)[j % 2]
            slot = 2 * (j // 2) + 1 - j % 2
            start = ((scalars[0] ^ slot) % owners) * width
            for part in range(3):
                at = pl.multiple_of((part - 1) * GROUP + start, width)
                if part == 0:
                    piece = jnp.zeros((width, dim), bf16)
                    for o in range(owners):
                        same = start == o * width
                        piece = jnp.where(same, sums_q[o * width : (o + 1) * width], piece)
                else:
                    piece = grad_acc[pl.ds(at, width), :].astype(bf16)
                place_rows(out, scalars, j // 2, part * width, piece, aligned)
            place_rows(out, scalars, j // 2, 3 * width, wo_g[slot], aligned)


def place_rows(out, scalars, slot, start, piece, aligned):
    rows = slice(start, start + piece.shape[0])
    half = piece.shape[1] // PAIR
    if aligned:
        for m in range(piece.shape[1] // LANES):
            place = slice((m // PAIR) * LANES, (m // PAIR + 1) * LANES)
            out[slot, scalars[1] ^ (m % PAIR), rows, place] = piece[:, m * LANES : (m + 1) * LANES]
    else:
        for n in range(PAIR):
            out[slot, n, rows, :] = piece[:, n * half : (n + 1) * half]


def patch_back_kernel(
    frames, scalars, kv_a, kv_b, stat_a, stat_b, norm_stat, patches, time, gain, wk_a, wv_a, wk_b, wv_b, _, grad_o
):
    turned = ((0,), (1,))
    inverse = 1.0 / gain.shape[1]
    for f in range(frames):
        rows = pl.ds(f * PATCH, PATCH)
        span = slice(f * PATCH, (f + 1) * PATCH)
        scale = norm_stat[1:2, span]
        first = (stat_a[0:1, span] + stat_b[0:1, span]) * inverse
        second = (stat_a[1:2, span] + stat_b[1:2, span]) * inverse
        slope = scale * scale * second
        level = scale * first - norm_stat[0:1, span] * slope
        line = lax.broadcasted_iota(jnp.int32, (8, PATCH), 0)
        columns = jnp.where(line == 0, scale, jnp.where(line == 1, level, slope)).T
        grad = mul(kv_a[0, :, span], wk_a[...], turned)
        grad = grad + mul(kv_a[1, :, span], wv_a[...], turned)
        grad = grad + mul(kv_b[0, :, span], wk_b[...], turned)
        grad = grad + mul(kv_b[1, :, span], wv_b[...], turned)
        framed = patches[0, rows, :].astype(f32) + time[pl.ds(scalars[0] * frames + f, 1), :]
        back = grad * gain[...] * columns[:, 0:1] - columns[:, 1:2] - framed * columns[:, 2:3]
        grad_o[0, rows, :] = back.astype(bf16)


def latent_back_kernel(n_keys, frames, n_frames, scalars, latents, gain, mid_grad, media_small, ff_small, *refs):
    keys = refs[:8]
    wq = refs[8]
    slots = refs[9 : 9 + n_keys]
    lat_o, small_o = refs[9 + n_keys :]
    query = functools.reduce(jnp.add, [r[...].astype(f32) for r in slots]).astype(bf16)
    grad = mul(query, wq[...], NT)
    for i in range(4):
        grad = grad + mul(keys[2 * i][...], keys[2 * i + 1][...], NT)
    back, gain_grad, bias_grad = norm_back(latents[...], gain[...], grad)
    lat_o[...] = mid_grad[...] + back
    small_o[...] = jnp.zeros_like(small_o)
    for f in range(frames):
        small_o[pl.ds(scalars[0] * frames + f, 1), :] = media_small[f : f + 1, :]
    for i, line in enumerate(
        (media_small[frames : frames + 1, :], media_small[frames + 1 : frames + 2, :], gain_grad, bias_grad)
    ):
        small_o[n_frames + i : n_frames + i + 1, :] = line
    small_o[n_frames + 4 : n_frames + 6, :] = ff_small[...]


def finish_kernel(n_keys, width, scalars, up_keep, up_got, *refs):
    downs, parts = refs[:n_keys], refs[n_keys]
    q_o, k_o, v_o, out_o, up_o, down_o = refs[-6:]
    high = 3 * width + out_o.shape[0] * out_o.shape[1] // LANES
    total = parts[:high].astype(f32)
    for s in range(1, parts.shape[0] // high):
        total = total + parts[s * high : (s + 1) * high].astype(f32)
    for i, ref in enumerate((q_o, k_o, v_o)):
        ref[...] = total[i * width : (i + 1) * width].T
    r = out_o.shape[0]
    for h in range(out_o.shape[1] // LANES):
        out_o[:, h * LANES : (h + 1) * LANES] = total[3 * width + h * r : 3 * width + (h + 1) * r]
    units = up_keep.shape[0]
    near = scalars[1]
    own = pl.ds(pl.multiple_of(near * units, LANES), units)
    other = pl.ds(pl.multiple_of((1 - near) * units, LANES), units)
    up_o[:, own] = up_keep[...].astype(f32).T
    up_o[:, other] = up_got[...].astype(f32).T
    share = downs[0].shape[0]
    for s, ref in enumerate(downs):
        down_o[pl.ds(pl.multiple_of((scalars[0] ^ s) * share, share), share), :] = ref[...].astype(f32)


def whole(shape):
    return pl.BlockSpec(shape, lambda *_: (0,) * len(shape))


def struct(shape, dtype):
    return jax.ShapeDtypeStruct(shape, dtype)


def tree_sum(parts):
    while len(parts) > 1:
        parts = [parts[i] + parts[i + 1] for i in range(0, len(parts), 2)]
    return parts[0]


def shards(
    n_far,
    n_keys,
    latents,
    patches,
    frame_counts,
    time_embedding,
    media_gain,
    media_bias,
    latent_gain,
    latent_bias,
    ff_gain,
    ff_bias,
    query_weight,
    key_weight,
    value_weight,
    out_weight,
    up_weight,
    down_weight,
    cotangent,
):
    media, own, dim = latents.shape
    key_rows = patches.shape[1]
    inner = query_weight.shape[1]
    hidden = up_weight.shape[1]
    frames = key_rows // PATCH
    n_frames = time_embedding.shape[0]
    n_media = n_far * PAIR
    rows = media * own
    all_rows = media * key_rows
    width = inner // n_keys
    each = dim // n_media
    aligned = each == LANES and width % LANES == 0 and n_far == n_keys
    far = lax.axis_index("far")
    near = lax.axis_index("near")
    key = lax.axis_index("keys")
    own_group = key // (n_keys // 2)
    scalars = jnp.stack([key, near, far, far, key * PAIR + near, own_group, jnp.full_like(far, dim)])
    scalars = scalars.astype(jnp.int32)

    def over_keys(value, shift):
        return lax.ppermute(value, "keys", [(i, i ^ shift) for i in range(n_keys)])

    def over_near(value):
        return lax.ppermute(value, "near", [(0, 1), (1, 0)])

    def over_far(value, shift):
        return lax.ppermute(value, "far", [(i, i ^ shift) for i in range(n_far)])

    def exchange_keys(slots):
        return [slots[0]] + [over_keys(slots[s], s) for s in range(1, n_keys)]

    def gather_keys(value):
        slots = [None] * n_keys
        for s in range(0, n_keys, 2):
            slots[s] = value if s == 0 else over_keys(value, s)
        for s in range(0, n_keys, 2):
            slots[s + 1] = over_keys(slots[s], 1)
        return slots

    def add(left, right):
        return (left.astype(f32) + right.astype(f32)).astype(bf16)

    lat = latents.reshape(rows, dim)
    cot = cotangent.reshape(rows, dim)
    row = lambda v: v.reshape(1, dim)
    packed = inner + LANES
    patch_block = pl.BlockSpec((1, key_rows, dim), lambda i, *_: (i, 0, 0))
    inner_block = pl.BlockSpec((1, key_rows, inner), lambda i, *_: (i, 0, 0))
    time_block = whole((n_frames, dim))
    stat_block = pl.BlockSpec((8, key_rows), lambda i, *_: (0, i))
    patch_flops = 4 * all_rows * dim * inner
    att_flops = 4 * media * n_keys * own * (key_rows + own) * inner * (GROUP // HEAD)

    def call(kernel, name, grid, in_specs, out_specs, out_shape, price, prefetch=1, **more):
        run = pl.pallas_call(
            kernel,
            name=name,
            grid_spec=pltpu.PrefetchScalarGridSpec(
                num_scalar_prefetch=prefetch,
                grid=grid,
                in_specs=in_specs,
                out_specs=out_specs,
                scratch_shapes=more.pop("scratch_shapes", ()),
            ),
            out_shape=out_shape,
            compiler_params=params(),
            cost_estimate=price,
            **more,
        )

        def pinned(*args):
            args = list(args)
            for i in range(prefetch, len(args)):
                if in_specs[i - prefetch].memory_space is None:
                    args[i] = pltpu.with_memory_space_constraint(args[i], pltpu.HBM)
            return run(*args)

        return pinned

    own_rows, q_own = call(
        latent_kernel,
        "latent_project",
        (1,),
        [whole((rows, dim)), whole((1, dim)), whole((1, dim)), whole((rows, dim)), whole((dim, inner))],
        [whole((rows, 2 * dim)), whole((rows, inner))],
        (struct((rows, 2 * dim), bf16), struct((rows, inner), bf16)),
        cost(2 * rows * dim * inner, 2 * dim * inner + 14 * rows * dim),
        prefetch=0,
    )(lat, row(latent_gain), row(latent_bias), cot, query_weight)
    q_all = exchange_keys([q_own] * n_keys)
    rows_all = lax.all_gather(own_rows, ("near", "keys"), axis=0, tiled=True)

    out = call(
        functools.partial(patch_kernel, n_keys, frames),
        "project_attend",
        (media,),
        [
            patch_block,
            time_block,
            whole((1, dim)),
            whole((1, dim)),
            whole((dim, inner)),
            whole((dim, inner)),
            whole((rows, dim)),
        ]
        + [whole((rows, inner))] * n_keys,
        [
            patch_block,
            inner_block,
            inner_block,
            whole((rows, inner)),
            whole((rows, inner)),
            stat_block,
            pl.BlockSpec((1, key_rows, LANES), lambda i, *_: (i, 0, 0)),
            whole((8, 2 * inner)),
        ]
        + [whole((rows, packed))] * n_keys,
        [
            struct(patches.shape, bf16),
            struct((media, key_rows, inner), bf16),
            struct((media, key_rows, inner), bf16),
            struct((rows, inner), bf16),
            struct((rows, inner), bf16),
            struct((8, all_rows), f32),
            struct((media, key_rows, LANES), bf16),
            struct((8, 2 * inner), f32),
        ]
        + [struct((rows, packed), bf16)] * n_keys,
        cost(patch_flops + att_flops, 12 * all_rows * dim),
        prefetch=2,
    )(
        scalars,
        frame_counts,
        patches,
        time_embedding,
        row(media_gain),
        row(media_bias),
        key_weight,
        value_weight,
        own_rows,
        *q_all,
    )
    media_low, kp, vp, kl, vl, norm_stat, once, norm_vec = out[:8]
    shares = out[8:]
    joined = exchange_keys(shares)

    chunk = min(1024, hidden)
    wo_rows = inner * dim // n_keys // dim
    wo_shape = (n_keys, wo_rows, dim) if aligned else (inner, dim)
    resampled, mid_grad, pack, ff_small, out_slots, ff_low = call(
        functools.partial(forward_kernel, n_keys, aligned),
        "feed_forward",
        (hidden // chunk,),
        [
            whole((rows, dim)),
            whole((rows, dim)),
            pl.BlockSpec((rows, dim), lambda i, *_: (0, 1)),
            whole((1, dim)),
            whole((1, dim)),
            whole((inner, dim)),
            pl.BlockSpec((dim, chunk), lambda i, *_: (0, i)),
            pl.BlockSpec((chunk, dim), lambda i, *_: (i, 0)),
        ]
        + [whole((rows, packed))] * n_keys,
        [
            whole((rows, dim)),
            whole((rows, dim)),
            whole((rows, packed)),
            whole((2, dim)),
            whole(wo_shape),
            whole((rows, dim)),
        ],
        (
            struct((rows, dim), f32),
            struct((rows, dim), f32),
            struct((rows, packed), bf16),
            struct((2, dim), f32),
            struct(wo_shape, bf16),
            struct((rows, dim), bf16),
        ),
        cost(8 * rows * dim * hidden, 4 * dim * hidden + 24 * rows * dim),
        scratch_shapes=[
            pltpu.VMEM((rows, dim), f32),
            pltpu.VMEM((rows, dim), f32),
            pltpu.VMEM((inner, dim) if aligned else (8, LANES), f32),
            pltpu.VMEM((rows, inner), f32),
            pltpu.VMEM((rows, inner), bf16),
            pltpu.VMEM((rows, dim), f32),
            pltpu.VMEM((rows, LANES), f32),
        ],
    )(
        scalars,
        lat,
        cot,
        own_rows,
        row(ff_gain),
        row(ff_bias),
        out_weight,
        up_weight,
        down_weight,
        *joined,
    )
    ff_low, rows_all = tie(ff_low, rows_all)
    ff_all = lax.all_gather(ff_low, ("near", "keys"), axis=0, tiled=True)
    if not aligned:
        c = dim // n_keys
        out_slots = out_slots.reshape(n_media, inner // n_media, n_keys, c // each, each)
        out_slots = out_slots.transpose(2, 3, 1, 0, 4).reshape(n_keys, wo_rows, dim)
        out_slots = jnp.stack(
            [lax.dynamic_index_in_dim(out_slots, key ^ s, 0, False) for s in range(n_keys)]
        )
    packs = gather_keys(pack)

    half_keys = n_keys // 2
    pick = lambda turn: (lambda s: s[5] ^ (1 - turn))
    high = 3 * width + wo_rows

    def regroup(value):
        value = jnp.moveaxis(value, 1, 2).reshape(-1, high, n_far, PAIR, each)
        value = value.transpose(0, 3, 1, 2, 4).reshape(-1, PAIR, high, n_far * each)
        return jnp.where(near == 0, value, value[:, ::-1])

    def attend_back(turn, packs, q_before, small_before):
        g = pick(turn)
        own_cols = pl.BlockSpec((rows, GROUP), lambda i, s, *_: (0, g(s)))
        stat_cols = pl.BlockSpec((rows, LANES), lambda i, *_: (0, inner // LANES))
        key_cols = pl.BlockSpec((1, key_rows, GROUP), lambda i, s, *_: (i, 0, g(s)))
        far_spec = pl.BlockSpec(memory_space=pl.ANY)
        q_width = GROUP if turn == 0 else inner
        chain = (n_keys // 4, PAIR, high, dim // PAIR)
        out = call(
            functools.partial(
                attend_back_kernel, n_keys, frames, turn, inner // HEAD, width, aligned
            ),
            "attend_back",
            (media,),
            [own_cols] * (2 * n_keys)
            + [stat_cols] * n_keys
            + [key_cols, key_cols, own_cols, own_cols]
            + [
                pl.BlockSpec((8, GROUP), lambda i, s, *_: (0, g(s))),
                pl.BlockSpec((8, GROUP), lambda i, s, *_: (0, inner // GROUP + g(s))),
                patch_block,
                pl.BlockSpec((1, key_rows, LANES), lambda i, *_: (i, 0, 0)),
                whole((8, all_rows)),
                pl.BlockSpec((rows, dim), lambda i, *_: (0, 0)),
                whole((1, dim)),
                whole((1, dim)),
            ]
            + [far_spec] * 4
            + [whole((rows, GROUP))] * len(q_before)
            + [whole((8, dim))] * len(small_before),
            [
                pl.BlockSpec((2, GROUP, key_rows), lambda i, *_: (0, 0, i)),
                whole((8, all_rows)),
                whole((rows, GROUP)),
                whole((rows, GROUP)),
                whole(chain),
                whole(chain),
                whole((8, dim)),
            ]
            + [whole((rows, q_width))] * n_keys,
            [
                struct((2, GROUP, all_rows), bf16),
                struct((8, all_rows), f32),
                struct((rows, GROUP), bf16),
                struct((rows, GROUP), bf16),
                struct(chain, bf16),
                struct(chain, bf16),
                struct((8, dim), f32),
            ]
            + [struct((rows, q_width), bf16)] * n_keys,
            cost(5 * att_flops // 4 + patch_flops // 2, 4 * all_rows * (inner + dim)),
            prefetch=2,
            scratch_shapes=[
                pltpu.VMEM((2 * GROUP + 16, dim), f32),
                pltpu.VMEM((2 * GROUP, LANES), f32),
                pltpu.VMEM((8, LANES), f32),
                pltpu.VMEM((n_keys * rows, GROUP), bf16),
                pltpu.VMEM((n_keys * rows, dim), bf16),
                pltpu.VMEM((GROUP // width, wo_rows, dim), bf16),
                pltpu.VMEM((dim, GROUP), bf16),
                pltpu.VMEM((dim, GROUP), bf16),
                pltpu.SemaphoreType.DMA((4,)),
            ],
        )(
            scalars,
            frame_counts,
            *q_all,
            *packs,
            *packs,
            kp,
            vp,
            kl,
            vl,
            norm_vec,
            norm_vec,
            media_low,
            once,
            norm_stat,
            own_rows,
            row(media_gain),
            row(media_bias),
            rows_all,
            out_slots,
            key_weight,
            value_weight,
            *q_before,
            *small_before,
        )
        chains = out[4:6] if aligned else [regroup(v) for v in out[4:6]]
        return out[:4], chains, out[6], out[7:]

    group_rows = PAIR * n_keys * rows
    (kv_a, stat_a, kl_a, vl_a), (given_a, kept_a), media_small, q_a = attend_back(0, packs, [], [])
    far_core = over_keys(given_a, 1)
    ff_all, kept_a = tie(ff_all, kept_a)

    units = hidden // (n_keys * PAIR)
    share = hidden // (n_media * n_keys)
    runs, per_run = (2, n_far // 2) if aligned else (1, 1)
    if aligned:
        own_up = [
            pl.BlockSpec(
                (dim, share),
                lambda i, s, n=n: (0, ((i * per_run + n) * PAIR + s[1]) * n_keys + s[0]),
            )
            for n in range(per_run)
        ]
        own_weights = [up_weight] * per_run
    else:
        shares = up_weight.reshape(dim, n_far, PAIR, n_keys, share)
        shares = lax.dynamic_index_in_dim(shares, key, 3, False)
        own_weights = [lax.dynamic_index_in_dim(shares, near, 2, False).reshape(dim, units)]
        own_up = [whole((dim, units))]
    ff_partial = call(
        functools.partial(ff_grad_kernel, n_keys, aligned),
        "feed_forward_weights",
        (runs,),
        [
            whole((group_rows, dim)),
            pl.BlockSpec((group_rows, dim), lambda i, s: (0, 1)),
            pl.BlockSpec((dim, units // runs), lambda i, s: (0, s[4] * runs + i)),
            pl.BlockSpec((units // runs, dim), lambda i, s: (s[4] * runs + i, 0)),
        ]
        + own_up,
        whole((2, units, dim)),
        struct((2, units, dim), bf16),
        cost(12 * group_rows * dim * units, 12 * dim * units + 4 * group_rows * dim),
    )(scalars, ff_all, rows_all, up_weight, down_weight, *own_weights)
    blocks = n_far // n_keys
    cols = dim // n_keys
    if not aligned:
        downs = ff_partial[1].reshape(n_far, share, n_keys, blocks, cols // blocks)
        downs = downs.transpose(2, 1, 3, 0, 4).reshape(n_keys, units // n_keys * dim)
        downs = jnp.stack(
            [lax.dynamic_index_in_dim(downs, key ^ s, 0, False) for s in range(n_keys)]
        )
        ups = ff_partial[0].reshape(units, n_far, PAIR, each)
        ups = jnp.where(near == 0, ups, ups[:, :, ::-1])
        ff_partial = jnp.stack([ups.reshape(units, dim), downs.reshape(units, dim)])
    ff_partial = ff_partial.reshape(2 * units, dim)
    far_core, ff_partial = tie(far_core, ff_partial)
    ff_sum = lax.psum_scatter(ff_partial, "far", scatter_dimension=1, tiled=True)
    far_sum = add(kept_a, far_core)
    far_sum, packs[0] = tie(far_sum, packs[0])
    far_near = over_near(far_sum[:, 1])
    (kv_b, stat_b, kl_b, vl_b), (given_b, kept_b), media_small, q_b = attend_back(
        1, packs, q_a, [media_small]
    )
    far_near, given_b, *q_b = tie(far_near, given_b, *q_b)
    far_half = add(far_sum[:, 0], far_near)

    col = lambda turn: pl.BlockSpec((dim, GROUP), lambda i, s: (0, s[5] ^ (1 - turn)))
    both = lambda value: [value, value]

    pieces = 3
    each_piece = media // pieces

    def patch_back(piece, gain, patches_grad):
        at = piece * each_piece
        block = pl.BlockSpec((1, key_rows, dim), lambda i, *_: (i + at, 0, 0))
        keys = pl.BlockSpec((2, GROUP, key_rows), lambda i, *_: (0, 0, i + at))
        stat = pl.BlockSpec((8, key_rows), lambda i, *_: (0, i + at))
        return call(
            functools.partial(patch_back_kernel, frames),
            "patch_back",
            (each_piece,),
            [
                keys,
                keys,
                stat,
                stat,
                stat,
                block,
                time_block,
                whole((1, dim)),
                col(0),
                col(0),
                col(1),
                col(1),
                pl.BlockSpec(memory_space=pl.ANY),
            ],
            block,
            struct(patches.shape, bf16),
            cost(patch_flops // pieces, 8 * all_rows * dim // pieces),
            **({} if piece == 0 else {"input_output_aliases": {13: 0}}),
        )(
            scalars,
            kv_a,
            kv_b,
            stat_a,
            stat_b,
            norm_stat,
            patches,
            time_embedding,
            gain,
            key_weight,
            value_weight,
            key_weight,
            value_weight,
            gain if piece == 0 else patches_grad,
        )

    def sum_far(value):
        return tree_sum([value] + [over_far(value, s) for s in range(1, n_far)])

    gain = row(media_gain)
    far_half, gain, given_b, *q_b = tie(far_half, gain, given_b, *q_b)
    far_got = [over_keys(far_half[j], half_keys + 2 * j) for j in range(n_keys // 4)]
    near_core = over_keys(given_b, 1)
    q_slots = exchange_keys(q_b)
    patches_grad = patch_back(0, gain, None)
    patches_grad, near_core, *q_slots = tie(patches_grad, near_core, *q_slots)
    near_sum = add(kept_b, near_core)
    near_sum, lat = tie(near_sum, lat)
    total = near_sum[0]
    for j in range(1, n_keys // 4):
        total = add(total, over_keys(near_sum[j], 2 * j))
    near_got = over_near(total[1])
    small_rows = -(-(n_frames + 6) // 8) * 8
    latents_grad, small = call(
        functools.partial(latent_back_kernel, n_keys, frames, n_frames),
        "latent_back",
        (1,),
        [whole((rows, dim)), whole((1, dim)), whole((rows, dim)), whole((8, dim)), whole((2, dim))]
        + [whole((rows, GROUP)), col(0), whole((rows, GROUP)), col(0)]
        + [whole((rows, GROUP)), col(1), whole((rows, GROUP)), col(1)]
        + [whole((dim, inner))]
        + [whole((rows, inner))] * n_keys,
        [whole((rows, dim)), whole((small_rows, dim))],
        (struct((rows, dim), f32), struct((small_rows, dim), f32)),
        cost(6 * rows * dim * inner, 6 * dim * inner + 20 * rows * dim),
    )(
        scalars,
        lat,
        row(latent_gain),
        mid_grad,
        media_small,
        ff_small,
        kl_a,
        key_weight,
        vl_a,
        value_weight,
        kl_b,
        key_weight,
        vl_b,
        value_weight,
        query_weight,
        *q_slots,
    )

    gain, small = tie(gain, small)
    small = tree_sum([small] + [over_keys(small, s) for s in range(1, n_keys)])
    patches_grad = patch_back(1, gain, patches_grad)
    patches_grad, small, near_got, *far_got = tie(patches_grad, small, near_got, *far_got)
    total = total[0]
    for value in far_got:
        total = add(total, value)
    total = add(total, near_got)
    total, small, gain, ff_sum = tie(total, small, gain, ff_sum)
    parts = lax.all_to_all(total, "far", split_axis=1, concat_axis=0, tiled=True)
    small = small + over_near(small)
    up_keep = ff_sum[:units, :each]
    up_got = over_near(ff_sum[:units, each:])
    downs = ff_sum[units:].reshape(n_keys, share, cols)
    downs = exchange_keys([downs[s] for s in range(n_keys)])
    patches_grad = patch_back(2, gain, patches_grad)
    patches_grad, small, up_got, parts, *downs = tie(patches_grad, small, up_got, parts, *downs)
    small = sum_far(small)
    if aligned:
        q_grad, k_grad, v_grad, out_grad, up_grad, down_grad = call(
            functools.partial(finish_kernel, n_keys, width),
            "finish_weights",
            (1,),
            [whole((units, each))] * 2
            + [whole((share, cols))] * n_keys
            + [whole(parts.shape)],
            [whole((each, width))] * 3
            + [
                whole((inner // n_media, dim // n_keys)),
                whole((each, PAIR * units)),
                whole((units, dim // n_keys)),
            ],
            [struct((each, width), f32)] * 3
            + [
                struct((inner // n_media, dim // n_keys), f32),
                struct((each, PAIR * units), f32),
                struct((units, dim // n_keys), f32),
            ],
            cost(0, 16 * width * each + 12 * units * each),
        )(scalars, up_keep, up_got, *downs, parts)
    else:
        total = jnp.sum(parts.reshape(n_far, -1, each).astype(f32), 0)
        q_grad, k_grad, v_grad = (total[i * width : (i + 1) * width].T for i in range(3))
        out_grad = total[3 * width :].reshape(-1, inner // n_media, each)
        out_grad = out_grad.transpose(1, 0, 2).reshape(inner // n_media, dim // n_keys)
        up_grad = jnp.where(
            near == 0,
            jnp.concatenate([up_keep, up_got], 0),
            jnp.concatenate([up_got, up_keep], 0),
        ).T.astype(f32)
        down_grad = jnp.zeros((units // blocks, cols), f32)
        for s in range(n_keys):
            down_grad = lax.dynamic_update_slice_in_dim(
                down_grad, downs[s].astype(f32), (key ^ s) * share, 0
            )

    return (
        resampled.reshape(latents.shape),
        patches_grad,
        latents_grad.reshape(latents.shape),
        small[:n_frames],
        small[n_frames],
        small[n_frames + 1],
        small[n_frames + 2],
        small[n_frames + 3],
        small[n_frames + 4],
        small[n_frames + 5],
        q_grad,
        k_grad,
        v_grad,
        out_grad,
        up_grad,
        down_grad,
    )


def solution(mesh):
    n_media, n_keys = mesh.shape["media"], mesh.shape["keys"]
    n_far = n_media // PAIR
    fine = Mesh(mesh.devices.reshape(n_far, PAIR, n_keys), ("far", "near", "keys"))
    split = P(("far", "near"), "keys", None)
    return jax.shard_map(
        functools.partial(shards, n_far, n_keys),
        mesh=fine,
        in_specs=(split, split, P(("far", "near"))) + (P(),) * 13 + (split,),
        out_specs=(split,) * 3 + (P(),) * 7 + (P(("far", "near"), "keys"),) * 6,
        check_vma=False,
    )
```

```python
import functools

import jax
import jax.numpy as jnp
from jax import lax
from jax.experimental import pallas as pl
from jax.experimental.pallas import tpu as pltpu
from jax.sharding import Mesh, PartitionSpec as P

HEAD = 64
PATCH = 256
GROUP = 256
LANES = 128

VMEM_LIMIT = 44 << 20

EPS = 1e-05
NEG = -1e30
SIDE = 2
PAIR = 2

f32 = jnp.float32
bf16 = jnp.bfloat16


def mul(left, right, contract=((1,), (0,)), precision=None):
    return lax.dot_general(
        left, right, (contract, ((), ())), precision=precision, preferred_element_type=f32
    )


NN = ((1,), (0,))
NT = ((1,), (1,))
TN = ((0,), (0,))


def norm_parts(values):
    centre = jnp.mean(values, -1, keepdims=True)
    shifted = values - centre
    spread = jnp.mean(shifted * shifted, -1, keepdims=True)
    return centre, lax.rsqrt(spread + EPS), shifted


def norm(values, gain, bias):
    _, scale, shifted = norm_parts(values)
    return shifted * scale * gain + bias


def norm_back(values, gain, grad):
    _, scale, shifted = norm_parts(values)
    unit = shifted * scale
    scaled = grad * gain
    first = jnp.mean(scaled, -1, keepdims=True)
    second = jnp.mean(scaled * unit, -1, keepdims=True)
    back = scale * (scaled - first - unit * second)
    return (
        back,
        jnp.sum(grad * unit, 0, keepdims=True),
        jnp.sum(grad, 0, keepdims=True),
    )


def gelu_parts(hidden):
    cdf = 0.5 * (1.0 + lax.erf(hidden * (2.0**-0.5)))
    pdf = jnp.exp(-0.5 * hidden * hidden) * 0.3989422804014327
    return cdf, cdf + hidden * pdf


def head_mask(rows, width, heads):
    row = lax.broadcasted_iota(jnp.int32, (heads * rows, width), 0) // rows
    col = lax.broadcasted_iota(jnp.int32, (heads * rows, width), 1)
    return row, col


def spread_heads(values):
    heads = values.shape[1] // HEAD
    row, col = head_mask(values.shape[0], values.shape[1], heads)
    return jnp.where(row == col // HEAD, jnp.concatenate([values] * heads, 0), jnp.zeros((), values.dtype))


def fold_heads(values):
    heads = values.shape[1] // HEAD
    rows = values.shape[0] // heads
    row, col = head_mask(rows, values.shape[1], heads)
    kept = jnp.where(row == col // HEAD, values, 0.0)
    total = kept[:rows]
    for h in range(1, heads):
        total = total + kept[h * rows : (h + 1) * rows]
    return total


def three_parts(values, lane, start, slots):
    high = values.astype(bf16).astype(f32)
    rest = values - high
    middle = rest.astype(bf16).astype(f32)
    low = rest - middle
    place = lane // slots - start
    return jnp.where(place == 0, high, jnp.where(place == 1, middle, jnp.where(place == 2, low, 0.0)))


def cost(flops, moved, special=0):
    return pl.CostEstimate(flops=int(flops), bytes_accessed=int(moved), transcendentals=int(special))


def params():
    return pltpu.CompilerParams(vmem_limit_bytes=VMEM_LIMIT)


def tie(*values):
    return lax.optimization_barrier(values)


def latent_kernel(lat, gain, bias, cot, wq, rows_o, q_o):
    dim = lat.shape[1]
    low = norm(lat[...], gain[...], bias[...]).astype(bf16)
    rows_o[:, :dim] = low
    rows_o[:, dim:] = cot[...].astype(bf16)
    q_o[...] = mul(low, wq[...]).astype(bf16)


def two_parts(values):
    high = values.astype(bf16)
    return high, (values - high.astype(f32)).astype(bf16)


def masked_scores(query, keys, frames, first, count):
    scores = mul(query, keys, NT)
    parts = []
    for f in range(frames):
        part = scores[:, f * PATCH : (f + 1) * PATCH]
        parts.append(jnp.where(first + f < count, part, NEG))
    return jnp.concatenate(parts + [scores[:, frames * PATCH :]], 1)


def patch_kernel(n_keys, frames, scalars, counts, patches, time, gain, bias, wk, wv, lat_low, *refs):
    q = refs[:n_keys]
    low_o, k_o, v_o, kl_o, vl_o, stat_o, once_o, vec_o = refs[n_keys : n_keys + 8]
    outs = refs[n_keys + 8 :]
    step = pl.program_id(0)

    @pl.when(step == 0)
    def _():
        kl_o[...] = mul(lat_low[...], wk[...]).astype(bf16)
        vl_o[...] = mul(lat_low[...], wv[...]).astype(bf16)
        row = lax.broadcasted_iota(jnp.int32, (16, gain.shape[1]), 0)
        both = jnp.where(row % 2 == 0, gain[...], bias[...])
        high, low = two_parts(both)
        both = jnp.where(row < 2, high.astype(f32), jnp.where(row < 4, low.astype(f32), 0.0)).astype(bf16)
        for i, w in enumerate((wk, wv)):
            term = mul(both, w[...])
            vec_o[:, i * w.shape[1] : (i + 1) * w.shape[1]] = term[:8] + pltpu.roll(term, 14, 0)[:8]

    for f in range(frames):
        rows = pl.ds(f * PATCH, PATCH)
        framed = patches[0, rows, :].astype(f32) + time[pl.ds(scalars[0] * frames + f, 1), :]
        centre, scale, shifted = norm_parts(framed)
        low = (shifted * scale * gain[...] + bias[...]).astype(bf16)
        low_o[0, rows, :] = low
        k_o[0, rows, :] = mul(low, wk[...]).astype(bf16)
        v_o[0, rows, :] = mul(low, wv[...]).astype(bf16)
        lane = lax.broadcasted_iota(jnp.int32, (PATCH, LANES), 1)
        stat = jnp.where(lane == 0, centre, jnp.where(lane == 1, scale, 0.0))
        stat_o[:, f * PATCH : (f + 1) * PATCH] = stat.T[:8]
        high = scale.astype(bf16).astype(f32)
        once = jnp.where(lane == 0, 1.0, jnp.where(lane == 1 + f, high, 0.0))
        once_o[0, rows, :] = jnp.where(lane == 1 + frames + f, scale - high, once).astype(bf16)

    own = q[0].shape[0] // pl.num_programs(0)
    inner = q[0].shape[1]
    heads = inner // HEAD
    count = counts[step]
    first = scalars[0] * frames
    here = pl.ds(pl.multiple_of(step * own, own), own)
    query = jnp.concatenate([r[here, :] for r in q], 0)
    rows = query.shape[0]
    stats = jnp.zeros((rows, LANES), f32)
    shares = []
    for g in range(inner // GROUP):
        cols = slice(g * GROUP, (g + 1) * GROUP)
        wide = spread_heads(query[:, cols] * bf16(HEAD**-0.5))
        keys = jnp.concatenate([k_o[0, :, cols], kl_o[here, cols]], 0)
        values = jnp.concatenate([v_o[0, :, cols], vl_o[here, cols]], 0)
        scores = masked_scores(wide, keys, frames, first, count)
        top = jnp.max(scores, -1, keepdims=True)
        raw = jnp.exp(scores - top)
        total = jnp.sum(raw, -1, keepdims=True)
        share = mul(raw.astype(bf16), values) * (1.0 / total)
        shares.append(fold_heads(share).astype(bf16))
        level = top + jnp.log(total)
        row, lane = head_mask(rows, LANES, GROUP // HEAD)
        kept = jnp.where(lane % heads == row + g * (GROUP // HEAD), level, 0.0)
        for h in range(GROUP // HEAD):
            stats = stats + kept[h * rows : (h + 1) * rows]
    lane = lax.broadcasted_iota(jnp.int32, stats.shape, 1)
    packed = jnp.concatenate(shares + [three_parts(stats, lane, 0, heads).astype(bf16)], 1)
    for s in range(n_keys):
        outs[s][here, :] = packed[s * own : (s + 1) * own]


def sum_runs(stats, heads, start):
    total = None
    for part in range(3):
        shift = (-(start + part) * heads) % LANES
        term = pltpu.roll(stats, shift, 1) if shift else stats
        total = term if total is None else total + term
    return total


def join(latents, gain, bias, wo, slots, att_o, low_o, mid_o, ff_o, lse_o):
    inner = att_o.shape[1]
    heads = inner // HEAD
    levels = [sum_runs(r[:, inner:].astype(f32), heads, 0) for r in slots]
    top = functools.reduce(jnp.maximum, levels)
    weights = [jnp.exp(v - top) for v in levels]
    total = functools.reduce(jnp.add, weights)
    inverse = 1.0 / total
    lane = lax.broadcasted_iota(jnp.int32, (LANES, inner), 0)
    col = lax.broadcasted_iota(jnp.int32, (LANES, inner), 1)
    select = jnp.where(lane == col // HEAD, 1.0, 0.0)
    attended = None
    for s in range(len(slots)):
        wide = mul(weights[s] * inverse, select, NN, lax.Precision.HIGHEST)
        term = wide * slots[s][:, :inner].astype(f32)
        attended = term if attended is None else attended + term
    low = attended.astype(bf16)
    middle = latents[...] + mul(low, wo[...])
    att_o[...] = attended
    low_o[...] = low
    mid_o[...] = middle
    ff_o[...] = norm(middle, gain[...], bias[...]).astype(bf16)
    lse_o[...] = top + jnp.log(total)


def forward_kernel(
    n_keys,
    aligned,
    scalars,
    latents,
    cot,
    out_low,
    gain,
    bias,
    wo,
    up,
    down,
    *refs,
):
    slots = refs[:n_keys]
    res_o, mid_grad_o, pack_o, small_o, wo_grad_o, ff_low = refs[n_keys : n_keys + 6]
    res_acc, in_acc, wo_acc, attended, att_low, middle, lse = refs[n_keys + 6 :]
    step = pl.program_id(0)

    @pl.when(step == 0)
    def _():
        res_acc[...] = jnp.zeros_like(res_acc)
        in_acc[...] = jnp.zeros_like(in_acc)
        join(latents, gain, bias, wo, slots, attended, att_low, middle, ff_low, lse)

    hidden = mul(ff_low[...], up[...])
    act_grad = mul(out_low[...], down[...], NT)
    cdf, slope = gelu_parts(hidden)
    res_acc[...] += mul((hidden * cdf).astype(bf16), down[...])
    in_acc[...] += mul((act_grad * slope).astype(bf16), up[...], NT)

    @pl.when(step == pl.num_programs(0) - 1)
    def _():
        inner = attended.shape[1]
        heads = inner // HEAD
        res_o[...] = middle[...] + res_acc[...]
        back, gain_grad, bias_grad = norm_back(middle[...], gain[...], in_acc[...])
        small_o[0:1, :] = gain_grad
        small_o[1:2, :] = bias_grad
        mid_grad = cot[...] + back
        mid_grad_o[...] = mid_grad
        branch = mid_grad.astype(bf16)
        att_grad = mul(branch, wo[...], NT).astype(bf16)
        col = lax.broadcasted_iota(jnp.int32, (inner, LANES), 0)
        lane = lax.broadcasted_iota(jnp.int32, (inner, LANES), 1)
        select = jnp.where(col // HEAD == lane % heads, 1.0, 0.0)
        delta = mul(attended[...] * att_grad.astype(f32), select, NN, lax.Precision.HIGHEST)
        lane = lax.broadcasted_iota(jnp.int32, delta.shape, 1)
        level = jnp.where(lane < heads, lse[...], 0.0)
        level = level + pltpu.roll(level, heads, 1) + pltpu.roll(level, 2 * heads, 1)
        stats = three_parts(level, lane, 0, heads) + three_parts(delta, lane, 3, heads)
        pack_o[...] = jnp.concatenate([att_grad, stats.astype(bf16)], 1)
        wo_grad = mul(att_low[...], branch, TN)
        if aligned:
            wo_acc[...] = wo_grad
            slot_rows(scalars, wo_acc, wo_grad_o, n_keys)
        else:
            wo_grad_o[...] = wo_grad.astype(bf16)


def slot_rows(scalars, full, out, n_keys):
    lanes = LANES
    n_media = out.shape[2] // lanes
    r = full.shape[0] // n_media
    c = full.shape[1] // n_keys
    for s in range(n_keys):
        owner = (scalars[0] ^ s) * c
        for m in range(n_media):
            place = slice(m * lanes, (m + 1) * lanes)
            for h in range(c // lanes):
                start = pl.multiple_of(owner + h * lanes, lanes)
                out[s, h * r : (h + 1) * r, place] = full[
                    m * r : (m + 1) * r, pl.ds(start, lanes)
                ].astype(bf16)


def ff_grad_kernel(n_keys, aligned, scalars, ff_all, out_all, up, down, *refs):
    own_ups, grad_o = refs[:-1], refs[-1]
    units, dim = down.shape
    step = pl.program_id(0)
    hidden = mul(ff_all[...], up[...])
    act_grad = mul(out_all[...], down[...], NT)
    _, slope = gelu_parts(hidden)
    up_grad = mul((act_grad * slope).astype(bf16), ff_all[...], TN).astype(bf16)
    rows = pl.ds(pl.multiple_of(step * units, 8), units)
    if not aligned:
        grad_o[0] = up_grad
        hidden = mul(ff_all[...], own_ups[0][...])
        cdf, _ = gelu_parts(hidden)
        grad_o[1] = mul((hidden * cdf).astype(bf16), out_all[...], TN).astype(bf16)
        return
    for j in range(dim // LANES):
        place = ((j // PAIR) * PAIR + (scalars[1] ^ (j % PAIR))) * LANES
        grad_o[0, rows, pl.ds(pl.multiple_of(place, LANES), LANES)] = up_grad[
            :, j * LANES : (j + 1) * LANES
        ]
    each = own_ups[0].shape[1]
    cols = dim // n_keys
    hidden = mul(ff_all[...], jnp.concatenate([r[...] for r in own_ups], 1))
    cdf, _ = gelu_parts(hidden)
    down_grad = mul((hidden * cdf).astype(bf16), out_all[...], TN).astype(bf16)
    for n in range(len(own_ups)):
        lanes = pl.ds(pl.multiple_of((step * len(own_ups) + n) * cols, LANES), cols)
        for k in range(n_keys):
            place = pl.ds(pl.multiple_of((scalars[0] ^ k) * each, each), each)
            grad_o[1, place, lanes] = down_grad[
                n * each : (n + 1) * each, k * cols : (k + 1) * cols
            ]


def attend_back_kernel(n_keys, frames, turn, heads, width, aligned, scalars, counts, *refs):
    refs = list(refs)
    take = lambda n: [refs.pop(0) for _ in range(n)]
    q, grads, stat = take(n_keys), take(n_keys), take(n_keys)
    kp, vp, kl, vl, k_vec, v_vec, low, once, norm_stat, lat_own, gain, bias = take(12)
    rows_far, wo_far, wk_far, wv_far = take(4)
    q_before = take(n_keys if turn else 0)
    small_before = take(turn)
    kv_t_o, stat_o, kl_o, vl_o, given, kept, small = take(7)
    q_o = take(n_keys)
    grad_acc, sums, scalar_sums, q_acc, rows_all, wo_g, wk, wv, sems = refs
    n = kp.shape[0]
    each = range(n)
    rows = kl_o.shape[0]
    own = rows // (pl.num_programs(0) * n)
    dim = low.shape[2]
    per = GROUP // HEAD
    step = pl.program_id(0)
    first_frame = scalars[0] * frames
    group = scalars[5] ^ (1 - turn)
    owners = GROUP // width
    group_cols = pl.ds(pl.multiple_of(group * GROUP, GROUP), GROUP)
    near_rows = pl.ds(pl.multiple_of(scalars[1] * n_keys * rows, 8), n_keys * rows)
    fetches = [
        pltpu.make_async_copy(rows_far.at[near_rows, pl.ds(0, dim)], rows_all, sems.at[0]),
        pltpu.make_async_copy(wo_far.at[pl.ds(owners * (1 - turn), owners)], wo_g, sems.at[1]),
        pltpu.make_async_copy(wk_far.at[:, group_cols], wk, sems.at[2]),
        pltpu.make_async_copy(wv_far.at[:, group_cols], wv, sems.at[3]),
    ]

    @pl.when(step == 0)
    def _():
        for fetch in fetches:
            fetch.start()
        grad_acc[...] = jnp.zeros_like(grad_acc)
        sums[...] = jnp.zeros_like(sums)
        scalar_sums[...] = jnp.zeros_like(scalar_sums)

    here = [pl.ds(pl.multiple_of((step * n + m) * own, own), own) for m in each]
    n_patch = kp.shape[1]
    n_query = n_keys * own
    row, lane = head_mask(n_query, LANES, per)
    mine = lane % heads == row + group * per
    levels = mine & (lane < 3 * heads)
    deltas = mine & (lane >= 3 * heads) & (lane < 6 * heads)
    wide, wide_grad, keys, values, level, delta = [], [], [], [], [], []
    for m in each:
        wide.append(
            spread_heads(jnp.concatenate([r[here[m], :] for r in q], 0) * bf16(HEAD**-0.5))
        )
        wide_grad.append(spread_heads(jnp.concatenate([r[here[m], :] for r in grads], 0)))
        keys.append(jnp.concatenate([kp[m], kl[here[m], :]], 0))
        values.append(jnp.concatenate([vp[m], vl[here[m], :]], 0))
    scores = [
        masked_scores(wide[m], keys[m], frames, first_frame, counts[step * n + m]) for m in each
    ]
    prob_grad = [mul(wide_grad[m], values[m], NT) for m in each]
    for m in each:
        stats = jnp.concatenate([r[here[m], :] for r in stat], 0).astype(f32)
        tiled = jnp.concatenate([stats] * per, 0)
        level.append(jnp.sum(jnp.where(levels, tiled, 0.0), -1, keepdims=True))
        delta.append(jnp.sum(jnp.where(deltas, tiled, 0.0), -1, keepdims=True))
    probs = [jnp.exp(scores[m] - level[m]) for m in each]
    score_grad = [probs[m] * (prob_grad[m] - delta[m]) for m in each]
    along = [
        jnp.sum(score_grad[m] * scores[m] + probs[m] * prob_grad[m], 0, keepdims=True) for m in each
    ]
    score_grad = [v.astype(bf16) for v in score_grad]
    probs = [v.astype(bf16) for v in probs]
    beside = lambda value, vec: jnp.concatenate(
        [value, mul(value, vec[...].astype(bf16), NT).astype(bf16)], 1
    )
    key_side = [beside(v, k_vec) for v in wide]
    value_side = [beside(v, v_vec) for v in wide_grad]
    key_t = [mul(key_side[m], score_grad[m], TN) for m in each]
    value_t = [mul(value_side[m], probs[m], TN) for m in each]
    query_grad = [mul(score_grad[m], keys[m]) for m in each]
    frame = lax.broadcasted_iota(jnp.int32, (16, n_patch), 1) // PATCH
    row16 = lax.broadcasted_iota(jnp.int32, (16, n_patch), 0)
    same = frame == row16 % frames
    sides, kvs = [], []
    line8 = lax.broadcasted_iota(jnp.int32, scalar_sums.shape, 0)
    adds = jnp.zeros(scalar_sums.shape, f32)
    for m in each:
        kl_o[here[m], :] = key_t[m][:GROUP, n_patch:].T.astype(bf16)
        vl_o[here[m], :] = value_t[m][:GROUP, n_patch:].T.astype(bf16)
        kv = jnp.concatenate([key_t[m][:GROUP, :n_patch], value_t[m][:GROUP, :n_patch]], 0)
        kv = kv.astype(bf16)
        kv_t_o[0, :, m * n_patch : (m + 1) * n_patch] = kv[:GROUP]
        kv_t_o[1, :, m * n_patch : (m + 1) * n_patch] = kv[GROUP:]
        ends = key_t[m][GROUP:, :n_patch] + value_t[m][GROUP:, :n_patch]
        line = lax.broadcasted_iota(jnp.int32, ends.shape, 0)
        stat_rows = jnp.where(line == 1, along[m][:, :n_patch] - ends, ends)
        span = pl.ds(pl.multiple_of((step * n + m) * n_patch, n_patch), n_patch)
        stat_o[:, span] = stat_rows
        scale = norm_stat[1:2, span] * (1.0 / dim)
        first = stat_rows[0:1, :] * scale
        second = stat_rows[1:2, :] * scale
        high = second.astype(bf16).astype(f32)
        ends = jnp.where(same & (row16 < frames), high, 0.0)
        ends = jnp.where(same & (row16 >= frames) & (row16 < 2 * frames), second - high, ends)
        kvs.append(kv)
        sides.append(jnp.concatenate([kv, ends.astype(bf16)], 0))
        for f in range(frames):
            cut = slice(f * PATCH, (f + 1) * PATCH)
            one = jnp.sum(first[:, cut], -1, keepdims=True)
            two = jnp.sum(second[:, cut], -1, keepdims=True)
            adds = adds + jnp.where(line8 == f, one, jnp.where(line8 == frames + f, two, 0.0))
    scalar_sums[...] += adds
    grad_acc[...] += mul(jnp.concatenate(sides, 1), low[...].reshape(n * n_patch, dim))
    sums[...] += mul(jnp.concatenate(kvs, 1), once[...].reshape(n * n_patch, LANES))

    for m in each:
        part = (fold_heads(query_grad[m]) * HEAD**-0.5).astype(bf16)
        for s in range(n_keys):
            piece = part[s * own : (s + 1) * own]
            place = pl.multiple_of((scalars[0] ^ s) * rows + (step * n + m) * own, own)
            q_acc[pl.ds(place, own), :] = piece
            if turn == 0:
                q_o[s][here[m], :] = piece
            else:
                other = pl.ds(pl.multiple_of((1 - group) * GROUP, GROUP), GROUP)
                q_o[s][here[m], group_cols] = piece
                q_o[s][here[m], other] = q_before[s][here[m], :]

    @pl.when(step == pl.num_programs(0) - 1)
    def _():
        for fetch in fetches:
            fetch.wait()
        behind = None
        for part in two_parts(sums[...]):
            for i, w in enumerate((wk, wv)):
                term = mul(part[i * GROUP : (i + 1) * GROUP], w[...], ((0,), (1,)))
                behind = term if behind is None else behind + term
        bias_grad = behind[0:1]
        main = grad_acc[: 2 * GROUP, :]
        ends = grad_acc[2 * GROUP :, :]
        total = jnp.sum(main[:GROUP] * wk[...].astype(f32).T, 0, keepdims=True)
        total = total + jnp.sum(main[GROUP:] * wv[...].astype(f32).T, 0, keepdims=True)
        over = 1.0 / gain[...]
        lines = []
        for f in range(frames):
            along = ends[f : f + 1] + ends[frames + f : frames + f + 1]
            scaled = behind[1 + f : 2 + f] + behind[1 + frames + f : 2 + frames + f]
            second_sum = scalar_sums[frames + f : frames + f + 1, 0:1]
            lines.append(
                gain[...] * scaled
                - scalar_sums[f : f + 1, 0:1]
                - (along - bias[...] * second_sum) * over
            )
        lines += [(total - bias[...] * bias_grad) * over, bias_grad]
        for i, value in enumerate(lines):
            small[i : i + 1, :] = value + small_before[0][i : i + 1, :] if turn else value
        kv_lat = jnp.concatenate([kl_o[...], vl_o[...]], 1)
        grad_acc[: 2 * GROUP, :] = main + mul(kv_lat, lat_own[...], TN)
        q_grad = mul(q_acc[...], rows_all[...], TN)
        sums_q = q_grad.astype(bf16)
        near = scalars[1] if aligned else 0
        runs = dim // PAIR // LANES
        for j in range(owners):
            out = (given, kept)[j % 2]
            slot = 2 * (j // 2) + 1 - j % 2
            start = ((scalars[0] ^ slot) % owners) * width
            for part in range(3):
                at = pl.multiple_of((part - 1) * GROUP + start, width)
                if part == 0:
                    piece = jnp.zeros((width, dim), bf16)
                    for o in range(owners):
                        same = start == o * width
                        piece = jnp.where(same, sums_q[o * width : (o + 1) * width], piece)
                else:
                    piece = grad_acc[pl.ds(at, width), :].astype(bf16)
                place_rows(out, scalars, j // 2, part * width, piece, aligned)
            place_rows(out, scalars, j // 2, 3 * width, wo_g[slot], aligned)


def place_rows(out, scalars, slot, start, piece, aligned):
    rows = slice(start, start + piece.shape[0])
    half = piece.shape[1] // PAIR
    if aligned:
        for m in range(piece.shape[1] // LANES):
            place = slice((m // PAIR) * LANES, (m // PAIR + 1) * LANES)
            out[slot, scalars[1] ^ (m % PAIR), rows, place] = piece[:, m * LANES : (m + 1) * LANES]
    else:
        for n in range(PAIR):
            out[slot, n, rows, :] = piece[:, n * half : (n + 1) * half]


def patch_back_kernel(
    frames, scalars, kv_a, kv_b, stat_a, stat_b, norm_stat, patches, time, gain, wk_a, wv_a, wk_b, wv_b, _, grad_o
):
    turned = ((0,), (1,))
    inverse = 1.0 / gain.shape[1]
    for f in range(frames):
        rows = pl.ds(f * PATCH, PATCH)
        span = slice(f * PATCH, (f + 1) * PATCH)
        scale = norm_stat[1:2, span]
        first = (stat_a[0:1, span] + stat_b[0:1, span]) * inverse
        second = (stat_a[1:2, span] + stat_b[1:2, span]) * inverse
        slope = scale * scale * second
        level = scale * first - norm_stat[0:1, span] * slope
        line = lax.broadcasted_iota(jnp.int32, (8, PATCH), 0)
        columns = jnp.where(line == 0, scale, jnp.where(line == 1, level, slope)).T
        grad = mul(kv_a[0, :, span], wk_a[...], turned)
        grad = grad + mul(kv_a[1, :, span], wv_a[...], turned)
        grad = grad + mul(kv_b[0, :, span], wk_b[...], turned)
        grad = grad + mul(kv_b[1, :, span], wv_b[...], turned)
        framed = patches[0, rows, :].astype(f32) + time[pl.ds(scalars[0] * frames + f, 1), :]
        back = grad * gain[...] * columns[:, 0:1] - columns[:, 1:2] - framed * columns[:, 2:3]
        grad_o[0, rows, :] = back.astype(bf16)


def latent_back_kernel(n_keys, frames, n_frames, scalars, latents, gain, mid_grad, media_small, ff_small, *refs):
    keys = refs[:8]
    wq = refs[8]
    slots = refs[9 : 9 + n_keys]
    lat_o, small_o = refs[9 + n_keys :]
    query = functools.reduce(jnp.add, [r[...].astype(f32) for r in slots]).astype(bf16)
    grad = mul(query, wq[...], NT)
    for i in range(4):
        grad = grad + mul(keys[2 * i][...], keys[2 * i + 1][...], NT)
    back, gain_grad, bias_grad = norm_back(latents[...], gain[...], grad)
    lat_o[...] = mid_grad[...] + back
    small_o[...] = jnp.zeros_like(small_o)
    for f in range(frames):
        small_o[pl.ds(scalars[0] * frames + f, 1), :] = media_small[f : f + 1, :]
    for i, line in enumerate(
        (media_small[frames : frames + 1, :], media_small[frames + 1 : frames + 2, :], gain_grad, bias_grad)
    ):
        small_o[n_frames + i : n_frames + i + 1, :] = line
    small_o[n_frames + 4 : n_frames + 6, :] = ff_small[...]


def finish_kernel(n_keys, width, scalars, up_keep, up_got, *refs):
    downs, parts = refs[:n_keys], refs[n_keys]
    q_o, k_o, v_o, out_o, up_o, down_o = refs[-6:]
    high = 3 * width + out_o.shape[0] * out_o.shape[1] // LANES
    total = parts[:high].astype(f32)
    for s in range(1, parts.shape[0] // high):
        total = total + parts[s * high : (s + 1) * high].astype(f32)
    for i, ref in enumerate((q_o, k_o, v_o)):
        ref[...] = total[i * width : (i + 1) * width].T
    r = out_o.shape[0]
    for h in range(out_o.shape[1] // LANES):
        out_o[:, h * LANES : (h + 1) * LANES] = total[3 * width + h * r : 3 * width + (h + 1) * r]
    units = up_keep.shape[0]
    near = scalars[1]
    own = pl.ds(pl.multiple_of(near * units, LANES), units)
    other = pl.ds(pl.multiple_of((1 - near) * units, LANES), units)
    up_o[:, own] = up_keep[...].astype(f32).T
    up_o[:, other] = up_got[...].astype(f32).T
    share = downs[0].shape[0]
    for s, ref in enumerate(downs):
        down_o[pl.ds(pl.multiple_of((scalars[0] ^ s) * share, share), share), :] = ref[...].astype(f32)


def whole(shape):
    return pl.BlockSpec(shape, lambda *_: (0,) * len(shape))


def struct(shape, dtype):
    return pltpu.HBM(shape, dtype)


def tree_sum(parts):
    while len(parts) > 1:
        parts = [parts[i] + parts[i + 1] for i in range(0, len(parts), 2)]
    return parts[0]


def shards(
    n_far,
    n_keys,
    latents,
    patches,
    frame_counts,
    time_embedding,
    media_gain,
    media_bias,
    latent_gain,
    latent_bias,
    ff_gain,
    ff_bias,
    query_weight,
    key_weight,
    value_weight,
    out_weight,
    up_weight,
    down_weight,
    cotangent,
):
    media, own, dim = latents.shape
    key_rows = patches.shape[1]
    inner = query_weight.shape[1]
    hidden = up_weight.shape[1]
    frames = key_rows // PATCH
    n_frames = time_embedding.shape[0]
    n_media = n_far * PAIR
    rows = media * own
    all_rows = media * key_rows
    width = inner // n_keys
    each = dim // n_media
    aligned = each == LANES and width % LANES == 0 and n_far == n_keys
    far = lax.axis_index("far")
    near = lax.axis_index("near")
    key = lax.axis_index("keys")
    own_group = key // (n_keys // 2)
    scalars = jnp.stack([key, near, far, far, key * PAIR + near, own_group, jnp.full_like(far, dim)])
    scalars = scalars.astype(jnp.int32)

    def over_keys(value, shift):
        return lax.ppermute(value, "keys", [(i, i ^ shift) for i in range(n_keys)])

    def over_near(value):
        return lax.ppermute(value, "near", [(0, 1), (1, 0)])

    def over_far(value, shift):
        return lax.ppermute(value, "far", [(i, i ^ shift) for i in range(n_far)])

    def exchange_keys(slots):
        return [slots[0]] + [over_keys(slots[s], s) for s in range(1, n_keys)]

    def gather_keys(value):
        slots = [None] * n_keys
        for s in range(0, n_keys, 2):
            slots[s] = value if s == 0 else over_keys(value, s)
        for s in range(0, n_keys, 2):
            slots[s + 1] = over_keys(slots[s], 1)
        return slots

    def add(left, right):
        return (left.astype(f32) + right.astype(f32)).astype(bf16)

    lat = latents.reshape(rows, dim)
    cot = cotangent.reshape(rows, dim)
    row = lambda v: v.reshape(1, dim)
    packed = inner + LANES
    patch_block = pl.BlockSpec((1, key_rows, dim), lambda i, *_: (i, 0, 0))
    inner_block = pl.BlockSpec((1, key_rows, inner), lambda i, *_: (i, 0, 0))
    time_block = whole((n_frames, dim))
    stat_block = pl.BlockSpec((8, key_rows), lambda i, *_: (0, i))
    patch_flops = 4 * all_rows * dim * inner
    att_flops = 4 * media * n_keys * own * (key_rows + own) * inner * (GROUP // HEAD)

    def call(kernel, name, grid, in_specs, out_specs, out_shape, price, prefetch=1, free=(), **more):
        run = pl.pallas_call(
            kernel,
            name=name,
            grid_spec=pltpu.PrefetchScalarGridSpec(
                num_scalar_prefetch=prefetch,
                grid=grid,
                in_specs=in_specs,
                out_specs=out_specs,
                scratch_shapes=more.pop("scratch_shapes", ()),
            ),
            out_shape=out_shape,
            compiler_params=params(),
            cost_estimate=price,
            **more,
        )

        def pinned(*args):
            args = list(args)
            for i in range(prefetch, len(args)):
                if i - prefetch not in free:
                    args[i] = pltpu.with_memory_space_constraint(args[i], pltpu.HBM)
            return run(*args)

        return pinned

    own_rows, q_own = call(
        latent_kernel,
        "latent_project",
        (1,),
        [whole((rows, dim)), whole((1, dim)), whole((1, dim)), whole((rows, dim)), whole((dim, inner))],
        [whole((rows, 2 * dim)), whole((rows, inner))],
        (struct((rows, 2 * dim), bf16), struct((rows, inner), bf16)),
        cost(2 * rows * dim * inner, 2 * dim * inner + 14 * rows * dim),
        prefetch=0,
    )(lat, row(latent_gain), row(latent_bias), cot, query_weight)
    q_all = exchange_keys([q_own] * n_keys)
    rows_all = lax.all_gather(own_rows, ("near", "keys"), axis=0, tiled=True)

    out = call(
        functools.partial(patch_kernel, n_keys, frames),
        "project_attend",
        (media,),
        [
            patch_block,
            time_block,
            whole((1, dim)),
            whole((1, dim)),
            whole((dim, inner)),
            whole((dim, inner)),
            whole((rows, dim)),
        ]
        + [whole((rows, inner))] * n_keys,
        [
            patch_block,
            inner_block,
            inner_block,
            whole((rows, inner)),
            whole((rows, inner)),
            stat_block,
            pl.BlockSpec((1, key_rows, LANES), lambda i, *_: (i, 0, 0)),
            whole((8, 2 * inner)),
        ]
        + [whole((rows, packed))] * n_keys,
        [
            struct(patches.shape, bf16),
            struct((media, key_rows, inner), bf16),
            struct((media, key_rows, inner), bf16),
            struct((rows, inner), bf16),
            struct((rows, inner), bf16),
            struct((8, all_rows), f32),
            struct((media, key_rows, LANES), bf16),
            struct((8, 2 * inner), f32),
        ]
        + [struct((rows, packed), bf16)] * n_keys,
        cost(patch_flops + att_flops, 12 * all_rows * dim),
        prefetch=2,
        free=range(8, 7 + n_keys),
    )(
        scalars,
        frame_counts,
        patches,
        time_embedding,
        row(media_gain),
        row(media_bias),
        key_weight,
        value_weight,
        own_rows,
        *q_all,
    )
    media_low, kp, vp, kl, vl, norm_stat, once, norm_vec = out[:8]
    shares = out[8:]
    joined = exchange_keys(shares)

    chunk = min(1024, hidden)
    wo_rows = inner * dim // n_keys // dim
    wo_shape = (n_keys, wo_rows, dim) if aligned else (inner, dim)
    resampled, mid_grad, pack, ff_small, out_slots, ff_low = call(
        functools.partial(forward_kernel, n_keys, aligned),
        "feed_forward",
        (hidden // chunk,),
        [
            whole((rows, dim)),
            whole((rows, dim)),
            pl.BlockSpec((rows, dim), lambda i, *_: (0, 1)),
            whole((1, dim)),
            whole((1, dim)),
            whole((inner, dim)),
            pl.BlockSpec((dim, chunk), lambda i, *_: (0, i)),
            pl.BlockSpec((chunk, dim), lambda i, *_: (i, 0)),
        ]
        + [whole((rows, packed))] * n_keys,
        [
            whole((rows, dim)),
            whole((rows, dim)),
            whole((rows, packed)),
            whole((2, dim)),
            whole(wo_shape),
            whole((rows, dim)),
        ],
        (
            struct((rows, dim), f32),
            struct((rows, dim), f32),
            struct((rows, packed), bf16),
            struct((2, dim), f32),
            struct(wo_shape, bf16),
            struct((rows, dim), bf16),
        ),
        cost(8 * rows * dim * hidden, 4 * dim * hidden + 24 * rows * dim),
        free=range(9, 8 + n_keys),
        scratch_shapes=[
            pltpu.VMEM((rows, dim), f32),
            pltpu.VMEM((rows, dim), f32),
            pltpu.VMEM((inner, dim) if aligned else (8, LANES), f32),
            pltpu.VMEM((rows, inner), f32),
            pltpu.VMEM((rows, inner), bf16),
            pltpu.VMEM((rows, dim), f32),
            pltpu.VMEM((rows, LANES), f32),
        ],
    )(
        scalars,
        lat,
        cot,
        own_rows,
        row(ff_gain),
        row(ff_bias),
        out_weight,
        up_weight,
        down_weight,
        *joined,
    )
    ff_low, rows_all = tie(ff_low, rows_all)
    ff_all = lax.all_gather(ff_low, ("near", "keys"), axis=0, tiled=True)
    if not aligned:
        c = dim // n_keys
        out_slots = out_slots.reshape(n_media, inner // n_media, n_keys, c // each, each)
        out_slots = out_slots.transpose(2, 3, 1, 0, 4).reshape(n_keys, wo_rows, dim)
        out_slots = jnp.stack(
            [lax.dynamic_index_in_dim(out_slots, key ^ s, 0, False) for s in range(n_keys)]
        )
    packs = gather_keys(pack)

    half_keys = n_keys // 2
    pick = lambda turn: (lambda s: s[5] ^ (1 - turn))
    high = 3 * width + wo_rows

    def regroup(value):
        value = jnp.moveaxis(value, 1, 2).reshape(-1, high, n_far, PAIR, each)
        value = value.transpose(0, 3, 1, 2, 4).reshape(-1, PAIR, high, n_far * each)
        return jnp.where(near == 0, value, value[:, ::-1])

    def attend_back(turn, packs, q_before, small_before):
        g = pick(turn)
        own_cols = pl.BlockSpec((rows, GROUP), lambda i, s, *_: (0, g(s)))
        stat_cols = pl.BlockSpec((rows, LANES), lambda i, *_: (0, inner // LANES))
        n = SIDE if media % SIDE == 0 else 1
        key_cols = pl.BlockSpec((n, key_rows, GROUP), lambda i, s, *_: (i, 0, g(s)))
        far_spec = pl.BlockSpec(memory_space=pl.ANY)
        q_width = GROUP if turn == 0 else inner
        chain = (n_keys // 4, PAIR, high, dim // PAIR)
        out = call(
            functools.partial(
                attend_back_kernel, n_keys, frames, turn, inner // HEAD, width, aligned
            ),
            "attend_back",
            (media // n,),
            [own_cols] * (2 * n_keys)
            + [stat_cols] * n_keys
            + [key_cols, key_cols, own_cols, own_cols]
            + [
                pl.BlockSpec((8, GROUP), lambda i, s, *_: (0, g(s))),
                pl.BlockSpec((8, GROUP), lambda i, s, *_: (0, inner // GROUP + g(s))),
                pl.BlockSpec((n, key_rows, dim), lambda i, *_: (i, 0, 0)),
                pl.BlockSpec((n, key_rows, LANES), lambda i, *_: (i, 0, 0)),
                whole((8, all_rows)),
                pl.BlockSpec((rows, dim), lambda i, *_: (0, 0)),
                whole((1, dim)),
                whole((1, dim)),
            ]
            + [far_spec] * 4
            + [whole((rows, GROUP))] * len(q_before)
            + [whole((8, dim))] * len(small_before),
            [
                pl.BlockSpec((2, GROUP, n * key_rows), lambda i, *_: (0, 0, i)),
                whole((8, all_rows)),
                whole((rows, GROUP)),
                whole((rows, GROUP)),
                whole(chain),
                whole(chain),
                whole((8, dim)),
            ]
            + [whole((rows, q_width))] * n_keys,
            [
                struct((2, GROUP, all_rows), bf16),
                struct((8, all_rows), f32),
                struct((rows, GROUP), bf16),
                struct((rows, GROUP), bf16),
                struct(chain, bf16),
                struct(chain, bf16),
                struct((8, dim), f32),
            ]
            + [struct((rows, q_width), bf16)] * n_keys,
            cost(5 * att_flops // 4 + patch_flops // 2, 4 * all_rows * (inner + dim)),
            prefetch=2,
            free=tuple(j * n_keys + s for j in range(3) for s in range(1, n_keys)),
            scratch_shapes=[
                pltpu.VMEM((2 * GROUP + 16, dim), f32),
                pltpu.VMEM((2 * GROUP, LANES), f32),
                pltpu.VMEM((8, LANES), f32),
                pltpu.VMEM((n_keys * rows, GROUP), bf16),
                pltpu.VMEM((n_keys * rows, dim), bf16),
                pltpu.VMEM((GROUP // width, wo_rows, dim), bf16),
                pltpu.VMEM((dim, GROUP), bf16),
                pltpu.VMEM((dim, GROUP), bf16),
                pltpu.SemaphoreType.DMA((4,)),
            ],
        )(
            scalars,
            frame_counts,
            *q_all,
            *packs,
            *packs,
            kp,
            vp,
            kl,
            vl,
            norm_vec,
            norm_vec,
            media_low,
            once,
            norm_stat,
            own_rows,
            row(media_gain),
            row(media_bias),
            rows_all,
            out_slots,
            key_weight,
            value_weight,
            *q_before,
            *small_before,
        )
        chains = out[4:6] if aligned else [regroup(v) for v in out[4:6]]
        return out[:4], chains, out[6], out[7:]

    group_rows = PAIR * n_keys * rows
    (kv_a, stat_a, kl_a, vl_a), (given_a, kept_a), media_small, q_a = attend_back(0, packs, [], [])
    far_core = over_keys(given_a, 1)
    ff_all, kept_a = tie(ff_all, kept_a)

    units = hidden // (n_keys * PAIR)
    share = hidden // (n_media * n_keys)
    runs, per_run = (2, n_far // 2) if aligned else (1, 1)
    if aligned:
        own_up = [
            pl.BlockSpec(
                (dim, share),
                lambda i, s, n=n: (0, ((i * per_run + n) * PAIR + s[1]) * n_keys + s[0]),
            )
            for n in range(per_run)
        ]
        own_weights = [up_weight] * per_run
    else:
        shares = up_weight.reshape(dim, n_far, PAIR, n_keys, share)
        shares = lax.dynamic_index_in_dim(shares, key, 3, False)
        own_weights = [lax.dynamic_index_in_dim(shares, near, 2, False).reshape(dim, units)]
        own_up = [whole((dim, units))]
    ff_partial = call(
        functools.partial(ff_grad_kernel, n_keys, aligned),
        "feed_forward_weights",
        (runs,),
        [
            whole((group_rows, dim)),
            pl.BlockSpec((group_rows, dim), lambda i, s: (0, 1)),
            pl.BlockSpec((dim, units // runs), lambda i, s: (0, s[4] * runs + i)),
            pl.BlockSpec((units // runs, dim), lambda i, s: (s[4] * runs + i, 0)),
        ]
        + own_up,
        whole((2, units, dim)),
        struct((2, units, dim), bf16),
        cost(12 * group_rows * dim * units, 12 * dim * units + 4 * group_rows * dim),
    )(scalars, ff_all, rows_all, up_weight, down_weight, *own_weights)
    blocks = n_far // n_keys
    cols = dim // n_keys
    if not aligned:
        downs = ff_partial[1].reshape(n_far, share, n_keys, blocks, cols // blocks)
        downs = downs.transpose(2, 1, 3, 0, 4).reshape(n_keys, units // n_keys * dim)
        downs = jnp.stack(
            [lax.dynamic_index_in_dim(downs, key ^ s, 0, False) for s in range(n_keys)]
        )
        ups = ff_partial[0].reshape(units, n_far, PAIR, each)
        ups = jnp.where(near == 0, ups, ups[:, :, ::-1])
        ff_partial = jnp.stack([ups.reshape(units, dim), downs.reshape(units, dim)])
    ff_partial = ff_partial.reshape(2 * units, dim)
    far_core, ff_partial = tie(far_core, ff_partial)
    ff_sum = lax.psum_scatter(ff_partial, "far", scatter_dimension=1, tiled=True)
    far_sum = add(kept_a, far_core)
    far_sum, packs[0] = tie(far_sum, packs[0])
    far_near = over_near(far_sum[:, 1])
    (kv_b, stat_b, kl_b, vl_b), (given_b, kept_b), media_small, q_b = attend_back(
        1, packs, q_a, [media_small]
    )
    far_near, given_b, *q_b = tie(far_near, given_b, *q_b)
    far_half = add(far_sum[:, 0], far_near)

    col = lambda turn: pl.BlockSpec((dim, GROUP), lambda i, s: (0, s[5] ^ (1 - turn)))
    both = lambda value: [value, value]

    pieces = 3
    each_piece = media // pieces

    def patch_back(piece, gain, patches_grad):
        at = piece * each_piece
        block = pl.BlockSpec((1, key_rows, dim), lambda i, *_: (i + at, 0, 0))
        keys = pl.BlockSpec((2, GROUP, key_rows), lambda i, *_: (0, 0, i + at))
        stat = pl.BlockSpec((8, key_rows), lambda i, *_: (0, i + at))
        return call(
            functools.partial(patch_back_kernel, frames),
            "patch_back",
            (each_piece,),
            [
                keys,
                keys,
                stat,
                stat,
                stat,
                block,
                time_block,
                whole((1, dim)),
                col(0),
                col(0),
                col(1),
                col(1),
                pl.BlockSpec(memory_space=pl.ANY),
            ],
            block,
            struct(patches.shape, bf16),
            cost(patch_flops // pieces, 8 * all_rows * dim // pieces),
            **({} if piece == 0 else {"input_output_aliases": {13: 0}}),
        )(
            scalars,
            kv_a,
            kv_b,
            stat_a,
            stat_b,
            norm_stat,
            patches,
            time_embedding,
            gain,
            key_weight,
            value_weight,
            key_weight,
            value_weight,
            gain if piece == 0 else patches_grad,
        )

    def sum_far(value):
        return tree_sum([value] + [over_far(value, s) for s in range(1, n_far)])

    gain = row(media_gain)
    far_half, gain, given_b, *q_b = tie(far_half, gain, given_b, *q_b)
    far_got = [over_keys(far_half[j], half_keys + 2 * j) for j in range(n_keys // 4)]
    near_core = over_keys(given_b, 1)
    q_slots = exchange_keys(q_b)
    patches_grad = patch_back(0, gain, None)
    patches_grad, near_core, *q_slots = tie(patches_grad, near_core, *q_slots)
    near_sum = add(kept_b, near_core)
    near_sum, lat = tie(near_sum, lat)
    total = near_sum[0]
    for j in range(1, n_keys // 4):
        total = add(total, over_keys(near_sum[j], 2 * j))
    near_got = over_near(total[1])
    small_rows = -(-(n_frames + 6) // 8) * 8
    latents_grad, small = call(
        functools.partial(latent_back_kernel, n_keys, frames, n_frames),
        "latent_back",
        (1,),
        [whole((rows, dim)), whole((1, dim)), whole((rows, dim)), whole((8, dim)), whole((2, dim))]
        + [whole((rows, GROUP)), col(0), whole((rows, GROUP)), col(0)]
        + [whole((rows, GROUP)), col(1), whole((rows, GROUP)), col(1)]
        + [whole((dim, inner))]
        + [whole((rows, inner))] * n_keys,
        [whole((rows, dim)), whole((small_rows, dim))],
        (struct((rows, dim), f32), struct((small_rows, dim), f32)),
        cost(6 * rows * dim * inner, 6 * dim * inner + 20 * rows * dim),
        free=range(15, 14 + n_keys),
    )(
        scalars,
        lat,
        row(latent_gain),
        mid_grad,
        media_small,
        ff_small,
        kl_a,
        key_weight,
        vl_a,
        value_weight,
        kl_b,
        key_weight,
        vl_b,
        value_weight,
        query_weight,
        *q_slots,
    )

    gain, small = tie(gain, small)
    small = tree_sum([small] + [over_keys(small, s) for s in range(1, n_keys)])
    patches_grad = patch_back(1, gain, patches_grad)
    patches_grad, small, near_got, *far_got = tie(patches_grad, small, near_got, *far_got)
    total = total[0]
    for value in far_got:
        total = add(total, value)
    total = add(total, near_got)
    total, small, gain, ff_sum = tie(total, small, gain, ff_sum)
    parts = lax.all_to_all(total, "far", split_axis=1, concat_axis=0, tiled=True)
    small = small + over_near(small)
    up_keep = ff_sum[:units, :each]
    up_got = over_near(ff_sum[:units, each:])
    downs = ff_sum[units:].reshape(n_keys, share, cols)
    downs = exchange_keys([downs[s] for s in range(n_keys)])
    patches_grad = patch_back(2, gain, patches_grad)
    patches_grad, small, up_got, parts, *downs = tie(patches_grad, small, up_got, parts, *downs)
    small = sum_far(small)
    if aligned:
        q_grad, k_grad, v_grad, out_grad, up_grad, down_grad = call(
            functools.partial(finish_kernel, n_keys, width),
            "finish_weights",
            (1,),
            [whole((units, each))] * 2
            + [whole((share, cols))] * n_keys
            + [whole(parts.shape)],
            [whole((each, width))] * 3
            + [
                whole((inner // n_media, dim // n_keys)),
                whole((each, PAIR * units)),
                whole((units, dim // n_keys)),
            ],
            [struct((each, width), f32)] * 3
            + [
                struct((inner // n_media, dim // n_keys), f32),
                struct((each, PAIR * units), f32),
                struct((units, dim // n_keys), f32),
            ],
            cost(0, 16 * width * each + 12 * units * each),
            free=(1,) + tuple(range(3, 3 + n_keys)),
        )(scalars, up_keep, up_got, *downs, parts)
    else:
        total = jnp.sum(parts.reshape(n_far, -1, each).astype(f32), 0)
        q_grad, k_grad, v_grad = (total[i * width : (i + 1) * width].T for i in range(3))
        out_grad = total[3 * width :].reshape(-1, inner // n_media, each)
        out_grad = out_grad.transpose(1, 0, 2).reshape(inner // n_media, dim // n_keys)
        up_grad = jnp.where(
            near == 0,
            jnp.concatenate([up_keep, up_got], 0),
            jnp.concatenate([up_got, up_keep], 0),
        ).T.astype(f32)
        down_grad = jnp.zeros((units // blocks, cols), f32)
        for s in range(n_keys):
            down_grad = lax.dynamic_update_slice_in_dim(
                down_grad, downs[s].astype(f32), (key ^ s) * share, 0
            )

    return (
        resampled.reshape(latents.shape),
        patches_grad,
        latents_grad.reshape(latents.shape),
        small[:n_frames],
        small[n_frames],
        small[n_frames + 1],
        small[n_frames + 2],
        small[n_frames + 3],
        small[n_frames + 4],
        small[n_frames + 5],
        q_grad,
        k_grad,
        v_grad,
        out_grad,
        up_grad,
        down_grad,
    )


def solution(mesh):
    n_media, n_keys = mesh.shape["media"], mesh.shape["keys"]
    n_far = n_media // PAIR
    fine = Mesh(mesh.devices.reshape(n_far, PAIR, n_keys), ("far", "near", "keys"))
    split = P(("far", "near"), "keys", None)
    return jax.shard_map(
        functools.partial(shards, n_far, n_keys),
        mesh=fine,
        in_specs=(split, split, P(("far", "near"))) + (P(),) * 13 + (split,),
        out_specs=(split,) * 3 + (P(),) * 7 + (P(("far", "near"), "keys"),) * 6,
        check_vma=False,
    )
```

```python
import functools

import jax
import jax.numpy as jnp
from jax import lax
from jax.experimental import pallas as pl
from jax.experimental.pallas import tpu as pltpu
from jax.sharding import Mesh, PartitionSpec as P

HEAD = 64
PATCH = 256
GROUP = 256
LANES = 128

VMEM_LIMIT = 44 << 20

EPS = 1e-05
NEG = -1e30
SIDE = 2
PAIR = 2

f32 = jnp.float32
bf16 = jnp.bfloat16


def mul(left, right, contract=((1,), (0,)), precision=None):
    return lax.dot_general(
        left, right, (contract, ((), ())), precision=precision, preferred_element_type=f32
    )


NN = ((1,), (0,))
NT = ((1,), (1,))
TN = ((0,), (0,))


def norm_parts(values):
    centre = jnp.mean(values, -1, keepdims=True)
    shifted = values - centre
    spread = jnp.mean(shifted * shifted, -1, keepdims=True)
    return centre, lax.rsqrt(spread + EPS), shifted


def norm(values, gain, bias):
    _, scale, shifted = norm_parts(values)
    return shifted * scale * gain + bias


def norm_back(values, gain, grad):
    _, scale, shifted = norm_parts(values)
    unit = shifted * scale
    scaled = grad * gain
    first = jnp.mean(scaled, -1, keepdims=True)
    second = jnp.mean(scaled * unit, -1, keepdims=True)
    back = scale * (scaled - first - unit * second)
    return (
        back,
        jnp.sum(grad * unit, 0, keepdims=True),
        jnp.sum(grad, 0, keepdims=True),
    )


def gelu_parts(hidden):
    cdf = 0.5 * (1.0 + lax.erf(hidden * (2.0**-0.5)))
    pdf = jnp.exp(-0.5 * hidden * hidden) * 0.3989422804014327
    return cdf, cdf + hidden * pdf


def head_mask(rows, width, heads):
    row = lax.broadcasted_iota(jnp.int32, (heads * rows, width), 0) // rows
    col = lax.broadcasted_iota(jnp.int32, (heads * rows, width), 1)
    return row, col


def spread_heads(values):
    heads = values.shape[1] // HEAD
    row, col = head_mask(values.shape[0], values.shape[1], heads)
    return jnp.where(row == col // HEAD, jnp.concatenate([values] * heads, 0), jnp.zeros((), values.dtype))


def fold_heads(values):
    heads = values.shape[1] // HEAD
    rows = values.shape[0] // heads
    row, col = head_mask(rows, values.shape[1], heads)
    kept = jnp.where(row == col // HEAD, values, 0.0)
    total = kept[:rows]
    for h in range(1, heads):
        total = total + kept[h * rows : (h + 1) * rows]
    return total


def three_parts(values, lane, start, slots):
    high = values.astype(bf16).astype(f32)
    rest = values - high
    middle = rest.astype(bf16).astype(f32)
    low = rest - middle
    place = lane // slots - start
    return jnp.where(place == 0, high, jnp.where(place == 1, middle, jnp.where(place == 2, low, 0.0)))


def cost(flops, moved, special=0):
    return pl.CostEstimate(flops=int(flops), bytes_accessed=int(moved), transcendentals=int(special))


def params():
    return pltpu.CompilerParams(vmem_limit_bytes=VMEM_LIMIT)


def tie(*values):
    return lax.optimization_barrier(values)


def latent_kernel(lat, gain, bias, cot, wq, rows_o, q_o):
    dim = lat.shape[1]
    low = norm(lat[...], gain[...], bias[...]).astype(bf16)
    rows_o[:, :dim] = low
    rows_o[:, dim:] = cot[...].astype(bf16)
    q_o[...] = mul(low, wq[...]).astype(bf16)


def two_parts(values):
    high = values.astype(bf16)
    return high, (values - high.astype(f32)).astype(bf16)


def masked_scores(query, keys, frames, first, count):
    scores = mul(query, keys, NT)
    parts = []
    for f in range(frames):
        part = scores[:, f * PATCH : (f + 1) * PATCH]
        parts.append(jnp.where(first + f < count, part, NEG))
    return jnp.concatenate(parts + [scores[:, frames * PATCH :]], 1)


def patch_kernel(n_keys, frames, scalars, counts, patches, time, gain, bias, wk, wv, lat_low, *refs):
    q = refs[:n_keys]
    low_o, k_o, v_o, kl_o, vl_o, stat_o, once_o, vec_o = refs[n_keys : n_keys + 8]
    outs = refs[n_keys + 8 :]
    step = pl.program_id(0)

    @pl.when(step == 0)
    def _():
        kl_o[...] = mul(lat_low[...], wk[...]).astype(bf16)
        vl_o[...] = mul(lat_low[...], wv[...]).astype(bf16)
        row = lax.broadcasted_iota(jnp.int32, (16, gain.shape[1]), 0)
        both = jnp.where(row % 2 == 0, gain[...], bias[...])
        high, low = two_parts(both)
        both = jnp.where(row < 2, high.astype(f32), jnp.where(row < 4, low.astype(f32), 0.0)).astype(bf16)
        for i, w in enumerate((wk, wv)):
            term = mul(both, w[...])
            vec_o[:, i * w.shape[1] : (i + 1) * w.shape[1]] = term[:8] + pltpu.roll(term, 14, 0)[:8]

    for f in range(frames):
        rows = pl.ds(f * PATCH, PATCH)
        framed = patches[0, rows, :].astype(f32) + time[pl.ds(scalars[0] * frames + f, 1), :]
        centre, scale, shifted = norm_parts(framed)
        low = (shifted * scale * gain[...] + bias[...]).astype(bf16)
        low_o[0, rows, :] = low
        k_o[0, rows, :] = mul(low, wk[...]).astype(bf16)
        v_o[0, rows, :] = mul(low, wv[...]).astype(bf16)
        lane = lax.broadcasted_iota(jnp.int32, (PATCH, LANES), 1)
        stat = jnp.where(lane == 0, centre, jnp.where(lane == 1, scale, 0.0))
        stat_o[:, f * PATCH : (f + 1) * PATCH] = stat.T[:8]
        high = scale.astype(bf16).astype(f32)
        once = jnp.where(lane == 0, 1.0, jnp.where(lane == 1 + f, high, 0.0))
        once_o[0, rows, :] = jnp.where(lane == 1 + frames + f, scale - high, once).astype(bf16)

    own = q[0].shape[0] // pl.num_programs(0)
    inner = q[0].shape[1]
    heads = inner // HEAD
    count = counts[step]
    first = scalars[0] * frames
    here = pl.ds(pl.multiple_of(step * own, own), own)
    query = jnp.concatenate([r[here, :] for r in q], 0)
    rows = query.shape[0]
    stats = jnp.zeros((rows, LANES), f32)
    shares = []
    for g in range(inner // GROUP):
        cols = slice(g * GROUP, (g + 1) * GROUP)
        wide = spread_heads(query[:, cols] * bf16(HEAD**-0.5))
        keys = jnp.concatenate([k_o[0, :, cols], kl_o[here, cols]], 0)
        values = jnp.concatenate([v_o[0, :, cols], vl_o[here, cols]], 0)
        scores = masked_scores(wide, keys, frames, first, count)
        top = jnp.max(scores, -1, keepdims=True)
        raw = jnp.exp(scores - top)
        total = jnp.sum(raw, -1, keepdims=True)
        share = mul(raw.astype(bf16), values) * (1.0 / total)
        shares.append(fold_heads(share).astype(bf16))
        level = top + jnp.log(total)
        row, lane = head_mask(rows, LANES, GROUP // HEAD)
        kept = jnp.where(lane % heads == row + g * (GROUP // HEAD), level, 0.0)
        for h in range(GROUP // HEAD):
            stats = stats + kept[h * rows : (h + 1) * rows]
    lane = lax.broadcasted_iota(jnp.int32, stats.shape, 1)
    packed = jnp.concatenate(shares + [three_parts(stats, lane, 0, heads).astype(bf16)], 1)
    for s in range(n_keys):
        outs[s][here, :] = packed[s * own : (s + 1) * own]


def sum_runs(stats, heads, start):
    total = None
    for part in range(3):
        shift = (-(start + part) * heads) % LANES
        term = pltpu.roll(stats, shift, 1) if shift else stats
        total = term if total is None else total + term
    return total


def join(latents, gain, bias, wo, slots, att_o, low_o, mid_o, ff_o, lse_o):
    inner = att_o.shape[1]
    heads = inner // HEAD
    levels = [sum_runs(r[:, inner:].astype(f32), heads, 0) for r in slots]
    top = functools.reduce(jnp.maximum, levels)
    weights = [jnp.exp(v - top) for v in levels]
    total = functools.reduce(jnp.add, weights)
    inverse = 1.0 / total
    lane = lax.broadcasted_iota(jnp.int32, (LANES, inner), 0)
    col = lax.broadcasted_iota(jnp.int32, (LANES, inner), 1)
    select = jnp.where(lane == col // HEAD, 1.0, 0.0)
    attended = None
    for s in range(len(slots)):
        wide = mul(weights[s] * inverse, select, NN, lax.Precision.HIGHEST)
        term = wide * slots[s][:, :inner].astype(f32)
        attended = term if attended is None else attended + term
    low = attended.astype(bf16)
    middle = latents[...] + mul(low, wo[...])
    att_o[...] = attended
    low_o[...] = low
    mid_o[...] = middle
    ff_o[...] = norm(middle, gain[...], bias[...]).astype(bf16)
    lse_o[...] = top + jnp.log(total)


def forward_kernel(
    n_keys,
    aligned,
    scalars,
    latents,
    cot,
    out_low,
    gain,
    bias,
    wo,
    up,
    down,
    *refs,
):
    slots = refs[:n_keys]
    res_o, mid_grad_o, pack_o, small_o, wo_grad_o, ff_low = refs[n_keys : n_keys + 6]
    res_acc, in_acc, wo_acc, attended, att_low, middle, lse = refs[n_keys + 6 :]
    step = pl.program_id(0)

    @pl.when(step == 0)
    def _():
        res_acc[...] = jnp.zeros_like(res_acc)
        in_acc[...] = jnp.zeros_like(in_acc)
        join(latents, gain, bias, wo, slots, attended, att_low, middle, ff_low, lse)

    hidden = mul(ff_low[...], up[...])
    act_grad = mul(out_low[...], down[...], NT)
    cdf, slope = gelu_parts(hidden)
    res_acc[...] += mul((hidden * cdf).astype(bf16), down[...])
    in_acc[...] += mul((act_grad * slope).astype(bf16), up[...], NT)

    @pl.when(step == pl.num_programs(0) - 1)
    def _():
        inner = attended.shape[1]
        heads = inner // HEAD
        res_o[...] = middle[...] + res_acc[...]
        back, gain_grad, bias_grad = norm_back(middle[...], gain[...], in_acc[...])
        small_o[0:1, :] = gain_grad
        small_o[1:2, :] = bias_grad
        mid_grad = cot[...] + back
        mid_grad_o[...] = mid_grad
        branch = mid_grad.astype(bf16)
        att_grad = mul(branch, wo[...], NT).astype(bf16)
        col = lax.broadcasted_iota(jnp.int32, (inner, LANES), 0)
        lane = lax.broadcasted_iota(jnp.int32, (inner, LANES), 1)
        select = jnp.where(col // HEAD == lane % heads, 1.0, 0.0)
        delta = mul(attended[...] * att_grad.astype(f32), select, NN, lax.Precision.HIGHEST)
        lane = lax.broadcasted_iota(jnp.int32, delta.shape, 1)
        level = jnp.where(lane < heads, lse[...], 0.0)
        level = level + pltpu.roll(level, heads, 1) + pltpu.roll(level, 2 * heads, 1)
        stats = three_parts(level, lane, 0, heads) + three_parts(delta, lane, 3, heads)
        pack_o[...] = jnp.concatenate([att_grad, stats.astype(bf16)], 1)
        wo_grad = mul(att_low[...], branch, TN)
        if aligned:
            wo_acc[...] = wo_grad
            slot_rows(scalars, wo_acc, wo_grad_o, n_keys)
        else:
            wo_grad_o[...] = wo_grad.astype(bf16)


def slot_rows(scalars, full, out, n_keys):
    lanes = LANES
    n_media = out.shape[2] // lanes
    r = full.shape[0] // n_media
    c = full.shape[1] // n_keys
    for s in range(n_keys):
        owner = (scalars[0] ^ s) * c
        for m in range(n_media):
            place = slice(m * lanes, (m + 1) * lanes)
            for h in range(c // lanes):
                start = pl.multiple_of(owner + h * lanes, lanes)
                out[s, h * r : (h + 1) * r, place] = full[
                    m * r : (m + 1) * r, pl.ds(start, lanes)
                ].astype(bf16)


def ff_grad_kernel(n_keys, aligned, scalars, ff_all, out_all, up, down, *refs):
    own_ups, grad_o = refs[:-1], refs[-1]
    units, dim = down.shape
    step = pl.program_id(0)
    hidden = mul(ff_all[...], up[...])
    act_grad = mul(out_all[...], down[...], NT)
    _, slope = gelu_parts(hidden)
    up_grad = mul((act_grad * slope).astype(bf16), ff_all[...], TN).astype(bf16)
    rows = pl.ds(pl.multiple_of(step * units, 8), units)
    if not aligned:
        grad_o[0] = up_grad
        hidden = mul(ff_all[...], own_ups[0][...])
        cdf, _ = gelu_parts(hidden)
        grad_o[1] = mul((hidden * cdf).astype(bf16), out_all[...], TN).astype(bf16)
        return
    for j in range(dim // LANES):
        place = ((j // PAIR) * PAIR + (scalars[1] ^ (j % PAIR))) * LANES
        grad_o[0, rows, pl.ds(pl.multiple_of(place, LANES), LANES)] = up_grad[
            :, j * LANES : (j + 1) * LANES
        ]
    each = own_ups[0].shape[1]
    cols = dim // n_keys
    hidden = mul(ff_all[...], jnp.concatenate([r[...] for r in own_ups], 1))
    cdf, _ = gelu_parts(hidden)
    down_grad = mul((hidden * cdf).astype(bf16), out_all[...], TN).astype(bf16)
    for n in range(len(own_ups)):
        lanes = pl.ds(pl.multiple_of((step * len(own_ups) + n) * cols, LANES), cols)
        for k in range(n_keys):
            place = pl.ds(pl.multiple_of((scalars[0] ^ k) * each, each), each)
            grad_o[1, place, lanes] = down_grad[
                n * each : (n + 1) * each, k * cols : (k + 1) * cols
            ]


def attend_back_kernel(n_keys, frames, turn, heads, width, aligned, scalars, counts, *refs):
    refs = list(refs)
    take = lambda n: [refs.pop(0) for _ in range(n)]
    q, grads, stat = take(n_keys), take(n_keys), take(n_keys)
    kp, vp, kl, vl, k_vec, v_vec, low, once, norm_stat, lat_own, gain, bias = take(12)
    rows_far, wo_far, wk_far, wv_far = take(4)
    q_before = take(n_keys if turn else 0)
    small_before = take(turn)
    kv_t_o, stat_o, kl_o, vl_o, given, kept, small = take(7)
    q_o = take(n_keys)
    grad_acc, sums, scalar_sums, q_acc, rows_all, wo_g, wk, wv, sems = refs
    n = kp.shape[0]
    each = range(n)
    rows = kl_o.shape[0]
    own = rows // (pl.num_programs(0) * n)
    dim = low.shape[2]
    per = GROUP // HEAD
    step = pl.program_id(0)
    first_frame = scalars[0] * frames
    group = scalars[5] ^ (1 - turn)
    owners = GROUP // width
    group_cols = pl.ds(pl.multiple_of(group * GROUP, GROUP), GROUP)
    near_rows = pl.ds(pl.multiple_of(scalars[1] * n_keys * rows, 8), n_keys * rows)
    fetches = [
        pltpu.make_async_copy(rows_far.at[near_rows, pl.ds(0, dim)], rows_all, sems.at[0]),
        pltpu.make_async_copy(wo_far.at[pl.ds(owners * (1 - turn), owners)], wo_g, sems.at[1]),
        pltpu.make_async_copy(wk_far.at[:, group_cols], wk, sems.at[2]),
        pltpu.make_async_copy(wv_far.at[:, group_cols], wv, sems.at[3]),
    ]

    @pl.when(step == 0)
    def _():
        for fetch in fetches:
            fetch.start()
        grad_acc[...] = jnp.zeros_like(grad_acc)
        sums[...] = jnp.zeros_like(sums)
        scalar_sums[...] = jnp.zeros_like(scalar_sums)

    here = [pl.ds(pl.multiple_of((step * n + m) * own, own), own) for m in each]
    n_patch = kp.shape[1]
    n_query = n_keys * own
    row, lane = head_mask(n_query, LANES, per)
    mine = lane % heads == row + group * per
    levels = mine & (lane < 3 * heads)
    deltas = mine & (lane >= 3 * heads) & (lane < 6 * heads)
    wide, wide_grad, keys, values, level, delta = [], [], [], [], [], []
    for m in each:
        wide.append(
            spread_heads(jnp.concatenate([r[here[m], :] for r in q], 0) * bf16(HEAD**-0.5))
        )
        wide_grad.append(spread_heads(jnp.concatenate([r[here[m], :] for r in grads], 0)))
        keys.append(jnp.concatenate([kp[m], kl[here[m], :]], 0))
        values.append(jnp.concatenate([vp[m], vl[here[m], :]], 0))
    scores = [
        masked_scores(wide[m], keys[m], frames, first_frame, counts[step * n + m]) for m in each
    ]
    prob_grad = [mul(wide_grad[m], values[m], NT) for m in each]
    for m in each:
        stats = jnp.concatenate([r[here[m], :] for r in stat], 0).astype(f32)
        tiled = jnp.concatenate([stats] * per, 0)
        level.append(jnp.sum(jnp.where(levels, tiled, 0.0), -1, keepdims=True))
        delta.append(jnp.sum(jnp.where(deltas, tiled, 0.0), -1, keepdims=True))
    probs = [jnp.exp(scores[m] - level[m]) for m in each]
    score_grad = [probs[m] * (prob_grad[m] - delta[m]) for m in each]
    along = [
        jnp.sum(score_grad[m] * scores[m] + probs[m] * prob_grad[m], 0, keepdims=True) for m in each
    ]
    score_grad = [v.astype(bf16) for v in score_grad]
    probs = [v.astype(bf16) for v in probs]
    beside = lambda value, vec: jnp.concatenate(
        [value, mul(value, vec[...].astype(bf16), NT).astype(bf16)], 1
    )
    key_side = [beside(v, k_vec) for v in wide]
    value_side = [beside(v, v_vec) for v in wide_grad]
    key_t = [mul(key_side[m], score_grad[m], TN) for m in each]
    value_t = [mul(value_side[m], probs[m], TN) for m in each]
    query_grad = [mul(score_grad[m], keys[m]) for m in each]
    frame = lax.broadcasted_iota(jnp.int32, (16, n_patch), 1) // PATCH
    row16 = lax.broadcasted_iota(jnp.int32, (16, n_patch), 0)
    same = frame == row16 % frames
    sides, kvs = [], []
    line8 = lax.broadcasted_iota(jnp.int32, scalar_sums.shape, 0)
    adds = jnp.zeros(scalar_sums.shape, f32)
    for m in each:
        kl_o[here[m], :] = key_t[m][:GROUP, n_patch:].T.astype(bf16)
        vl_o[here[m], :] = value_t[m][:GROUP, n_patch:].T.astype(bf16)
        kv = jnp.concatenate([key_t[m][:GROUP, :n_patch], value_t[m][:GROUP, :n_patch]], 0)
        kv = kv.astype(bf16)
        kv_t_o[0, :, m * n_patch : (m + 1) * n_patch] = kv[:GROUP]
        kv_t_o[1, :, m * n_patch : (m + 1) * n_patch] = kv[GROUP:]
        ends = key_t[m][GROUP:, :n_patch] + value_t[m][GROUP:, :n_patch]
        line = lax.broadcasted_iota(jnp.int32, ends.shape, 0)
        stat_rows = jnp.where(line == 1, along[m][:, :n_patch] - ends, ends)
        span = pl.ds(pl.multiple_of((step * n + m) * n_patch, n_patch), n_patch)
        stat_o[:, span] = stat_rows
        scale = norm_stat[1:2, span] * (1.0 / dim)
        first = stat_rows[0:1, :] * scale
        second = stat_rows[1:2, :] * scale
        high = second.astype(bf16).astype(f32)
        ends = jnp.where(same & (row16 < frames), high, 0.0)
        ends = jnp.where(same & (row16 >= frames) & (row16 < 2 * frames), second - high, ends)
        kvs.append(kv)
        sides.append(jnp.concatenate([kv, ends.astype(bf16)], 0))
        for f in range(frames):
            cut = slice(f * PATCH, (f + 1) * PATCH)
            one = jnp.sum(first[:, cut], -1, keepdims=True)
            two = jnp.sum(second[:, cut], -1, keepdims=True)
            adds = adds + jnp.where(line8 == f, one, jnp.where(line8 == frames + f, two, 0.0))
    scalar_sums[...] += adds
    grad_acc[...] += mul(jnp.concatenate(sides, 1), low[...].reshape(n * n_patch, dim))
    sums[...] += mul(jnp.concatenate(kvs, 1), once[...].reshape(n * n_patch, LANES))

    for m in each:
        part = (fold_heads(query_grad[m]) * HEAD**-0.5).astype(bf16)
        for s in range(n_keys):
            piece = part[s * own : (s + 1) * own]
            place = pl.multiple_of((scalars[0] ^ s) * rows + (step * n + m) * own, own)
            q_acc[pl.ds(place, own), :] = piece
            if turn == 0:
                q_o[s][here[m], :] = piece
            else:
                other = pl.ds(pl.multiple_of((1 - group) * GROUP, GROUP), GROUP)
                q_o[s][here[m], group_cols] = piece
                q_o[s][here[m], other] = q_before[s][here[m], :]

    @pl.when(step == pl.num_programs(0) - 1)
    def _():
        for fetch in fetches:
            fetch.wait()
        behind = None
        for part in two_parts(sums[...]):
            for i, w in enumerate((wk, wv)):
                term = mul(part[i * GROUP : (i + 1) * GROUP], w[...], ((0,), (1,)))
                behind = term if behind is None else behind + term
        bias_grad = behind[0:1]
        main = grad_acc[: 2 * GROUP, :]
        ends = grad_acc[2 * GROUP :, :]
        total = jnp.sum(main[:GROUP] * wk[...].astype(f32).T, 0, keepdims=True)
        total = total + jnp.sum(main[GROUP:] * wv[...].astype(f32).T, 0, keepdims=True)
        over = 1.0 / gain[...]
        lines = []
        for f in range(frames):
            along = ends[f : f + 1] + ends[frames + f : frames + f + 1]
            scaled = behind[1 + f : 2 + f] + behind[1 + frames + f : 2 + frames + f]
            second_sum = scalar_sums[frames + f : frames + f + 1, 0:1]
            lines.append(
                gain[...] * scaled
                - scalar_sums[f : f + 1, 0:1]
                - (along - bias[...] * second_sum) * over
            )
        lines += [(total - bias[...] * bias_grad) * over, bias_grad]
        for i, value in enumerate(lines):
            small[i : i + 1, :] = value + small_before[0][i : i + 1, :] if turn else value
        kv_lat = jnp.concatenate([kl_o[...], vl_o[...]], 1)
        grad_acc[: 2 * GROUP, :] = main + mul(kv_lat, lat_own[...], TN)
        q_grad = mul(q_acc[...], rows_all[...], TN)
        sums_q = q_grad.astype(bf16)
        near = scalars[1] if aligned else 0
        runs = dim // PAIR // LANES
        for j in range(owners):
            out = (given, kept)[j % 2]
            slot = 2 * (j // 2) + 1 - j % 2
            start = ((scalars[0] ^ slot) % owners) * width
            for part in range(3):
                at = pl.multiple_of((part - 1) * GROUP + start, width)
                if part == 0:
                    piece = jnp.zeros((width, dim), bf16)
                    for o in range(owners):
                        same = start == o * width
                        piece = jnp.where(same, sums_q[o * width : (o + 1) * width], piece)
                else:
                    piece = grad_acc[pl.ds(at, width), :].astype(bf16)
                place_rows(out, scalars, j // 2, part * width, piece, aligned)
            place_rows(out, scalars, j // 2, 3 * width, wo_g[slot], aligned)


def place_rows(out, scalars, slot, start, piece, aligned):
    rows = slice(start, start + piece.shape[0])
    half = piece.shape[1] // PAIR
    if aligned:
        for m in range(piece.shape[1] // LANES):
            place = slice((m // PAIR) * LANES, (m // PAIR + 1) * LANES)
            out[slot, scalars[1] ^ (m % PAIR), rows, place] = piece[:, m * LANES : (m + 1) * LANES]
    else:
        for n in range(PAIR):
            out[slot, n, rows, :] = piece[:, n * half : (n + 1) * half]


def patch_back_kernel(
    frames, scalars, kv_a, kv_b, stat_a, stat_b, norm_stat, patches, time, gain, wk_a, wv_a, wk_b, wv_b, _, grad_o
):
    turned = ((0,), (1,))
    inverse = 1.0 / gain.shape[1]
    for f in range(frames):
        rows = pl.ds(f * PATCH, PATCH)
        span = slice(f * PATCH, (f + 1) * PATCH)
        scale = norm_stat[1:2, span]
        first = (stat_a[0:1, span] + stat_b[0:1, span]) * inverse
        second = (stat_a[1:2, span] + stat_b[1:2, span]) * inverse
        slope = scale * scale * second
        level = scale * first - norm_stat[0:1, span] * slope
        line = lax.broadcasted_iota(jnp.int32, (8, PATCH), 0)
        columns = jnp.where(line == 0, scale, jnp.where(line == 1, level, slope)).T
        grad = mul(kv_a[0, :, span], wk_a[...], turned)
        grad = grad + mul(kv_a[1, :, span], wv_a[...], turned)
        grad = grad + mul(kv_b[0, :, span], wk_b[...], turned)
        grad = grad + mul(kv_b[1, :, span], wv_b[...], turned)
        framed = patches[0, rows, :].astype(f32) + time[pl.ds(scalars[0] * frames + f, 1), :]
        back = grad * gain[...] * columns[:, 0:1] - columns[:, 1:2] - framed * columns[:, 2:3]
        grad_o[0, rows, :] = back.astype(bf16)


def latent_back_kernel(n_keys, frames, n_frames, scalars, latents, gain, mid_grad, media_small, ff_small, *refs):
    keys = refs[:8]
    wq = refs[8]
    slots = refs[9 : 9 + n_keys]
    lat_o, small_o = refs[9 + n_keys :]
    query = functools.reduce(jnp.add, [r[...].astype(f32) for r in slots]).astype(bf16)
    grad = mul(query, wq[...], NT)
    for i in range(4):
        grad = grad + mul(keys[2 * i][...], keys[2 * i + 1][...], NT)
    back, gain_grad, bias_grad = norm_back(latents[...], gain[...], grad)
    lat_o[...] = mid_grad[...] + back
    small_o[...] = jnp.zeros_like(small_o)
    for f in range(frames):
        small_o[pl.ds(scalars[0] * frames + f, 1), :] = media_small[f : f + 1, :]
    for i, line in enumerate(
        (media_small[frames : frames + 1, :], media_small[frames + 1 : frames + 2, :], gain_grad, bias_grad)
    ):
        small_o[n_frames + i : n_frames + i + 1, :] = line
    small_o[n_frames + 4 : n_frames + 6, :] = ff_small[...]


def finish_kernel(n_keys, width, scalars, up_keep, up_got, *refs):
    downs, parts = refs[:n_keys], refs[n_keys]
    q_o, k_o, v_o, out_o, up_o, down_o = refs[-6:]
    high = 3 * width + out_o.shape[0] * out_o.shape[1] // LANES
    total = parts[:high].astype(f32)
    for s in range(1, parts.shape[0] // high):
        total = total + parts[s * high : (s + 1) * high].astype(f32)
    for i, ref in enumerate((q_o, k_o, v_o)):
        ref[...] = total[i * width : (i + 1) * width].T
    r = out_o.shape[0]
    for h in range(out_o.shape[1] // LANES):
        out_o[:, h * LANES : (h + 1) * LANES] = total[3 * width + h * r : 3 * width + (h + 1) * r]
    units = up_keep.shape[0]
    near = scalars[1]
    own = pl.ds(pl.multiple_of(near * units, LANES), units)
    other = pl.ds(pl.multiple_of((1 - near) * units, LANES), units)
    up_o[:, own] = up_keep[...].astype(f32).T
    up_o[:, other] = up_got[...].astype(f32).T
    share = downs[0].shape[0]
    for s, ref in enumerate(downs):
        down_o[pl.ds(pl.multiple_of((scalars[0] ^ s) * share, share), share), :] = ref[...].astype(f32)


def whole(shape):
    return pl.BlockSpec(shape, lambda *_: (0,) * len(shape))


def struct(shape, dtype):
    return pltpu.HBM(shape, dtype)


def tree_sum(parts):
    while len(parts) > 1:
        parts = [parts[i] + parts[i + 1] for i in range(0, len(parts), 2)]
    return parts[0]


def shards(
    n_far,
    n_keys,
    latents,
    patches,
    frame_counts,
    time_embedding,
    media_gain,
    media_bias,
    latent_gain,
    latent_bias,
    ff_gain,
    ff_bias,
    query_weight,
    key_weight,
    value_weight,
    out_weight,
    up_weight,
    down_weight,
    cotangent,
):
    media, own, dim = latents.shape
    key_rows = patches.shape[1]
    inner = query_weight.shape[1]
    hidden = up_weight.shape[1]
    frames = key_rows // PATCH
    n_frames = time_embedding.shape[0]
    n_media = n_far * PAIR
    rows = media * own
    all_rows = media * key_rows
    width = inner // n_keys
    each = dim // n_media
    aligned = each == LANES and width % LANES == 0 and n_far == n_keys
    far = lax.axis_index("far")
    near = lax.axis_index("near")
    key = lax.axis_index("keys")
    own_group = key // (n_keys // 2)
    scalars = jnp.stack([key, near, far, far, key * PAIR + near, own_group, jnp.full_like(far, dim)])
    scalars = scalars.astype(jnp.int32)

    def over_keys(value, shift):
        return lax.ppermute(value, "keys", [(i, i ^ shift) for i in range(n_keys)])

    def over_near(value):
        return lax.ppermute(value, "near", [(0, 1), (1, 0)])

    def over_far(value, shift):
        return lax.ppermute(value, "far", [(i, i ^ shift) for i in range(n_far)])

    def exchange_keys(slots):
        return [slots[0]] + [over_keys(slots[s], s) for s in range(1, n_keys)]

    def gather_keys(value):
        slots = [None] * n_keys
        for s in range(0, n_keys, 2):
            slots[s] = value if s == 0 else over_keys(value, s)
        for s in range(0, n_keys, 2):
            slots[s + 1] = over_keys(slots[s], 1)
        return slots

    def add(left, right):
        return (left.astype(f32) + right.astype(f32)).astype(bf16)

    lat = latents.reshape(rows, dim)
    cot = cotangent.reshape(rows, dim)
    row = lambda v: v.reshape(1, dim)
    packed = inner + LANES
    patch_block = pl.BlockSpec((1, key_rows, dim), lambda i, *_: (i, 0, 0))
    inner_block = pl.BlockSpec((1, key_rows, inner), lambda i, *_: (i, 0, 0))
    time_block = whole((n_frames, dim))
    stat_block = pl.BlockSpec((8, key_rows), lambda i, *_: (0, i))
    patch_flops = 4 * all_rows * dim * inner
    att_flops = 4 * media * n_keys * own * (key_rows + own) * inner * (GROUP // HEAD)

    def call(kernel, name, grid, in_specs, out_specs, out_shape, price, prefetch=1, free=(), **more):
        run = pl.pallas_call(
            kernel,
            name=name,
            grid_spec=pltpu.PrefetchScalarGridSpec(
                num_scalar_prefetch=prefetch,
                grid=grid,
                in_specs=in_specs,
                out_specs=out_specs,
                scratch_shapes=more.pop("scratch_shapes", ()),
            ),
            out_shape=out_shape,
            compiler_params=params(),
            cost_estimate=price,
            **more,
        )

        def pinned(*args):
            args = list(args)
            for i in range(prefetch, len(args)):
                if i - prefetch not in free:
                    args[i] = pltpu.with_memory_space_constraint(args[i], pltpu.HBM)
            return run(*args)

        return pinned

    own_rows, q_own = call(
        latent_kernel,
        "latent_project",
        (1,),
        [whole((rows, dim)), whole((1, dim)), whole((1, dim)), whole((rows, dim)), whole((dim, inner))],
        [whole((rows, 2 * dim)), whole((rows, inner))],
        (struct((rows, 2 * dim), bf16), struct((rows, inner), bf16)),
        cost(2 * rows * dim * inner, 2 * dim * inner + 14 * rows * dim),
        prefetch=0,
    )(lat, row(latent_gain), row(latent_bias), cot, query_weight)
    q_all = exchange_keys([q_own] * n_keys)
    rows_all = lax.all_gather(own_rows, ("near", "keys"), axis=0, tiled=True)

    out = call(
        functools.partial(patch_kernel, n_keys, frames),
        "project_attend",
        (media,),
        [
            patch_block,
            time_block,
            whole((1, dim)),
            whole((1, dim)),
            whole((dim, inner)),
            whole((dim, inner)),
            whole((rows, dim)),
        ]
        + [whole((rows, inner))] * n_keys,
        [
            patch_block,
            inner_block,
            inner_block,
            whole((rows, inner)),
            whole((rows, inner)),
            stat_block,
            pl.BlockSpec((1, key_rows, LANES), lambda i, *_: (i, 0, 0)),
            whole((8, 2 * inner)),
        ]
        + [whole((rows, packed))] * n_keys,
        [
            struct(patches.shape, bf16),
            struct((media, key_rows, inner), bf16),
            struct((media, key_rows, inner), bf16),
            struct((rows, inner), bf16),
            struct((rows, inner), bf16),
            struct((8, all_rows), f32),
            struct((media, key_rows, LANES), bf16),
            struct((8, 2 * inner), f32),
        ]
        + [struct((rows, packed), bf16)] * n_keys,
        cost(patch_flops + att_flops, 12 * all_rows * dim),
        prefetch=2,
        free=range(8, 7 + n_keys),
    )(
        scalars,
        frame_counts,
        patches,
        time_embedding,
        row(media_gain),
        row(media_bias),
        key_weight,
        value_weight,
        own_rows,
        *q_all,
    )
    media_low, kp, vp, kl, vl, norm_stat, once, norm_vec = out[:8]
    shares = out[8:]
    joined = exchange_keys(shares)

    chunk = min(1024, hidden)
    wo_rows = inner * dim // n_keys // dim
    wo_shape = (n_keys, wo_rows, dim) if aligned else (inner, dim)
    resampled, mid_grad, pack, ff_small, out_slots, ff_low = call(
        functools.partial(forward_kernel, n_keys, aligned),
        "feed_forward",
        (hidden // chunk,),
        [
            whole((rows, dim)),
            whole((rows, dim)),
            pl.BlockSpec((rows, dim), lambda i, *_: (0, 1)),
            whole((1, dim)),
            whole((1, dim)),
            whole((inner, dim)),
            pl.BlockSpec((dim, chunk), lambda i, *_: (0, i)),
            pl.BlockSpec((chunk, dim), lambda i, *_: (i, 0)),
        ]
        + [whole((rows, packed))] * n_keys,
        [
            whole((rows, dim)),
            whole((rows, dim)),
            whole((rows, packed)),
            whole((2, dim)),
            whole(wo_shape),
            whole((rows, dim)),
        ],
        (
            struct((rows, dim), f32),
            struct((rows, dim), f32),
            struct((rows, packed), bf16),
            struct((2, dim), f32),
            struct(wo_shape, bf16),
            struct((rows, dim), bf16),
        ),
        cost(8 * rows * dim * hidden, 4 * dim * hidden + 24 * rows * dim),
        free=range(9, 8 + n_keys),
        scratch_shapes=[
            pltpu.VMEM((rows, dim), f32),
            pltpu.VMEM((rows, dim), f32),
            pltpu.VMEM((inner, dim) if aligned else (8, LANES), f32),
            pltpu.VMEM((rows, inner), f32),
            pltpu.VMEM((rows, inner), bf16),
            pltpu.VMEM((rows, dim), f32),
            pltpu.VMEM((rows, LANES), f32),
        ],
    )(
        scalars,
        lat,
        cot,
        own_rows,
        row(ff_gain),
        row(ff_bias),
        out_weight,
        up_weight,
        down_weight,
        *joined,
    )
    ff_low, rows_all = tie(ff_low, rows_all)
    ff_all = lax.all_gather(ff_low, ("near", "keys"), axis=0, tiled=True)
    if not aligned:
        c = dim // n_keys
        out_slots = out_slots.reshape(n_media, inner // n_media, n_keys, c // each, each)
        out_slots = out_slots.transpose(2, 3, 1, 0, 4).reshape(n_keys, wo_rows, dim)
        out_slots = jnp.stack(
            [lax.dynamic_index_in_dim(out_slots, key ^ s, 0, False) for s in range(n_keys)]
        )
    packs = gather_keys(pack)

    half_keys = n_keys // 2
    pick = lambda turn: (lambda s: s[5] ^ (1 - turn))
    high = 3 * width + wo_rows

    def regroup(value):
        value = jnp.moveaxis(value, 1, 2).reshape(-1, high, n_far, PAIR, each)
        value = value.transpose(0, 3, 1, 2, 4).reshape(-1, PAIR, high, n_far * each)
        return jnp.where(near == 0, value, value[:, ::-1])

    def attend_back(turn, packs, q_before, small_before):
        g = pick(turn)
        own_cols = pl.BlockSpec((rows, GROUP), lambda i, s, *_: (0, g(s)))
        stat_cols = pl.BlockSpec((rows, LANES), lambda i, *_: (0, inner // LANES))
        n = SIDE if media % SIDE == 0 else 1
        key_cols = pl.BlockSpec((n, key_rows, GROUP), lambda i, s, *_: (i, 0, g(s)))
        far_spec = pl.BlockSpec(memory_space=pl.ANY)
        q_width = GROUP if turn == 0 else inner
        chain = (n_keys // 4, PAIR, high, dim // PAIR)
        out = call(
            functools.partial(
                attend_back_kernel, n_keys, frames, turn, inner // HEAD, width, aligned
            ),
            "attend_back",
            (media // n,),
            [own_cols] * (2 * n_keys)
            + [stat_cols] * n_keys
            + [key_cols, key_cols, own_cols, own_cols]
            + [
                pl.BlockSpec((8, GROUP), lambda i, s, *_: (0, g(s))),
                pl.BlockSpec((8, GROUP), lambda i, s, *_: (0, inner // GROUP + g(s))),
                pl.BlockSpec((n, key_rows, dim), lambda i, *_: (i, 0, 0)),
                pl.BlockSpec((n, key_rows, LANES), lambda i, *_: (i, 0, 0)),
                whole((8, all_rows)),
                pl.BlockSpec((rows, dim), lambda i, *_: (0, 0)),
                whole((1, dim)),
                whole((1, dim)),
            ]
            + [far_spec] * 4
            + [whole((rows, GROUP))] * len(q_before)
            + [whole((8, dim))] * len(small_before),
            [
                pl.BlockSpec((2, GROUP, n * key_rows), lambda i, *_: (0, 0, i)),
                whole((8, all_rows)),
                whole((rows, GROUP)),
                whole((rows, GROUP)),
                whole(chain),
                whole(chain),
                whole((8, dim)),
            ]
            + [whole((rows, q_width))] * n_keys,
            [
                struct((2, GROUP, all_rows), bf16),
                struct((8, all_rows), f32),
                struct((rows, GROUP), bf16),
                struct((rows, GROUP), bf16),
                struct(chain, bf16),
                struct(chain, bf16),
                struct((8, dim), f32),
            ]
            + [struct((rows, q_width), bf16)] * n_keys,
            cost(5 * att_flops // 4 + patch_flops // 2, 4 * all_rows * (inner + dim)),
            prefetch=2,
            free=tuple(j * n_keys + s for j in range(3) for s in range(1, n_keys)),
            scratch_shapes=[
                pltpu.VMEM((2 * GROUP + 16, dim), f32),
                pltpu.VMEM((2 * GROUP, LANES), f32),
                pltpu.VMEM((8, LANES), f32),
                pltpu.VMEM((n_keys * rows, GROUP), bf16),
                pltpu.VMEM((n_keys * rows, dim), bf16),
                pltpu.VMEM((GROUP // width, wo_rows, dim), bf16),
                pltpu.VMEM((dim, GROUP), bf16),
                pltpu.VMEM((dim, GROUP), bf16),
                pltpu.SemaphoreType.DMA((4,)),
            ],
        )(
            scalars,
            frame_counts,
            *q_all,
            *packs,
            *packs,
            kp,
            vp,
            kl,
            vl,
            norm_vec,
            norm_vec,
            media_low,
            once,
            norm_stat,
            own_rows,
            row(media_gain),
            row(media_bias),
            rows_all,
            out_slots,
            key_weight,
            value_weight,
            *q_before,
            *small_before,
        )
        chains = out[4:6] if aligned else [regroup(v) for v in out[4:6]]
        return out[:4], chains, out[6], out[7:]

    group_rows = PAIR * n_keys * rows
    (kv_a, stat_a, kl_a, vl_a), (given_a, kept_a), media_small, q_a = attend_back(0, packs, [], [])
    far_core = over_keys(given_a, 1)
    ff_all, kept_a = tie(ff_all, kept_a)

    units = hidden // (n_keys * PAIR)
    share = hidden // (n_media * n_keys)
    runs, per_run = (2, n_far // 2) if aligned else (1, 1)
    if aligned:
        own_up = [
            pl.BlockSpec(
                (dim, share),
                lambda i, s, n=n: (0, ((i * per_run + n) * PAIR + s[1]) * n_keys + s[0]),
            )
            for n in range(per_run)
        ]
        own_weights = [up_weight] * per_run
    else:
        shares = up_weight.reshape(dim, n_far, PAIR, n_keys, share)
        shares = lax.dynamic_index_in_dim(shares, key, 3, False)
        own_weights = [lax.dynamic_index_in_dim(shares, near, 2, False).reshape(dim, units)]
        own_up = [whole((dim, units))]
    ff_partial = call(
        functools.partial(ff_grad_kernel, n_keys, aligned),
        "feed_forward_weights",
        (runs,),
        [
            whole((group_rows, dim)),
            pl.BlockSpec((group_rows, dim), lambda i, s: (0, 1)),
            pl.BlockSpec((dim, units // runs), lambda i, s: (0, s[4] * runs + i)),
            pl.BlockSpec((units // runs, dim), lambda i, s: (s[4] * runs + i, 0)),
        ]
        + own_up,
        whole((2, units, dim)),
        struct((2, units, dim), bf16),
        cost(12 * group_rows * dim * units, 12 * dim * units + 4 * group_rows * dim),
    )(scalars, ff_all, rows_all, up_weight, down_weight, *own_weights)
    blocks = n_far // n_keys
    cols = dim // n_keys
    if not aligned:
        downs = ff_partial[1].reshape(n_far, share, n_keys, blocks, cols // blocks)
        downs = downs.transpose(2, 1, 3, 0, 4).reshape(n_keys, units // n_keys * dim)
        downs = jnp.stack(
            [lax.dynamic_index_in_dim(downs, key ^ s, 0, False) for s in range(n_keys)]
        )
        ups = ff_partial[0].reshape(units, n_far, PAIR, each)
        ups = jnp.where(near == 0, ups, ups[:, :, ::-1])
        ff_partial = jnp.stack([ups.reshape(units, dim), downs.reshape(units, dim)])
    ff_partial = ff_partial.reshape(2 * units, dim)
    far_core, ff_partial = tie(far_core, ff_partial)
    ff_sum = lax.psum_scatter(ff_partial, "far", scatter_dimension=1, tiled=True)
    far_sum = add(kept_a, far_core)
    far_sum, packs[0] = tie(far_sum, packs[0])
    far_near = over_near(far_sum[:, 1])
    (kv_b, stat_b, kl_b, vl_b), (given_b, kept_b), media_small, q_b = attend_back(
        1, packs, q_a, [media_small]
    )
    far_near, given_b, *q_b = tie(far_near, given_b, *q_b)
    far_half = add(far_sum[:, 0], far_near)

    col = lambda turn: pl.BlockSpec((dim, GROUP), lambda i, s: (0, s[5] ^ (1 - turn)))
    both = lambda value: [value, value]

    pieces = 3
    each_piece = media // pieces

    def patch_back(piece, gain, patches_grad):
        at = piece * each_piece
        block = pl.BlockSpec((1, key_rows, dim), lambda i, *_: (i + at, 0, 0))
        keys = pl.BlockSpec((2, GROUP, key_rows), lambda i, *_: (0, 0, i + at))
        stat = pl.BlockSpec((8, key_rows), lambda i, *_: (0, i + at))
        return call(
            functools.partial(patch_back_kernel, frames),
            "patch_back",
            (each_piece,),
            [
                keys,
                keys,
                stat,
                stat,
                stat,
                block,
                time_block,
                whole((1, dim)),
                col(0),
                col(0),
                col(1),
                col(1),
                pl.BlockSpec(memory_space=pl.ANY),
            ],
            block,
            struct(patches.shape, bf16),
            cost(patch_flops // pieces, 8 * all_rows * dim // pieces),
            **({} if piece == 0 else {"input_output_aliases": {13: 0}}),
        )(
            scalars,
            kv_a,
            kv_b,
            stat_a,
            stat_b,
            norm_stat,
            patches,
            time_embedding,
            gain,
            key_weight,
            value_weight,
            key_weight,
            value_weight,
            gain if piece == 0 else patches_grad,
        )

    def sum_far(value):
        return tree_sum([value] + [over_far(value, s) for s in range(1, n_far)])

    gain = row(media_gain)
    far_half, gain, given_b, *q_b = tie(far_half, gain, given_b, *q_b)
    far_got = [over_keys(far_half[j], half_keys + 2 * j) for j in range(n_keys // 4)]
    near_core = over_keys(given_b, 1)
    q_slots = exchange_keys(q_b)
    patches_grad = patch_back(0, gain, None)
    patches_grad, near_core, *q_slots = tie(patches_grad, near_core, *q_slots)
    near_sum = add(kept_b, near_core)
    near_sum, lat = tie(near_sum, lat)
    total = near_sum[0]
    for j in range(1, n_keys // 4):
        total = add(total, over_keys(near_sum[j], 2 * j))
    near_got = over_near(total[1])
    small_rows = -(-(n_frames + 6) // 8) * 8
    latents_grad, small = call(
        functools.partial(latent_back_kernel, n_keys, frames, n_frames),
        "latent_back",
        (1,),
        [whole((rows, dim)), whole((1, dim)), whole((rows, dim)), whole((8, dim)), whole((2, dim))]
        + [whole((rows, GROUP)), col(0), whole((rows, GROUP)), col(0)]
        + [whole((rows, GROUP)), col(1), whole((rows, GROUP)), col(1)]
        + [whole((dim, inner))]
        + [whole((rows, inner))] * n_keys,
        [whole((rows, dim)), whole((small_rows, dim))],
        (struct((rows, dim), f32), struct((small_rows, dim), f32)),
        cost(6 * rows * dim * inner, 6 * dim * inner + 20 * rows * dim),
        free=range(15, 14 + n_keys),
    )(
        scalars,
        lat,
        row(latent_gain),
        mid_grad,
        media_small,
        ff_small,
        kl_a,
        key_weight,
        vl_a,
        value_weight,
        kl_b,
        key_weight,
        vl_b,
        value_weight,
        query_weight,
        *q_slots,
    )

    gain, small = tie(gain, small)
    small = tree_sum([small] + [over_keys(small, s) for s in range(1, n_keys)])
    patches_grad = patch_back(1, gain, patches_grad)
    patches_grad, small, near_got, *far_got = tie(patches_grad, small, near_got, *far_got)
    total = total[0]
    for value in far_got:
        total = add(total, value)
    total = add(total, near_got)
    total, small, gain, ff_sum = tie(total, small, gain, ff_sum)
    parts = lax.all_to_all(total, "far", split_axis=1, concat_axis=0, tiled=True)
    small = small + over_near(small)
    up_keep = ff_sum[:units, :each]
    up_got = over_near(ff_sum[:units, each:])
    downs = ff_sum[units:].reshape(n_keys, share, cols)
    downs = exchange_keys([downs[s] for s in range(n_keys)])
    patches_grad = patch_back(2, gain, patches_grad)
    patches_grad, small, up_got, parts, *downs = tie(patches_grad, small, up_got, parts, *downs)
    small = sum_far(small)
    if aligned:
        q_grad, k_grad, v_grad, out_grad, up_grad, down_grad = call(
            functools.partial(finish_kernel, n_keys, width),
            "finish_weights",
            (1,),
            [whole((units, each))] * 2
            + [pl.BlockSpec((share, cols), lambda i, *_: (units // share, 0))]
            + [whole((share, cols))] * (n_keys - 1)
            + [whole(parts.shape)],
            [whole((each, width))] * 3
            + [
                whole((inner // n_media, dim // n_keys)),
                whole((each, PAIR * units)),
                whole((units, dim // n_keys)),
            ],
            [struct((each, width), f32)] * 3
            + [
                struct((inner // n_media, dim // n_keys), f32),
                struct((each, PAIR * units), f32),
                struct((units, dim // n_keys), f32),
            ],
            cost(0, 16 * width * each + 12 * units * each),
            free=(1,) + tuple(range(3, 3 + n_keys)),
        )(scalars, ff_sum, up_got, ff_sum, *downs[1:], parts)
    else:
        total = jnp.sum(parts.reshape(n_far, -1, each).astype(f32), 0)
        q_grad, k_grad, v_grad = (total[i * width : (i + 1) * width].T for i in range(3))
        out_grad = total[3 * width :].reshape(-1, inner // n_media, each)
        out_grad = out_grad.transpose(1, 0, 2).reshape(inner // n_media, dim // n_keys)
        up_grad = jnp.where(
            near == 0,
            jnp.concatenate([up_keep, up_got], 0),
            jnp.concatenate([up_got, up_keep], 0),
        ).T.astype(f32)
        down_grad = jnp.zeros((units // blocks, cols), f32)
        for s in range(n_keys):
            down_grad = lax.dynamic_update_slice_in_dim(
                down_grad, downs[s].astype(f32), (key ^ s) * share, 0
            )

    return (
        resampled.reshape(latents.shape),
        patches_grad,
        latents_grad.reshape(latents.shape),
        small[:n_frames],
        small[n_frames],
        small[n_frames + 1],
        small[n_frames + 2],
        small[n_frames + 3],
        small[n_frames + 4],
        small[n_frames + 5],
        q_grad,
        k_grad,
        v_grad,
        out_grad,
        up_grad,
        down_grad,
    )


def solution(mesh):
    n_media, n_keys = mesh.shape["media"], mesh.shape["keys"]
    n_far = n_media // PAIR
    fine = Mesh(mesh.devices.reshape(n_far, PAIR, n_keys), ("far", "near", "keys"))
    split = P(("far", "near"), "keys", None)
    return jax.shard_map(
        functools.partial(shards, n_far, n_keys),
        mesh=fine,
        in_specs=(split, split, P(("far", "near"))) + (P(),) * 13 + (split,),
        out_specs=(split,) * 3 + (P(),) * 7 + (P(("far", "near"), "keys"),) * 6,
        check_vma=False,
    )
```
